32 devices in a mesh: dp: 8 (over z, x), shard: 4 (over y, core).
Axes of the slice: x: 2, y: 2, z: 4, core: 2. Of those that a mesh axis runs over, the one named last changes fastest.
Arguments:
- tokens: bfloat16 [8, 2048, 2048], P('dp', 'shard'), may hold values from -6 to 6
- cotangent: bfloat16 [8, 2048, 2048], P('dp', 'shard'), may hold values from -6 to 6
- lengths: int32 [8], replicated, may hold values from 1024 to 2048, as said below
- slot_sequence: int32 [8], P('dp'), may hold values from 0 to 7, each once
- attn_gain: float32 [2048], P(('dp', 'shard')), may hold values from 0.1 to 1.9
- w_qkv: float32 [2048, 1536], P(('dp', 'shard')), may hold values from -0.125 to 0.125
- q_gain: float32 [64], replicated, may hold values from 0.6 to 1.8
- k_gain: float32 [64], replicated, may hold values from 0.6 to 1.8
- w_out: float32 [1024, 2048], P(None, ('dp', 'shard')), may hold values from -1.5 to 1.5
- ffn_gain: float32 [2048], P(('dp', 'shard')), may hold values from 0.1 to 1.9
- w_gate: float32 [2048, 1024], P(('dp', 'shard')), may hold values from -0.125 to 0.125
- w_up: float32 [2048, 1024], P(('dp', 'shard')), may hold values from -0.125 to 0.125
- w_down: float32 [1024, 2048], P(None, ('dp', 'shard')), may hold values from -0.1875 to 0.1875
Outputs:
- output: bfloat16 [8, 2048, 2048], P('dp', 'shard')
- input_grad: float32 [8, 2048, 2048], P('dp', 'shard')
- grad_attn_gain: float32 [2048], P(('dp', 'shard'))
- grad_w_qkv: float32 [2048, 1536], P(('dp', 'shard'))
- grad_q_gain: float32 [64], replicated
- grad_k_gain: float32 [64], replicated
- grad_w_out: float32 [1024, 2048], P(None, ('dp', 'shard'))
- grad_ffn_gain: float32 [2048], P(('dp', 'shard'))
- grad_w_gate: float32 [2048, 1024], P(('dp', 'shard'))
- grad_w_up: float32 [2048, 1024], P(('dp', 'shard'))
- grad_w_down: float32 [1024, 2048], P(None, ('dp', 'shard'))
The draws below stay inside these ranges and needn't reach their ends.
Inputs may be any that keep to these rules, and one draw needn't show every extreme that they name: `lengths`: some sequence has exactly 2048 tokens. `slot_sequence`: each row holds a different sequence.
All inputs are finite; a program needn't handle non-finite values.
Results may differ from the reference program's by a relative error of at most 0.015.
The reference program's roundings to bfloat16 on the way count: a program that leaves them out, or rounds other values in their place, can miss the bound.
Values may be sent and summed in bfloat16 or wider, within the bound.
No kernel may reach another device: no remote copies, remote signals or barrier semaphores. Data moves between devices by JAX's collectives and lax.ppermute only.
A program may use at most 192 MiB of HBM per device.

```python
import math
import jax
import jax.numpy as jnp
from jax import lax

D = 2048
HEADS = 16
KV = 4
HD = 64
FF = 1024
ROW_LEN = 2048
ROWS = 8
QKV = 1536


def draw_lengths(key, part):
    key_one, key_two = jax.random.split(jax.random.fold_in(key, 7))
    half_len = ROW_LEN // 2
    base = jax.random.randint(key_one, (ROWS,), 0, half_len + 1)
    tail_len = base * base // half_len * base // half_len
    chosen = jax.random.randint(key_two, (), 0, ROWS)
    values = jnp.where(jnp.arange(ROWS) == chosen, ROW_LEN, half_len + tail_len)
    return values.astype(jnp.int32)


def shard_levels(key, shape, cuts, low, high):
    def one(dim, blocks):
        draws = jax.random.uniform(jax.random.fold_in(jax.random.fold_in(key, 6), dim), (blocks,), jnp.float32, low / len(cuts), high / len(cuts))
        return jnp.repeat(jnp.exp(draws), shape[dim] // blocks).reshape((-1,) + (1,) * (len(shape) - dim - 1))

    level = one(*cuts[0])
    for cut in cuts[1:]:
        level = level * one(*cut)
    return level


def normal_values(own_key, dims, scale, bound, pieces=(), kind=jnp.bfloat16):
    entries = scale * jax.random.normal(own_key, dims, jnp.float32)
    if pieces:
        entries = entries * shard_levels(own_key, dims, pieces, -0.22, 0.18)
    return jnp.clip(entries, -bound, bound).astype(kind)


def setup_inputs(seed: int = 0) -> dict:
    keys = jax.random.split(jax.random.key(seed), 14)
    tokens = normal_values(keys[0], (ROWS, ROW_LEN, D), 1.0, 6.0, ((0, 8), (1, 4)))
    cotangent = normal_values(keys[1], (ROWS, ROW_LEN, D), 1.0, 6.0, ((0, 8), (1, 4)))
    lengths = draw_lengths(jax.random.fold_in(keys[13], 71), 0)
    slot_sequence = jax.random.permutation(keys[3], ROWS).astype(jnp.int32)
    attn_gain = jnp.clip(1.0 + 0.18 * jax.random.normal(keys[4], (D,), jnp.float32), 0.1, 1.9)
    w_qkv = normal_values(keys[5], (D, QKV), D ** -0.5, 0.125, ((0, 32),), jnp.float32)
    q_gain = jnp.clip(jax.random.uniform(keys[6], (HD,), jnp.float32, 0.6, 1.8), 0.6, 1.8)
    k_gain = jnp.clip(jax.random.uniform(keys[7], (HD,), jnp.float32, 0.6, 1.8), 0.6, 1.8)
    w_out = normal_values(keys[8], (HEADS * HD, D), 16 ** -0.5, 1.5, ((1, 32),), jnp.float32)
    ffn_gain = jnp.clip(1.0 + 0.18 * jax.random.normal(keys[9], (D,), jnp.float32), 0.1, 1.9)
    w_gate = normal_values(keys[10], (D, FF), D ** -0.5, 0.125, ((0, 32),), jnp.float32)
    w_up = normal_values(keys[11], (D, FF), D ** -0.5, 0.125, ((0, 32),), jnp.float32)
    w_down = normal_values(keys[12], (FF, D), FF ** -0.5, 0.1875, ((1, 32),), jnp.float32)
    return {"tokens": tokens, "cotangent": cotangent, "lengths": lengths, "slot_sequence": slot_sequence, "attn_gain": attn_gain, "w_qkv": w_qkv, "q_gain": q_gain, "k_gain": k_gain, "w_out": w_out, "ffn_gain": ffn_gain, "w_gate": w_gate, "w_up": w_up, "w_down": w_down}


@jax.custom_vjp
def low(v):
    return lax.optimization_barrier(v.astype(jnp.bfloat16)).astype(jnp.float32)

@jax.custom_vjp
def low_back(v):
    return v

def low_keep(v):
    return (low(v), None)

def low_pass(kept, grad):
    return (grad,)

def back_keep(v):
    return (v, None)

def back_low(kept, grad):
    return (low(grad),)
low.defvjp(low_keep, low_pass)
low_back.defvjp(back_keep, back_low)
EPS = 1e-06
HIGHEST = lax.Precision.HIGHEST

def rms_norm(values):
    return values * lax.rsqrt(lax.optimization_barrier(jnp.mean(values * values, axis=-1, keepdims=True)) + EPS)

def rotate(values, cos_t, sin_t):
    half_len = values.shape[-1] // 2
    turned = jnp.concatenate([-values[..., half_len:], values[..., :half_len]], axis=-1)
    return values * cos_t + turned * sin_t

def tables(positions):
    freq = 10000.0 ** (-(2.0 * jnp.arange(HD // 2, dtype=jnp.float32)) / HD)
    angles = positions.astype(jnp.float32)[:, None] * freq[None, :]
    angles = jnp.concatenate([angles, angles], axis=-1)
    return (jnp.cos(angles), jnp.sin(angles))

def attention(q_low, k_low, v_low, row_lens):
    group_rows = q_low.shape[0]
    group_size = HEADS // KV
    block_len = min(512, ROW_LEN)
    scale_factor = 1.0 / math.sqrt(HD)
    q_split = q_low.reshape(group_rows, ROW_LEN, KV, group_size, HD)
    key_pos = jnp.arange(ROW_LEN, dtype=jnp.int32)
    key_live = key_pos[None, :] < row_lens[:, None]

    def one_block(block_start):
        q_block = lax.dynamic_slice_in_dim(q_split, block_start, block_len, 1)
        scores = low_back(scale_factor * jnp.einsum('rqgph,rkgh->rgpqk', q_block, k_low, precision=HIGHEST))
        query_pos = block_start + jnp.arange(block_len, dtype=jnp.int32)
        allowed = (key_pos[None, :] <= query_pos[:, None])[None, None, None, :, :] & key_live[:, None, None, None, :]
        exps = jnp.where(allowed, jnp.exp(scores), 0.0)
        sums = lax.optimization_barrier(jnp.sum(exps, axis=-1, keepdims=True))
        unscaled = low_back(jnp.einsum('rgpqk,rkgh->rgpqh', low(exps), v_low, precision=HIGHEST))
        return unscaled / sums
    starts = jnp.arange(0, ROW_LEN, block_len, dtype=jnp.int32)
    blocks = lax.map(jax.checkpoint(one_block), starts)
    return blocks.transpose(1, 0, 4, 2, 3, 5).reshape(group_rows, ROW_LEN, HEADS * HD)

def layer(tokens_f, row_lens, weights):
    attn_gain, w_qkv, q_gain, k_gain, w_out, ffn_gain, w_gate, w_up, w_down = weights
    group_rows = tokens_f.shape[0]
    q_width = HEADS * HD
    kv_width = KV * HD
    cos_t, sin_t = tables(jnp.arange(ROW_LEN, dtype=jnp.float32))
    cos_h = cos_t[None, :, None, :]
    sin_h = sin_t[None, :, None, :]
    normed_low = low(rms_norm(tokens_f) * low(attn_gain))
    projected = low_back(jnp.einsum('rtd,de->rte', normed_low, low(w_qkv), precision=HIGHEST))
    queries = projected[..., :q_width].reshape(group_rows, ROW_LEN, HEADS, HD)
    keys_raw = projected[..., q_width:q_width + kv_width].reshape(group_rows, ROW_LEN, KV, HD)
    values_raw = projected[..., q_width + kv_width:].reshape(group_rows, ROW_LEN, KV, HD)
    q_low = low(rotate(rms_norm(queries) * q_gain, cos_h, sin_h))
    k_low = low(rotate(rms_norm(keys_raw) * k_gain, cos_h, sin_h))
    v_low = low(values_raw)
    attended = low(attention(q_low, k_low, v_low, row_lens))
    middle = tokens_f + low_back(jnp.einsum('rtc,cd->rtd', attended, low(w_out), precision=HIGHEST))
    ffn_in = low(rms_norm(middle) * low(ffn_gain))
    gate_proj = low_back(jnp.einsum('rtd,df->rtf', ffn_in, low(w_gate), precision=HIGHEST))
    up_proj = low_back(jnp.einsum('rtd,df->rtf', ffn_in, low(w_up), precision=HIGHEST))
    activated = low(jax.nn.silu(gate_proj) * up_proj)
    return middle + low_back(jnp.einsum('rtf,fd->rtd', activated, low(w_down), precision=HIGHEST))

def add_pair(left, right):
    return left + right

def reference(tokens, cotangent, lengths, slot_sequence, attn_gain, w_qkv, q_gain, k_gain, w_out, ffn_gain, w_gate, w_up, w_down):
    group_rows = math.gcd(ROWS, max(1, 4096 // ROW_LEN))
    group_count = ROWS // group_rows
    row_lens = jnp.take(lengths, slot_sequence).astype(jnp.int32)
    weights = (attn_gain, w_qkv, q_gain, k_gain, w_out, ffn_gain, w_gate, w_up, w_down)
    stacked_tokens = tokens.astype(jnp.float32).reshape(group_count, group_rows, ROW_LEN, D)
    stacked_cot = cotangent.astype(jnp.float32).reshape(group_count, group_rows, ROW_LEN, D)
    stacked_lens = row_lens.reshape(group_count, group_rows)

    def group_step(summed, group_item):
        group_tokens, group_cot, group_lens = group_item
        live_mask = (jnp.arange(ROW_LEN, dtype=jnp.int32)[None, :] < group_lens[:, None]).astype(jnp.float32)

        def forward(inputs, params):
            return layer(inputs, group_lens, params)
        output, pullback = jax.vjp(forward, group_tokens, weights)
        input_grad, weight_part = pullback(group_cot * live_mask[..., None])
        summed = jax.tree.map(add_pair, summed, weight_part)
        return (summed, (output.astype(jnp.bfloat16), input_grad))
    zero_grads = jax.tree.map(jnp.zeros_like, weights)
    weight_grads, (out_rows, grad_rows) = lax.scan(group_step, zero_grads, (stacked_tokens, stacked_cot, stacked_lens))
    return (out_rows.reshape(ROWS, ROW_LEN, D), grad_rows.reshape(ROWS, ROW_LEN, D), weight_grads[0], weight_grads[1], weight_grads[2], weight_grads[3], weight_grads[4], weight_grads[5], weight_grads[6], weight_grads[7], weight_grads[8])
```

```python
import math

import jax
import jax.numpy as jnp
from jax import lax
from jax.experimental import pallas as pl
from jax.experimental.pallas import tpu as pltpu
from jax.sharding import PartitionSpec as P

HEADS = 16
KV = 4
HD = 64


EPS = 1e-06


def normalize(values):
    inverse = lax.rsqrt(jnp.mean(values * values, axis=-1, keepdims=True) + EPS)
    return (values * inverse, inverse)


def norm_back(values, inverse, grad_normed):
    cubed = inverse * inverse * inverse
    return inverse * grad_normed - values * cubed * jnp.mean(
        grad_normed * values, axis=-1, keepdims=True
    )


def rotate(values, cos_t, sin_t):
    half_len = values.shape[-1] // 2
    turned = jnp.concatenate([-values[..., half_len:], values[..., :half_len]], axis=-1)
    return values * cos_t + turned * sin_t


def rotate_back(grad_in, cos_t, sin_t):
    half_len = grad_in.shape[-1] // 2
    along = grad_in * sin_t
    return grad_in * cos_t + jnp.concatenate(
        [along[..., half_len:], -along[..., :half_len]], axis=-1
    )


def tables(positions):
    freq = 10000.0 ** (-(2.0 * jnp.arange(HD // 2, dtype=jnp.float32)) / HD)
    angles = positions.astype(jnp.float32)[:, None] * freq[None, :]
    angles = jnp.concatenate([angles, angles], axis=-1)
    return (jnp.cos(angles), jnp.sin(angles))


ANY = pl.BlockSpec(memory_space=pl.ANY)


def swap(values, mask, devices):
    return lax.ppermute(values, ("dp", "shard"), [(i, i ^ mask) for i in range(devices)])


def place(blocks, masks, me, total_rows):
    count = len(blocks)
    sizes = [array.shape[0] // len(own) for array, own in zip(blocks, masks)]
    copies = sum(len(own) for own in masks)

    def kernel(me_ref, *refs):
        sources, out_ref, sems = refs[:count], refs[count], refs[count + 1]
        started = []
        for array, own, size in zip(sources, masks, sizes):
            for at, mask in enumerate(own):
                row = pl.multiple_of((me_ref[0] ^ mask) * size, size)
                copy = pltpu.make_async_copy(
                    array.at[pl.ds(at * size, size)], out_ref.at[pl.ds(row, size)], sems.at[len(started)]
                )
                copy.start()
                started.append(copy)
        for copy in started:
            copy.wait()

    return pl.pallas_call(
        kernel,
        out_shape=jax.ShapeDtypeStruct((total_rows,) + blocks[0].shape[1:], blocks[0].dtype),
        in_specs=[pl.BlockSpec(memory_space=pltpu.SMEM)] + [ANY] * count,
        out_specs=ANY,
        scratch_shapes=[pltpu.SemaphoreType.DMA((copies,))],
    )(me, *blocks)


def pick(array, orders, me, size):
    copies = sum(len(own) for own in orders)

    def kernel(me_ref, in_ref, *refs):
        outs, sems = refs[:-1], refs[-1]
        started = []
        for out, own in zip(outs, orders):
            for at, mask in enumerate(own):
                row = pl.multiple_of((me_ref[0] ^ mask) * size, size)
                copy = pltpu.make_async_copy(
                    in_ref.at[pl.ds(row, size)], out.at[pl.ds(at * size, size)], sems.at[len(started)]
                )
                copy.start()
                started.append(copy)
        for copy in started:
            copy.wait()

    return pl.pallas_call(
        kernel,
        out_shape=[jax.ShapeDtypeStruct((len(own) * size,) + array.shape[1:], array.dtype) for own in orders],
        in_specs=[pl.BlockSpec(memory_space=pltpu.SMEM), ANY],
        out_specs=[ANY] * len(orders),
        scratch_shapes=[pltpu.SemaphoreType.DMA((copies,))],
    )(me, array)


def gather_rows(part, me, devices):
    if devices != 32:
        return lax.all_gather(part, ("dp", "shard"), axis=0, tiled=True)
    zs = [part] + [swap(part, m, devices) for m in (8, 16, 24)]
    near, far = jnp.concatenate(zs[:2]), jnp.concatenate(zs[2:])
    near_x, far_x = swap(near, 4, devices), swap(far, 4, devices)
    near_y, far_y = swap(near, 2, devices), swap(far, 2, devices)
    near_xy, far_xy = swap(near_x, 2, devices), swap(far_y, 4, devices)
    blocks, masks = [], []
    for array, shift, base in (
        (near, 0, 0), (far, 0, 16), (near_x, 4, 0), (far_y, 2, 16),
        (near_y, 2, 0), (far_x, 4, 16), (near_xy, 6, 0), (far_xy, 6, 16),
    ):
        blocks += [array, swap(array, 1, devices)]
        masks += [(base | shift, (base + 8) | shift), (base | shift | 1, (base + 8) | shift | 1)]
    return place(blocks, masks, me, part.shape[0] * devices)


def reduce_rows(grad, me, devices):
    if devices != 32:
        return lax.psum_scatter(
            grad.astype(jnp.float32), ("dp", "shard"), scatter_dimension=0, tiled=True
        )
    size = grad.shape[0] // devices
    order = [2, 10, 6, 14, 20, 28, 22, 30, 0, 8, 4, 12, 16, 24, 18, 26]
    keep, send = pick(grad, [order, [m | 1 for m in order]], me, size)
    came = swap(send, 1, devices)
    low = jnp.bfloat16
    def both(lo, hi):
        return keep[lo * size : hi * size].astype(jnp.float32) + came[lo * size : hi * size].astype(
            jnp.float32
        )
    from_y = swap(both(0, 4).astype(low), 2, devices)
    from_x = swap(both(4, 8).astype(low), 4, devices)
    near = both(8, 12) + from_y.astype(jnp.float32)
    far = both(12, 16) + from_x.astype(jnp.float32)
    from_x = swap(near[2 * size :].astype(low), 4, devices)
    from_y = swap(far[2 * size :].astype(low), 2, devices)
    near = near[: 2 * size] + from_x.astype(jnp.float32)
    far = far[: 2 * size] + from_y.astype(jnp.float32)
    one = swap(near[size:].astype(low), 8, devices)
    two = swap(far[:size].astype(low), 16, devices)
    three = swap(far[size:].astype(low), 24, devices)
    return (
        near[:size]
        + one.astype(jnp.float32)
        + (two.astype(jnp.float32) + three.astype(jnp.float32))
    )


def gather_row(part, devices, shards):
    if shards != 4:
        return lax.all_gather(part, "shard", axis=1, tiled=True)
    at = lax.axis_index("shard").reshape(1)
    flat = part[0]
    over = swap(flat, 2, devices)
    blocks = [flat, swap(flat, 1, devices), over, swap(over, 1, devices)]
    return place(blocks, [(0,), (1,), (2,), (3,)], at, 4 * flat.shape[0])[None]


def reduce_row(grad, devices, shards):
    if shards != 4:
        return lax.psum_scatter(grad, "shard", scatter_dimension=1, tiled=True)
    at = lax.axis_index("shard").reshape(1)
    size = grad.shape[1] // 4
    low = grad[0].astype(jnp.bfloat16)
    keep, send = pick(low, [(0, 2), (1, 3)], at, size)
    both = keep.astype(jnp.float32) + swap(send, 1, devices).astype(jnp.float32)
    over = swap(both[size:].astype(jnp.bfloat16), 2, devices)
    return (both[:size] + over.astype(jnp.float32))[None]


def small_gather(part, devices):
    if devices != 32:
        return lax.all_gather(part, ("dp", "shard"), axis=0)
    rows = part[None]
    for mask in (1, 2, 4, 8, 16):
        rows = jnp.concatenate([rows, swap(rows, mask, devices)])
    me = lax.axis_index("dp") * 4 + lax.axis_index("shard")
    return rows[jnp.arange(devices) ^ me]


def small_reduce(rows, shared, devices):
    if devices != 32:
        own = lax.psum_scatter(rows, ("dp", "shard"), scatter_dimension=0)
        return own, lax.psum(shared, ("dp", "shard"))
    me = lax.axis_index("dp") * 4 + lax.axis_index("shard")
    rows = rows[jnp.arange(devices) ^ me]
    for mask in (16, 8, 4, 2, 1):
        came = swap(jnp.concatenate([rows[mask:], shared]), mask, devices)
        rows, shared = rows[:mask] + came[:mask], shared + came[mask:]
    return rows[0], shared


def unchanged(running):
    return running


def local(
    tokens,
    cotangent,
    lengths,
    slot_sequence,
    attn_gain,
    w_qkv,
    q_gain,
    k_gain,
    w_out,
    ffn_gain,
    w_gate,
    w_up,
    w_down,
):
    row_count, piece_len, model_width = tokens.shape
    group_size = HEADS // KV
    q_width = HEADS * HD
    kv_width = KV * HD
    total_rows = lengths.shape[0]
    row_len = piece_len * lax.axis_size("shard")
    scale_factor = 1.0 / math.sqrt(HD)
    row_valid = jnp.sum(
        jnp.where(
            slot_sequence[:, None] == jnp.arange(total_rows, dtype=jnp.int32)[None, :],
            lengths[None, :],
            0,
        ),
        axis=1,
    )
    longest = jnp.max(row_valid)
    positions = lax.axis_index("shard") * piece_len + jnp.arange(piece_len, dtype=jnp.int32)
    last_query = lax.axis_index("shard") * piece_len + piece_len - 1
    live_mask = (positions[None, :] < row_valid[:, None]).astype(jnp.float32)
    cos_t, sin_t = tables(positions)
    cos_h = cos_t[None, :, None, :]
    sin_h = sin_t[None, :, None, :]
    query_pos = jnp.tile(positions, group_size)
    shards = lax.axis_size("shard")
    devices = lax.axis_size("dp") * shards
    me = (lax.axis_index("dp") * shards + lax.axis_index("shard")).reshape(1)
    gains = small_gather(jnp.concatenate([attn_gain, ffn_gain]).astype(jnp.bfloat16), devices)
    part_len = attn_gain.shape[0]
    gain_attn = gains[:, :part_len].reshape(model_width)
    gain_ffn = gains[:, part_len:].reshape(model_width)
    low = jnp.bfloat16
    wqkv_low = gather_rows(w_qkv.astype(low), me, devices)
    wout_low = gather_rows(w_out.astype(low).T, me, devices)
    wgate_low = gather_rows(w_gate.astype(low), me, devices)
    wup_low = gather_rows(w_up.astype(low), me, devices)
    wdown_low = gather_rows(w_down.astype(low).T, me, devices)
    gain_attn_f = gain_attn.astype(jnp.float32)
    x_float = tokens.astype(jnp.float32)
    normed_one, inverse_one = normalize(x_float)
    normed_low = (normed_one * gain_attn_f).astype(jnp.bfloat16)
    projected = jnp.einsum("rtd,de->rte", normed_low, wqkv_low, preferred_element_type=jnp.float32)
    q_raw = projected[..., :q_width].reshape(row_count, piece_len, HEADS, HD)
    k_raw = projected[..., q_width : q_width + kv_width].reshape(row_count, piece_len, KV, HD)
    v_raw = projected[..., q_width + kv_width :]
    q_unit, q_inverse = normalize(q_raw)
    k_unit, k_inverse = normalize(k_raw)
    q_low = rotate(q_unit * q_gain, cos_h, sin_h).astype(jnp.bfloat16)
    k_low = (
        rotate(k_unit * k_gain, cos_h, sin_h)
        .astype(jnp.bfloat16)
        .reshape(row_count, piece_len, kv_width)
    )
    v_low = v_raw.astype(jnp.bfloat16)
    q_group = (
        q_low.reshape(row_count, piece_len, KV, group_size, HD)
        .transpose(0, 2, 3, 1, 4)
        .reshape(row_count, KV, group_size * piece_len, HD)
    )

    def block_scores(key_piece, value_piece, offset, block_len):
        k_block = lax.dynamic_slice_in_dim(key_piece, offset, block_len, 1).reshape(
            row_count, block_len, KV, HD
        )
        v_block = lax.dynamic_slice_in_dim(value_piece, offset, block_len, 1).reshape(
            row_count, block_len, KV, HD
        )
        scores = scale_factor * jnp.einsum(
            "rgqh,rkgh->rgqk", q_group, k_block, preferred_element_type=jnp.float32
        )
        key_pos = offset + jnp.arange(block_len, dtype=jnp.int32)
        allowed = (key_pos[None, None, None, :] <= query_pos[None, None, :, None]) & (
            key_pos[None, None, None, :] < row_valid[:, None, None, None]
        )
        return (k_block, v_block, jnp.where(allowed, jnp.exp(scores), 0.0))

    def block_used(key_start):
        return (key_start <= last_query) & (key_start < longest)

    zero_accum = jnp.zeros((row_count, KV, group_size * piece_len, HD), jnp.float32)
    zero_sums = jnp.zeros((row_count, KV, group_size * piece_len), jnp.float32)
    both_piece = gather_row(jnp.concatenate([k_low, v_low], axis=-1), devices, shards)
    key_piece, value_piece = both_piece[..., :kv_width], both_piece[..., kv_width:]
    block_len = math.gcd(key_piece.shape[1], piece_len)
    block_count = key_piece.shape[1] // block_len

    def fold_block(block_index, running):
        offset = block_index * block_len

        def compute(state):
            accum_out, row_sums = state
            k_block, v_block, exps = block_scores(key_piece, value_piece, offset, block_len)
            row_sums = row_sums + jnp.sum(exps, axis=-1)
            accum_out = accum_out + jnp.einsum(
                "rgqk,rkgh->rgqh",
                exps.astype(jnp.bfloat16),
                v_block,
                preferred_element_type=jnp.float32,
            )
            return (accum_out, row_sums)

        return lax.cond(block_used(offset), compute, unchanged, running)

    accum_out, denominator = lax.fori_loop(0, block_count, fold_block, (zero_accum, zero_sums))
    o_group = accum_out / denominator[..., None]
    att_low = (
        o_group.reshape(row_count, KV, group_size, piece_len, HD)
        .transpose(0, 3, 1, 2, 4)
        .reshape(row_count, piece_len, q_width)
        .astype(jnp.bfloat16)
    )
    x_mid = x_float + jnp.einsum(
        "rtc,dc->rtd", att_low, wout_low, preferred_element_type=jnp.float32
    )
    gain_ffn_f = gain_ffn.astype(jnp.float32)
    normed_two, inverse_two = normalize(x_mid)
    ffn_in = (normed_two * gain_ffn_f).astype(jnp.bfloat16)
    gate_proj = jnp.einsum("rtd,df->rtf", ffn_in, wgate_low, preferred_element_type=jnp.float32)
    up_proj = jnp.einsum("rtd,df->rtf", ffn_in, wup_low, preferred_element_type=jnp.float32)
    gate_sig = jax.nn.sigmoid(gate_proj)
    silu_gate = gate_proj * gate_sig
    activated = (silu_gate * up_proj).astype(jnp.bfloat16)
    result = x_mid + jnp.einsum(
        "rtf,df->rtd", activated, wdown_low, preferred_element_type=jnp.float32
    )
    output = result.astype(jnp.bfloat16)
    grad_out = cotangent.astype(jnp.float32) * live_mask[..., None]
    grad_low = grad_out.astype(jnp.bfloat16)
    gain_ffn_k = gain_ffn_f
    wgate_k, wup_k, wdown_k = wgate_low, wup_low, wdown_low
    grad_down = jnp.einsum("rtd,rtf->df", grad_low, activated, preferred_element_type=jnp.float32).astype(low)
    grad_act = jnp.einsum("rtd,df->rtf", grad_low, wdown_k, preferred_element_type=jnp.float32)
    grad_gate = (grad_act * up_proj * gate_sig * (1.0 + gate_proj * (1.0 - gate_sig))).astype(
        jnp.bfloat16
    )
    grad_up = (grad_act * silu_gate).astype(jnp.bfloat16)
    grad_wgate = jnp.einsum("rtd,rtf->df", ffn_in, grad_gate, preferred_element_type=jnp.float32).astype(low)
    grad_wup = jnp.einsum("rtd,rtf->df", ffn_in, grad_up, preferred_element_type=jnp.float32).astype(low)
    grad_ffn_in = jnp.einsum(
        "rtf,df->rtd", grad_gate, wgate_k, preferred_element_type=jnp.float32
    ) + jnp.einsum("rtf,df->rtd", grad_up, wup_k, preferred_element_type=jnp.float32)
    grad_gain_two = jnp.sum(grad_ffn_in * normed_two, axis=(0, 1))
    grad_mid = grad_out + norm_back(x_mid, inverse_two, grad_ffn_in * gain_ffn_k)
    summed_down = reduce_rows(grad_down, me, devices).T
    summed_wgate = reduce_rows(grad_wgate, me, devices)
    summed_wup = reduce_rows(grad_wup, me, devices)
    wqkv_k, wout_k, gain_attn_k = wqkv_low, wout_low, gain_attn_f
    mid_low = grad_mid.astype(jnp.bfloat16)
    grad_wout = jnp.einsum("rtd,rtc->dc", mid_low, att_low, preferred_element_type=jnp.float32).astype(low)
    summed_wout = reduce_rows(grad_wout, me, devices).T
    grad_att = jnp.einsum("rtd,dc->rtc", mid_low, wout_k, preferred_element_type=jnp.float32)
    grad_group = (
        grad_att.reshape(row_count, piece_len, KV, group_size, HD)
        .transpose(0, 2, 3, 1, 4)
        .reshape(row_count, KV, group_size * piece_len, HD)
    )
    grad_sums = -jnp.sum(grad_group * o_group, axis=-1) / denominator
    grad_accum = (grad_group / denominator[..., None]).astype(jnp.bfloat16)
    zero_keys = jnp.zeros((row_count, row_len, kv_width), jnp.float32)
    attend_key_piece, attend_value_piece = key_piece, value_piece
    attend_block_len = math.gcd(attend_key_piece.shape[1], piece_len)
    block_count = attend_key_piece.shape[1] // attend_block_len

    def fold_block(block_index, running):
        offset = block_index * attend_block_len
        key_start = offset

        def compute(state):
            grad_query, grad_keys, grad_values = state
            k_block, v_block, exps = block_scores(
                attend_key_piece, attend_value_piece, offset, attend_block_len
            )
            grad_exps = (
                jnp.einsum(
                    "rgqh,rkgh->rgqk", grad_accum, v_block, preferred_element_type=jnp.float32
                )
                + grad_sums[..., None]
            )
            grad_scores = (exps * grad_exps).astype(jnp.bfloat16)
            grad_query = grad_query + scale_factor * jnp.einsum(
                "rgqk,rkgh->rgqh", grad_scores, k_block, preferred_element_type=jnp.float32
            )
            part_keys = scale_factor * jnp.einsum(
                "rgqk,rgqh->rkgh", grad_scores, q_group, preferred_element_type=jnp.float32
            )
            part_values = jnp.einsum(
                "rgqk,rgqh->rkgh",
                exps.astype(jnp.bfloat16),
                grad_accum,
                preferred_element_type=jnp.float32,
            )
            old_keys = lax.dynamic_slice_in_dim(grad_keys, key_start, attend_block_len, 1)
            old_values = lax.dynamic_slice_in_dim(grad_values, key_start, attend_block_len, 1)
            grad_keys = lax.dynamic_update_slice_in_dim(
                grad_keys,
                old_keys + part_keys.reshape(row_count, attend_block_len, kv_width),
                key_start,
                1,
            )
            grad_values = lax.dynamic_update_slice_in_dim(
                grad_values,
                old_values + part_values.reshape(row_count, attend_block_len, kv_width),
                key_start,
                1,
            )
            return (grad_query, grad_keys, grad_values)

        return lax.cond(block_used(key_start), compute, unchanged, running)

    grad_query, grad_keys_all, grad_values_all = lax.fori_loop(
        0, block_count, fold_block, (zero_accum, zero_keys, zero_keys)
    )
    grad_both = reduce_row(jnp.concatenate([grad_keys_all, grad_values_all], axis=-1), devices, shards)
    grad_keys, grad_values = grad_both[..., :kv_width], grad_both[..., kv_width:]
    grad_q_heads = (
        grad_query.reshape(row_count, KV, group_size, piece_len, HD)
        .transpose(0, 3, 1, 2, 4)
        .reshape(row_count, piece_len, HEADS, HD)
    )
    grad_q_scaled = rotate_back(grad_q_heads, cos_h, sin_h)
    grad_qgain = jnp.sum(grad_q_scaled * q_unit, axis=(0, 1, 2))
    grad_q_raw = norm_back(q_raw, q_inverse, grad_q_scaled * q_gain)
    grad_k_scaled = rotate_back(grad_keys.reshape(row_count, piece_len, KV, HD), cos_h, sin_h)
    grad_kgain = jnp.sum(grad_k_scaled * k_unit, axis=(0, 1, 2))
    grad_k_raw = norm_back(k_raw, k_inverse, grad_k_scaled * k_gain)
    grad_projected = jnp.concatenate(
        [
            grad_q_raw.reshape(row_count, piece_len, q_width),
            grad_k_raw.reshape(row_count, piece_len, kv_width),
            grad_values,
        ],
        axis=-1,
    ).astype(jnp.bfloat16)
    grad_wqkv = jnp.einsum(
        "rtd,rte->de", normed_low, grad_projected, preferred_element_type=jnp.float32
    ).astype(low)
    grad_normed = jnp.einsum(
        "rte,de->rtd", grad_projected, wqkv_k, preferred_element_type=jnp.float32
    )
    grad_gain_one = jnp.sum(grad_normed * normed_one, axis=(0, 1))
    input_grad = grad_mid + norm_back(x_float, inverse_one, grad_normed * gain_attn_k)
    summed_wqkv = reduce_rows(grad_wqkv, me, devices)
    own, shared = small_reduce(
        jnp.concatenate(
            [grad_gain_one.reshape(devices, part_len), grad_gain_two.reshape(devices, part_len)], axis=1
        ),
        jnp.concatenate([grad_qgain, grad_kgain])[None],
        devices,
    )
    summed_gain_one, summed_gain_two = own[:part_len], own[part_len:]
    summed_qgain, summed_kgain = shared[0, :HD], shared[0, HD:]
    return (
        output,
        input_grad,
        summed_gain_one,
        summed_wqkv,
        summed_qgain,
        summed_kgain,
        summed_wout,
        summed_gain_two,
        summed_wgate,
        summed_wup,
        summed_down,
    )


def solution(mesh):
    in_specs = (
        P("dp", "shard", None),
        P("dp", "shard", None),
        P(),
        P("dp"),
        P(("dp", "shard")),
        P(("dp", "shard"), None),
        P(),
        P(),
        P(None, ("dp", "shard")),
        P(("dp", "shard")),
        P(("dp", "shard"), None),
        P(("dp", "shard"), None),
        P(None, ("dp", "shard")),
    )
    out_specs = (
        P("dp", "shard", None),
        P("dp", "shard", None),
        P(("dp", "shard")),
        P(("dp", "shard"), None),
        P(),
        P(),
        P(None, ("dp", "shard")),
        P(("dp", "shard")),
        P(("dp", "shard"), None),
        P(("dp", "shard"), None),
        P(None, ("dp", "shard")),
    )
    return jax.shard_map(local, mesh=mesh, in_specs=in_specs, out_specs=out_specs, check_vma=False)
```

```python
import math

import jax
import jax.numpy as jnp
from jax import lax
from jax.experimental import pallas as pl
from jax.experimental.pallas import tpu as pltpu
from jax.sharding import PartitionSpec as P

HEADS = 16
KV = 4
HD = 64


EPS = 1e-06


def normalize(values):
    inverse = lax.rsqrt(jnp.mean(values * values, axis=-1, keepdims=True) + EPS)
    return (values * inverse, inverse)


def norm_back(values, inverse, grad_normed):
    cubed = inverse * inverse * inverse
    return inverse * grad_normed - values * cubed * jnp.mean(
        grad_normed * values, axis=-1, keepdims=True
    )


def rotate(values, cos_t, sin_t):
    half_len = values.shape[-1] // 2
    turned = jnp.concatenate([-values[..., half_len:], values[..., :half_len]], axis=-1)
    return values * cos_t + turned * sin_t


def rotate_back(grad_in, cos_t, sin_t):
    half_len = grad_in.shape[-1] // 2
    along = grad_in * sin_t
    return grad_in * cos_t + jnp.concatenate(
        [along[..., half_len:], -along[..., :half_len]], axis=-1
    )


def tables(positions):
    freq = 10000.0 ** (-(2.0 * jnp.arange(HD // 2, dtype=jnp.float32)) / HD)
    angles = positions.astype(jnp.float32)[:, None] * freq[None, :]
    angles = jnp.concatenate([angles, angles], axis=-1)
    return (jnp.cos(angles), jnp.sin(angles))


ANY = pl.BlockSpec(memory_space=pl.ANY)


def swap(values, mask, devices):
    return lax.ppermute(values, ("dp", "shard"), [(i, i ^ mask) for i in range(devices)])


def place(blocks, masks, me, total_rows):
    count = len(blocks)
    sizes = [array.shape[0] // len(own) for array, own in zip(blocks, masks)]
    copies = sum(len(own) for own in masks)

    def kernel(me_ref, *refs):
        sources, out_ref, sems = refs[:count], refs[count], refs[count + 1]
        started = []
        for array, own, size in zip(sources, masks, sizes):
            for at, mask in enumerate(own):
                row = pl.multiple_of((me_ref[0] ^ mask) * size, size)
                copy = pltpu.make_async_copy(
                    array.at[pl.ds(at * size, size)], out_ref.at[pl.ds(row, size)], sems.at[len(started)]
                )
                copy.start()
                started.append(copy)
        for copy in started:
            copy.wait()

    return pl.pallas_call(
        kernel,
        out_shape=jax.ShapeDtypeStruct((total_rows,) + blocks[0].shape[1:], blocks[0].dtype),
        in_specs=[pl.BlockSpec(memory_space=pltpu.SMEM)] + [ANY] * count,
        out_specs=pl.BlockSpec(memory_space=pltpu.VMEM),
        scratch_shapes=[pltpu.SemaphoreType.DMA((copies,))],
        compiler_params=pltpu.CompilerParams(vmem_limit_bytes=20 << 20),
    )(me, *blocks)


def pick(array, orders, me, size):
    copies = sum(len(own) for own in orders)

    def kernel(me_ref, in_ref, *refs):
        outs, sems = refs[:-1], refs[-1]
        started = []
        for out, own in zip(outs, orders):
            for at, mask in enumerate(own):
                row = pl.multiple_of((me_ref[0] ^ mask) * size, size)
                copy = pltpu.make_async_copy(
                    in_ref.at[pl.ds(row, size)], out.at[pl.ds(at * size, size)], sems.at[len(started)]
                )
                copy.start()
                started.append(copy)
        for copy in started:
            copy.wait()

    return pl.pallas_call(
        kernel,
        out_shape=[jax.ShapeDtypeStruct((len(own) * size,) + array.shape[1:], array.dtype) for own in orders],
        in_specs=[pl.BlockSpec(memory_space=pltpu.SMEM), pl.BlockSpec(memory_space=pltpu.VMEM)],
        out_specs=[ANY] * len(orders),
        scratch_shapes=[pltpu.SemaphoreType.DMA((copies,))],
        compiler_params=pltpu.CompilerParams(vmem_limit_bytes=20 << 20),
    )(me, array)


def gather_rows(part, me, devices):
    if devices != 32:
        return lax.all_gather(part, ("dp", "shard"), axis=0, tiled=True)
    zs = [part] + [swap(part, m, devices) for m in (8, 16, 24)]
    near, far = jnp.concatenate(zs[:2]), jnp.concatenate(zs[2:])
    near_x, far_x = swap(near, 4, devices), swap(far, 4, devices)
    near_y, far_y = swap(near, 2, devices), swap(far, 2, devices)
    near_xy, far_xy = swap(near_x, 2, devices), swap(far_y, 4, devices)
    blocks, masks = [], []
    for array, shift, base in (
        (near, 0, 0), (far, 0, 16), (near_x, 4, 0), (far_y, 2, 16),
        (near_y, 2, 0), (far_x, 4, 16), (near_xy, 6, 0), (far_xy, 6, 16),
    ):
        blocks += [array, swap(array, 1, devices)]
        masks += [(base | shift, (base + 8) | shift), (base | shift | 1, (base + 8) | shift | 1)]
    return place(blocks, masks, me, part.shape[0] * devices)


def reduce_rows(grad, me, devices):
    if devices != 32:
        return lax.psum_scatter(
            grad.astype(jnp.float32), ("dp", "shard"), scatter_dimension=0, tiled=True
        )
    size = grad.shape[0] // devices
    order = [2, 10, 6, 14, 20, 28, 22, 30, 0, 8, 4, 12, 16, 24, 18, 26]
    keep, send = pick(grad, [order, [m | 1 for m in order]], me, size)
    came = swap(send, 1, devices)
    low = jnp.bfloat16
    def both(lo, hi):
        return keep[lo * size : hi * size].astype(jnp.float32) + came[lo * size : hi * size].astype(
            jnp.float32
        )
    from_y = swap(both(0, 4).astype(low), 2, devices)
    from_x = swap(both(4, 8).astype(low), 4, devices)
    near = both(8, 12) + from_y.astype(jnp.float32)
    far = both(12, 16) + from_x.astype(jnp.float32)
    from_x = swap(near[2 * size :].astype(low), 4, devices)
    from_y = swap(far[2 * size :].astype(low), 2, devices)
    near = near[: 2 * size] + from_x.astype(jnp.float32)
    far = far[: 2 * size] + from_y.astype(jnp.float32)
    one = swap(near[size:].astype(low), 8, devices)
    two = swap(far[:size].astype(low), 16, devices)
    three = swap(far[size:].astype(low), 24, devices)
    return (
        near[:size]
        + one.astype(jnp.float32)
        + (two.astype(jnp.float32) + three.astype(jnp.float32))
    )


def gather_row(part, devices, shards):
    if shards != 4:
        return lax.all_gather(part, "shard", axis=1, tiled=True)
    at = lax.axis_index("shard").reshape(1)
    flat = part[0]
    over = swap(flat, 2, devices)
    blocks = [flat, swap(flat, 1, devices), over, swap(over, 1, devices)]
    return place(blocks, [(0,), (1,), (2,), (3,)], at, 4 * flat.shape[0])[None]


def reduce_row(grad, devices, shards):
    if shards != 4:
        return lax.psum_scatter(grad, "shard", scatter_dimension=1, tiled=True)
    at = lax.axis_index("shard").reshape(1)
    size = grad.shape[1] // 4
    low = grad[0].astype(jnp.bfloat16)
    keep, send = pick(low, [(0, 2), (1, 3)], at, size)
    both = keep.astype(jnp.float32) + swap(send, 1, devices).astype(jnp.float32)
    over = swap(both[size:].astype(jnp.bfloat16), 2, devices)
    return (both[:size] + over.astype(jnp.float32))[None]


def small_gather(part, devices):
    if devices != 32:
        return lax.all_gather(part, ("dp", "shard"), axis=0)
    rows = part[None]
    for mask in (1, 2, 4, 8, 16):
        rows = jnp.concatenate([rows, swap(rows, mask, devices)])
    me = lax.axis_index("dp") * 4 + lax.axis_index("shard")
    return rows[jnp.arange(devices) ^ me]


def small_reduce(rows, shared, devices):
    if devices != 32:
        own = lax.psum_scatter(rows, ("dp", "shard"), scatter_dimension=0)
        return own, lax.psum(shared, ("dp", "shard"))
    me = lax.axis_index("dp") * 4 + lax.axis_index("shard")
    rows = rows[jnp.arange(devices) ^ me]
    for mask in (16, 8, 4, 2, 1):
        came = swap(jnp.concatenate([rows[mask:], shared]), mask, devices)
        rows, shared = rows[:mask] + came[:mask], shared + came[mask:]
    return rows[0], shared


def unchanged(running):
    return running


def local(
    tokens,
    cotangent,
    lengths,
    slot_sequence,
    attn_gain,
    w_qkv,
    q_gain,
    k_gain,
    w_out,
    ffn_gain,
    w_gate,
    w_up,
    w_down,
):
    row_count, piece_len, model_width = tokens.shape
    group_size = HEADS // KV
    q_width = HEADS * HD
    kv_width = KV * HD
    total_rows = lengths.shape[0]
    row_len = piece_len * lax.axis_size("shard")
    scale_factor = 1.0 / math.sqrt(HD)
    row_valid = jnp.sum(
        jnp.where(
            slot_sequence[:, None] == jnp.arange(total_rows, dtype=jnp.int32)[None, :],
            lengths[None, :],
            0,
        ),
        axis=1,
    )
    longest = jnp.max(row_valid)
    positions = lax.axis_index("shard") * piece_len + jnp.arange(piece_len, dtype=jnp.int32)
    last_query = lax.axis_index("shard") * piece_len + piece_len - 1
    live_mask = (positions[None, :] < row_valid[:, None]).astype(jnp.float32)
    cos_t, sin_t = tables(positions)
    cos_h = cos_t[None, :, None, :]
    sin_h = sin_t[None, :, None, :]
    query_pos = jnp.tile(positions, group_size)
    shards = lax.axis_size("shard")
    devices = lax.axis_size("dp") * shards
    me = (lax.axis_index("dp") * shards + lax.axis_index("shard")).reshape(1)
    gains = small_gather(jnp.concatenate([attn_gain, ffn_gain]).astype(jnp.bfloat16), devices)
    part_len = attn_gain.shape[0]
    gain_attn = gains[:, :part_len].reshape(model_width)
    gain_ffn = gains[:, part_len:].reshape(model_width)
    low = jnp.bfloat16
    wqkv_low = gather_rows(w_qkv.astype(low), me, devices)
    wout_low = gather_rows(w_out.astype(low).T, me, devices)
    wgate_low = gather_rows(w_gate.astype(low), me, devices)
    wup_low = gather_rows(w_up.astype(low), me, devices)
    wdown_low = gather_rows(w_down.astype(low).T, me, devices)
    gain_attn_f = gain_attn.astype(jnp.float32)
    x_float = tokens.astype(jnp.float32)
    normed_one, inverse_one = normalize(x_float)
    normed_low = (normed_one * gain_attn_f).astype(jnp.bfloat16)
    projected = jnp.einsum("rtd,de->rte", normed_low, wqkv_low, preferred_element_type=jnp.float32)
    q_raw = projected[..., :q_width].reshape(row_count, piece_len, HEADS, HD)
    k_raw = projected[..., q_width : q_width + kv_width].reshape(row_count, piece_len, KV, HD)
    v_raw = projected[..., q_width + kv_width :]
    q_unit, q_inverse = normalize(q_raw)
    k_unit, k_inverse = normalize(k_raw)
    q_low = rotate(q_unit * q_gain, cos_h, sin_h).astype(jnp.bfloat16)
    k_low = (
        rotate(k_unit * k_gain, cos_h, sin_h)
        .astype(jnp.bfloat16)
        .reshape(row_count, piece_len, kv_width)
    )
    v_low = v_raw.astype(jnp.bfloat16)
    q_group = (
        q_low.reshape(row_count, piece_len, KV, group_size, HD)
        .transpose(0, 2, 3, 1, 4)
        .reshape(row_count, KV, group_size * piece_len, HD)
    )

    def block_scores(key_piece, value_piece, offset, block_len):
        k_block = lax.dynamic_slice_in_dim(key_piece, offset, block_len, 1).reshape(
            row_count, block_len, KV, HD
        )
        v_block = lax.dynamic_slice_in_dim(value_piece, offset, block_len, 1).reshape(
            row_count, block_len, KV, HD
        )
        scores = scale_factor * jnp.einsum(
            "rgqh,rkgh->rgqk", q_group, k_block, preferred_element_type=jnp.float32
        )
        key_pos = offset + jnp.arange(block_len, dtype=jnp.int32)
        allowed = (key_pos[None, None, None, :] <= query_pos[None, None, :, None]) & (
            key_pos[None, None, None, :] < row_valid[:, None, None, None]
        )
        return (k_block, v_block, jnp.where(allowed, jnp.exp(scores), 0.0))

    def block_used(key_start):
        return (key_start <= last_query) & (key_start < longest)

    zero_accum = jnp.zeros((row_count, KV, group_size * piece_len, HD), jnp.float32)
    zero_sums = jnp.zeros((row_count, KV, group_size * piece_len), jnp.float32)
    both_piece = gather_row(jnp.concatenate([k_low, v_low], axis=-1), devices, shards)
    key_piece, value_piece = both_piece[..., :kv_width], both_piece[..., kv_width:]
    block_len = math.gcd(key_piece.shape[1], piece_len)
    block_count = key_piece.shape[1] // block_len

    def fold_block(block_index, running):
        offset = block_index * block_len

        def compute(state):
            accum_out, row_sums = state
            k_block, v_block, exps = block_scores(key_piece, value_piece, offset, block_len)
            row_sums = row_sums + jnp.sum(exps, axis=-1)
            accum_out = accum_out + jnp.einsum(
                "rgqk,rkgh->rgqh",
                exps.astype(jnp.bfloat16),
                v_block,
                preferred_element_type=jnp.float32,
            )
            return (accum_out, row_sums)

        return lax.cond(block_used(offset), compute, unchanged, running)

    accum_out, denominator = lax.fori_loop(0, block_count, fold_block, (zero_accum, zero_sums))
    o_group = accum_out / denominator[..., None]
    att_low = (
        o_group.reshape(row_count, KV, group_size, piece_len, HD)
        .transpose(0, 3, 1, 2, 4)
        .reshape(row_count, piece_len, q_width)
        .astype(jnp.bfloat16)
    )
    x_mid = x_float + jnp.einsum(
        "rtc,dc->rtd", att_low, wout_low, preferred_element_type=jnp.float32
    )
    gain_ffn_f = gain_ffn.astype(jnp.float32)
    normed_two, inverse_two = normalize(x_mid)
    ffn_in = (normed_two * gain_ffn_f).astype(jnp.bfloat16)
    gate_proj = jnp.einsum("rtd,df->rtf", ffn_in, wgate_low, preferred_element_type=jnp.float32)
    up_proj = jnp.einsum("rtd,df->rtf", ffn_in, wup_low, preferred_element_type=jnp.float32)
    gate_sig = jax.nn.sigmoid(gate_proj)
    silu_gate = gate_proj * gate_sig
    activated = (silu_gate * up_proj).astype(jnp.bfloat16)
    result = x_mid + jnp.einsum(
        "rtf,df->rtd", activated, wdown_low, preferred_element_type=jnp.float32
    )
    output = result.astype(jnp.bfloat16)
    grad_out = cotangent.astype(jnp.float32) * live_mask[..., None]
    grad_low = grad_out.astype(jnp.bfloat16)
    gain_ffn_k = gain_ffn_f
    wgate_k, wup_k, wdown_k = wgate_low, wup_low, wdown_low
    grad_down = jnp.einsum("rtd,rtf->df", grad_low, activated, preferred_element_type=jnp.float32).astype(low)
    grad_act = jnp.einsum("rtd,df->rtf", grad_low, wdown_k, preferred_element_type=jnp.float32)
    grad_gate = (grad_act * up_proj * gate_sig * (1.0 + gate_proj * (1.0 - gate_sig))).astype(
        jnp.bfloat16
    )
    grad_up = (grad_act * silu_gate).astype(jnp.bfloat16)
    grad_wgate = jnp.einsum("rtd,rtf->df", ffn_in, grad_gate, preferred_element_type=jnp.float32).astype(low)
    grad_wup = jnp.einsum("rtd,rtf->df", ffn_in, grad_up, preferred_element_type=jnp.float32).astype(low)
    grad_ffn_in = jnp.einsum(
        "rtf,df->rtd", grad_gate, wgate_k, preferred_element_type=jnp.float32
    ) + jnp.einsum("rtf,df->rtd", grad_up, wup_k, preferred_element_type=jnp.float32)
    grad_gain_two = jnp.sum(grad_ffn_in * normed_two, axis=(0, 1))
    grad_mid = grad_out + norm_back(x_mid, inverse_two, grad_ffn_in * gain_ffn_k)
    summed_down = reduce_rows(grad_down, me, devices).T
    summed_wgate = reduce_rows(grad_wgate, me, devices)
    summed_wup = reduce_rows(grad_wup, me, devices)
    wqkv_k, wout_k, gain_attn_k = wqkv_low, wout_low, gain_attn_f
    mid_low = grad_mid.astype(jnp.bfloat16)
    grad_wout = jnp.einsum("rtd,rtc->dc", mid_low, att_low, preferred_element_type=jnp.float32).astype(low)
    summed_wout = reduce_rows(grad_wout, me, devices).T
    grad_att = jnp.einsum("rtd,dc->rtc", mid_low, wout_k, preferred_element_type=jnp.float32)
    grad_group = (
        grad_att.reshape(row_count, piece_len, KV, group_size, HD)
        .transpose(0, 2, 3, 1, 4)
        .reshape(row_count, KV, group_size * piece_len, HD)
    )
    grad_sums = -jnp.sum(grad_group * o_group, axis=-1) / denominator
    grad_accum = (grad_group / denominator[..., None]).astype(jnp.bfloat16)
    zero_keys = jnp.zeros((row_count, row_len, kv_width), jnp.float32)
    attend_key_piece, attend_value_piece = key_piece, value_piece
    attend_block_len = math.gcd(attend_key_piece.shape[1], piece_len)
    block_count = attend_key_piece.shape[1] // attend_block_len

    def fold_block(block_index, running):
        offset = block_index * attend_block_len
        key_start = offset

        def compute(state):
            grad_query, grad_keys, grad_values = state
            k_block, v_block, exps = block_scores(
                attend_key_piece, attend_value_piece, offset, attend_block_len
            )
            grad_exps = (
                jnp.einsum(
                    "rgqh,rkgh->rgqk", grad_accum, v_block, preferred_element_type=jnp.float32
                )
                + grad_sums[..., None]
            )
            grad_scores = (exps * grad_exps).astype(jnp.bfloat16)
            grad_query = grad_query + scale_factor * jnp.einsum(
                "rgqk,rkgh->rgqh", grad_scores, k_block, preferred_element_type=jnp.float32
            )
            part_keys = scale_factor * jnp.einsum(
                "rgqk,rgqh->rkgh", grad_scores, q_group, preferred_element_type=jnp.float32
            )
            part_values = jnp.einsum(
                "rgqk,rgqh->rkgh",
                exps.astype(jnp.bfloat16),
                grad_accum,
                preferred_element_type=jnp.float32,
            )
            old_keys = lax.dynamic_slice_in_dim(grad_keys, key_start, attend_block_len, 1)
            old_values = lax.dynamic_slice_in_dim(grad_values, key_start, attend_block_len, 1)
            grad_keys = lax.dynamic_update_slice_in_dim(
                grad_keys,
                old_keys + part_keys.reshape(row_count, attend_block_len, kv_width),
                key_start,
                1,
            )
            grad_values = lax.dynamic_update_slice_in_dim(
                grad_values,
                old_values + part_values.reshape(row_count, attend_block_len, kv_width),
                key_start,
                1,
            )
            return (grad_query, grad_keys, grad_values)

        return lax.cond(block_used(key_start), compute, unchanged, running)

    grad_query, grad_keys_all, grad_values_all = lax.fori_loop(
        0, block_count, fold_block, (zero_accum, zero_keys, zero_keys)
    )
    grad_both = reduce_row(jnp.concatenate([grad_keys_all, grad_values_all], axis=-1), devices, shards)
    grad_keys, grad_values = grad_both[..., :kv_width], grad_both[..., kv_width:]
    grad_q_heads = (
        grad_query.reshape(row_count, KV, group_size, piece_len, HD)
        .transpose(0, 3, 1, 2, 4)
        .reshape(row_count, piece_len, HEADS, HD)
    )
    grad_q_scaled = rotate_back(grad_q_heads, cos_h, sin_h)
    grad_qgain = jnp.sum(grad_q_scaled * q_unit, axis=(0, 1, 2))
    grad_q_raw = norm_back(q_raw, q_inverse, grad_q_scaled * q_gain)
    grad_k_scaled = rotate_back(grad_keys.reshape(row_count, piece_len, KV, HD), cos_h, sin_h)
    grad_kgain = jnp.sum(grad_k_scaled * k_unit, axis=(0, 1, 2))
    grad_k_raw = norm_back(k_raw, k_inverse, grad_k_scaled * k_gain)
    grad_projected = jnp.concatenate(
        [
            grad_q_raw.reshape(row_count, piece_len, q_width),
            grad_k_raw.reshape(row_count, piece_len, kv_width),
            grad_values,
        ],
        axis=-1,
    ).astype(jnp.bfloat16)
    grad_wqkv = jnp.einsum(
        "rtd,rte->de", normed_low, grad_projected, preferred_element_type=jnp.float32
    ).astype(low)
    grad_normed = jnp.einsum(
        "rte,de->rtd", grad_projected, wqkv_k, preferred_element_type=jnp.float32
    )
    grad_gain_one = jnp.sum(grad_normed * normed_one, axis=(0, 1))
    input_grad = grad_mid + norm_back(x_float, inverse_one, grad_normed * gain_attn_k)
    summed_wqkv = reduce_rows(grad_wqkv, me, devices)
    own, shared = small_reduce(
        jnp.concatenate(
            [grad_gain_one.reshape(devices, part_len), grad_gain_two.reshape(devices, part_len)], axis=1
        ),
        jnp.concatenate([grad_qgain, grad_kgain])[None],
        devices,
    )
    summed_gain_one, summed_gain_two = own[:part_len], own[part_len:]
    summed_qgain, summed_kgain = shared[0, :HD], shared[0, HD:]
    return (
        output,
        input_grad,
        summed_gain_one,
        summed_wqkv,
        summed_qgain,
        summed_kgain,
        summed_wout,
        summed_gain_two,
        summed_wgate,
        summed_wup,
        summed_down,
    )


def solution(mesh):
    in_specs = (
        P("dp", "shard", None),
        P("dp", "shard", None),
        P(),
        P("dp"),
        P(("dp", "shard")),
        P(("dp", "shard"), None),
        P(),
        P(),
        P(None, ("dp", "shard")),
        P(("dp", "shard")),
        P(("dp", "shard"), None),
        P(("dp", "shard"), None),
        P(None, ("dp", "shard")),
    )
    out_specs = (
        P("dp", "shard", None),
        P("dp", "shard", None),
        P(("dp", "shard")),
        P(("dp", "shard"), None),
        P(),
        P(),
        P(None, ("dp", "shard")),
        P(("dp", "shard")),
        P(("dp", "shard"), None),
        P(("dp", "shard"), None),
        P(None, ("dp", "shard")),
    )
    return jax.shard_map(local, mesh=mesh, in_specs=in_specs, out_specs=out_specs, check_vma=False)
```

```python
import functools
import math

import jax
import jax.numpy as jnp
from jax import lax
from jax.experimental import pallas as pl
from jax.experimental.pallas import tpu as pltpu
from jax.sharding import PartitionSpec as P

HEADS = 16
KV = 4
HD = 64
GROUP = HEADS // KV
EPS = 1e-06
LOW = jnp.bfloat16
ANY = pl.BlockSpec(memory_space=pl.ANY)
VMEM = pl.BlockSpec(memory_space=pltpu.VMEM)
SMEM = pl.BlockSpec(memory_space=pltpu.SMEM)
FIRST_FIRST = (((0,), (0,)), ((), ()))
LAST_FIRST = (((1,), (0,)), ((), ()))
LAST_LAST = (((1,), (1,)), ((), ()))


def dot(left, right, dims):
    return lax.dot_general(left, right, dims, preferred_element_type=jnp.float32)


def normalize(values, axis=-1):
    inverse = lax.rsqrt(jnp.mean(values * values, axis=axis, keepdims=True) + EPS)
    return (values * inverse, inverse)


def norm_back(values, inverse, grad_normed, axis=-1):
    cubed = inverse * inverse * inverse
    return inverse * grad_normed - values * cubed * jnp.mean(
        grad_normed * values, axis=axis, keepdims=True
    )


def rotate(values, cos_t, sin_t):
    half_len = HD // 2
    turned = jnp.concatenate([-values[:, :, half_len:], values[:, :, :half_len]], axis=2)
    return values * cos_t + turned * sin_t


def rotate_back(grad_in, cos_t, sin_t):
    half_len = HD // 2
    along = grad_in * sin_t
    return grad_in * cos_t + jnp.concatenate([along[:, :, half_len:], -along[:, :, :half_len]], axis=2)


def tables(positions):
    freq = 10000.0 ** (-(2.0 * jnp.arange(HD // 2, dtype=jnp.float32)) / HD)
    angles = freq[:, None] * positions.astype(jnp.float32)[None, :]
    angles = jnp.concatenate([angles, angles], axis=0)
    return (jnp.cos(angles), jnp.sin(angles))


def swap(values, mask, devices):
    return lax.ppermute(values, ("dp", "shard"), [(i, i ^ mask) for i in range(devices)])


def place(blocks, masks, widths, me, total_rows):
    count = len(blocks)
    size = blocks[0].shape[0] // len(masks[0])
    copies = sum(len(own) for own in masks) * len(widths)

    def kernel(me_ref, *refs):
        sources, outs, sems = refs[:count], refs[count:-1], refs[-1]
        started = []
        for array, own in zip(sources, masks):
            for at, mask in enumerate(own):
                row = pl.multiple_of((me_ref[0] ^ mask) * size, size)
                column = 0
                for out, width in zip(outs, widths):
                    copy = pltpu.make_async_copy(
                        array.at[pl.ds(at * size, size), pl.ds(column, width)],
                        out.at[pl.ds(row, size)],
                        sems.at[len(started)],
                    )
                    copy.start()
                    started.append(copy)
                    column += width
        for copy in started:
            copy.wait()

    return pl.pallas_call(
        kernel,
        out_shape=[jax.ShapeDtypeStruct((total_rows, width), blocks[0].dtype) for width in widths],
        in_specs=[SMEM] + [ANY] * count,
        out_specs=[VMEM] * len(widths),
        scratch_shapes=[pltpu.SemaphoreType.DMA((copies,))],
        compiler_params=pltpu.CompilerParams(vmem_limit_bytes=24 << 20),
    )(me, *blocks)


def pick(arrays, orders, me, size):
    count = len(arrays)
    copies = sum(len(own) for own in orders) * count
    width = sum(array.shape[1] for array in arrays)

    def kernel(me_ref, *refs):
        sources, outs, sems = refs[:count], refs[count:-1], refs[-1]
        started = []
        for out, own in zip(outs, orders):
            for at, mask in enumerate(own):
                row = pl.multiple_of((me_ref[0] ^ mask) * size, size)
                column = 0
                for array in sources:
                    copy = pltpu.make_async_copy(
                        array.at[pl.ds(row, size)],
                        out.at[pl.ds(at * size, size), pl.ds(column, array.shape[1])],
                        sems.at[len(started)],
                    )
                    copy.start()
                    started.append(copy)
                    column += array.shape[1]
        for copy in started:
            copy.wait()

    return pl.pallas_call(
        kernel,
        out_shape=[jax.ShapeDtypeStruct((len(own) * size, width), arrays[0].dtype) for own in orders],
        in_specs=[SMEM] + [VMEM] * count,
        out_specs=[ANY] * len(orders),
        scratch_shapes=[pltpu.SemaphoreType.DMA((copies,))],
        compiler_params=pltpu.CompilerParams(vmem_limit_bytes=24 << 20),
    )(me, *arrays)


def gather_rows(parts, me, devices):
    part = jnp.concatenate(parts, axis=1)
    widths = [one.shape[1] for one in parts]
    if devices != 32:
        whole = lax.all_gather(part, ("dp", "shard"), axis=0, tiled=True)
        return jnp.split(whole, [sum(widths[:i]) for i in range(1, len(widths))], axis=1)
    near = jnp.concatenate([part, swap(part, 8, devices)])
    far = jnp.concatenate([swap(part, 16, devices), swap(part, 24, devices)])
    near = jnp.concatenate([near, swap(near, 4, devices)])
    far = jnp.concatenate([far, swap(far, 2, devices)])
    near_masks, far_masks = (0, 8, 4, 12), (16, 24, 18, 26)
    blocks, masks = [near, far], [near_masks, far_masks]
    blocks += [swap(near, 2, devices), swap(far, 4, devices)]
    masks += [tuple(m | 2 for m in near_masks), tuple(m | 4 for m in far_masks)]
    blocks += [swap(block, 1, devices) for block in blocks]
    masks += [tuple(m | 1 for m in own) for own in masks]
    return place(blocks, masks, widths, me, part.shape[0] * devices)


def reduce_rows(grads, me, devices):
    if devices != 32:
        grad = jnp.concatenate([one.astype(jnp.float32) for one in grads], axis=1)
        return lax.psum_scatter(grad, ("dp", "shard"), scatter_dimension=0, tiled=True)
    size = grads[0].shape[0] // devices
    order = [2, 10, 6, 14, 20, 28, 22, 30, 0, 8, 4, 12, 16, 24, 18, 26]
    keep, send = pick(grads, [order, [m | 1 for m in order]], me, size)
    came = swap(send, 1, devices)

    def both(low, high):
        rows = slice(low * size, high * size)
        return keep[rows].astype(jnp.float32) + came[rows].astype(jnp.float32)

    from_y = swap(both(0, 4).astype(LOW), 2, devices)
    from_x = swap(both(4, 8).astype(LOW), 4, devices)
    near = both(8, 12) + from_y.astype(jnp.float32)
    far = both(12, 16) + from_x.astype(jnp.float32)
    from_x = swap(near[2 * size :].astype(LOW), 4, devices)
    from_y = swap(far[2 * size :].astype(LOW), 2, devices)
    near = near[: 2 * size] + from_x.astype(jnp.float32)
    far = far[: 2 * size] + from_y.astype(jnp.float32)
    one = swap(near[size:].astype(LOW), 8, devices)
    two = swap(far[:size].astype(LOW), 16, devices)
    three = swap(far[size:].astype(LOW), 24, devices)
    return (near[:size] + one.astype(jnp.float32)) + (two.astype(jnp.float32) + three.astype(jnp.float32))


def gather_pieces(part, devices, shards):
    at = lax.axis_index("shard")
    if shards != 4 or devices != 32:
        return lax.all_gather(part, "shard", axis=0), jnp.arange(shards, dtype=jnp.int32)
    over = swap(part, 2, devices)
    pieces = jnp.stack([part, swap(part, 1, devices), over, swap(over, 1, devices)])
    return pieces, jnp.arange(4, dtype=jnp.int32) ^ at


def reduce_pieces(grad, devices, shards):
    if shards != 4 or devices != 32:
        return lax.psum_scatter(grad, "shard", scatter_dimension=0)
    came = swap(jnp.stack([grad[1], grad[3]]).astype(LOW), 1, devices).astype(jnp.float32)
    over = swap((grad[2] + came[1]).astype(LOW), 2, devices)
    return grad[0] + came[0] + over.astype(jnp.float32)


def sum_over_devices(values, devices):
    if devices != 32:
        return lax.psum(values, ("dp", "shard"))
    for mask in (16, 8, 4, 2, 1):
        values = values + swap(values, mask, devices)
    return values


def allowed(base, start, valid, key_axis, shape):
    key = base + lax.broadcasted_iota(jnp.int32, shape, key_axis)
    query = start + lax.broadcasted_iota(jnp.int32, shape, 1 - key_axis)
    return (key <= query) & (key < valid)


def over_pieces(info_ref, pieces, length, row, tile, before=None, after=None):
    start, valid = info_ref[0], info_ref[1 + pieces + row]

    def one(piece, carry):
        base = info_ref[1 + piece]
        if before is not None:
            before()
        used = (base < start + length) & (base < valid)
        full = (base + length <= start) & (base + length <= valid)
        pl.when(used & full)(lambda: tile(piece, None))
        pl.when(used & jnp.logical_not(full))(lambda: tile(piece, (base, start, valid)))
        if after is not None:
            after(piece)
        return carry

    lax.fori_loop(0, pieces, one, 0)


def attention(info, queries, keys_values):
    rows, _, length = queries.shape
    pieces = keys_values.shape[0]
    group_width = GROUP * HD

    def kernel(info_ref, q_ref, k_ref, v_ref, out_ref, low_ref, sums_ref, accum_ref, part_ref):
        accum_ref[...] = jnp.zeros_like(accum_ref)
        part_ref[...] = jnp.zeros_like(part_ref)

        def tile(piece, bounds):
            key_t, value_t = k_ref[piece, 0], v_ref[piece, 0]
            if bounds is not None:
                mask = allowed(*bounds, 1, (length, length))
            for head in range(GROUP):
                exps = jnp.exp(dot(q_ref[0, head * HD : (head + 1) * HD, :], key_t, FIRST_FIRST))
                if bounds is not None:
                    exps = jnp.where(mask, exps, 0.0)
                width = min(128, length)
                part = exps[:, :width]
                for at in range(width, length, width):
                    part = part + exps[:, at : at + width]
                part_ref[head] += part
                accum_ref[head] += dot(exps.astype(LOW), value_t, LAST_LAST)

        over_pieces(info_ref, pieces, length, pl.program_id(0), tile)
        for head in range(GROUP):
            own = slice(head * HD, (head + 1) * HD)
            sums = jnp.sum(part_ref[head].T, axis=0, keepdims=True)
            sums_ref[0, 0, head : head + 1, :] = sums
            out = accum_ref[head].T / sums
            out_ref[0, own, :] = out
            low_ref[0, own, :] = out.astype(LOW)

    q_spec = pl.BlockSpec((1, group_width, length), lambda row, group, *_: (row, group, 0))
    k_spec = pl.BlockSpec((pieces, 1, HD, length), lambda row, group, *_: (0, row, group, 0))
    v_spec = pl.BlockSpec((pieces, 1, HD, length), lambda row, group, *_: (0, row, group + KV, 0))
    s_spec = pl.BlockSpec((1, 1, GROUP, length), lambda row, group, *_: (row, group, 0, 0))
    work = rows * HEADS * length * length * pieces
    return pl.pallas_call(
        kernel,
        out_shape=[
            jax.ShapeDtypeStruct(queries.shape, jnp.float32),
            jax.ShapeDtypeStruct(queries.shape, LOW),
            jax.ShapeDtypeStruct((rows, KV, GROUP, length), jnp.float32),
        ],
        grid_spec=pltpu.PrefetchScalarGridSpec(
            num_scalar_prefetch=1,
            grid=(rows, KV),
            in_specs=[q_spec, k_spec, v_spec],
            out_specs=[q_spec, q_spec, s_spec],
            scratch_shapes=[
                pltpu.VMEM((GROUP, length, HD), jnp.float32),
                pltpu.VMEM((GROUP, length, min(128, length)), jnp.float32),
            ],
        ),
        compiler_params=pltpu.CompilerParams(vmem_limit_bytes=40 << 20),
        cost_estimate=pl.CostEstimate(flops=work * 1000, transcendentals=work, bytes_accessed=10 << 20),
    )(info, queries, keys_values, keys_values)


def attention_back(info, queries, keys_values, out, sums, grad_out, first, groups):
    rows, _, length = queries.shape
    pieces = keys_values.shape[0]
    group_width = GROUP * HD

    def kernel(
        info_ref, q_ref, k_ref, v_ref, out_ref, sums_ref, grad_ref, dq_ref, dk_ref, dv_ref,
        grad_low, grad_sums, q_rows, grad_rows, k_accum, v_accum,
    ):
        dq_ref[...] = jnp.zeros_like(dq_ref)
        for head in range(GROUP):
            own = slice(head * HD, (head + 1) * HD)
            inverse = 1.0 / sums_ref[0, 0, head : head + 1, :]
            grad = grad_ref[0, own, :]
            grad_sums[head] = -jnp.sum(grad * out_ref[0, own, :], axis=0, keepdims=True) * inverse
            scaled = grad * inverse
            grad_low[own, :] = scaled.astype(LOW)
            grad_rows[head] = scaled.T.astype(LOW)
            q_rows[head] = q_ref[0, own, :].T

        def tile(piece, bounds):
            key_t, value_t = k_ref[piece, 0], v_ref[piece, 0]
            if bounds is not None:
                mask = allowed(*bounds, 0, (length, length))
            for head in range(GROUP):
                own = slice(head * HD, (head + 1) * HD)
                exps = jnp.exp(dot(key_t, q_ref[0, own, :], FIRST_FIRST))
                if bounds is not None:
                    exps = jnp.where(mask, exps, 0.0)
                grad_exps = dot(value_t, grad_low[own, :], FIRST_FIRST) + grad_sums[head]
                grad_scores = (exps * grad_exps).astype(LOW)
                v_accum[...] += dot(exps.astype(LOW), grad_rows[head], LAST_FIRST)
                k_accum[...] += dot(grad_scores, q_rows[head], LAST_FIRST)
                dq_ref[0, own, :] += dot(key_t, grad_scores, LAST_FIRST)

        def before():
            k_accum[...] = jnp.zeros_like(k_accum)
            v_accum[...] = jnp.zeros_like(v_accum)

        def after(piece):
            dk_ref[piece, 0] = k_accum[...].T
            dv_ref[piece, 0] = v_accum[...].T

        over_pieces(info_ref, pieces, length, pl.program_id(0), tile, before, after)

    q_spec = pl.BlockSpec((1, group_width, length), lambda row, group, *_: (row, group + first, 0))
    k_spec = pl.BlockSpec((pieces, 1, HD, length), lambda row, group, *_: (0, row, group + first, 0))
    v_spec = pl.BlockSpec(
        (pieces, 1, HD, length), lambda row, group, *_: (0, row, group + first + KV, 0)
    )
    s_spec = pl.BlockSpec((1, 1, GROUP, length), lambda row, group, *_: (row, group + first, 0, 0))
    dq_spec = pl.BlockSpec((1, group_width, length), lambda row, group, *_: (row, group, 0))
    dk_spec = pl.BlockSpec((pieces, 1, HD, length), lambda row, group, *_: (0, row, group, 0))
    work = rows * groups * GROUP * length * length * pieces
    pieces_shape = jax.ShapeDtypeStruct((pieces, rows, groups * HD, length), jnp.float32)
    return pl.pallas_call(
        kernel,
        out_shape=[
            jax.ShapeDtypeStruct((rows, groups * group_width, length), jnp.float32),
            pieces_shape,
            pieces_shape,
        ],
        grid_spec=pltpu.PrefetchScalarGridSpec(
            num_scalar_prefetch=1,
            grid=(rows, groups),
            in_specs=[q_spec, k_spec, v_spec, q_spec, s_spec, q_spec],
            out_specs=[dq_spec, dk_spec, dk_spec],
            scratch_shapes=[
                pltpu.VMEM((group_width, length), LOW),
                pltpu.VMEM((GROUP, 1, length), jnp.float32),
                pltpu.VMEM((GROUP, length, HD), LOW),
                pltpu.VMEM((GROUP, length, HD), LOW),
                pltpu.VMEM((length, HD), jnp.float32),
                pltpu.VMEM((length, HD), jnp.float32),
            ],
        ),
        compiler_params=pltpu.CompilerParams(vmem_limit_bytes=40 << 20),
        cost_estimate=pl.CostEstimate(flops=work * 2500, transcendentals=work, bytes_accessed=10 << 20),
    )(info, queries, keys_values, keys_values, out, sums, grad_out)


def local(
    tokens,
    cotangent,
    lengths,
    slot_sequence,
    attn_gain,
    w_qkv,
    q_gain,
    k_gain,
    w_out,
    ffn_gain,
    w_gate,
    w_up,
    w_down,
):
    row_count, piece_len, model_width = tokens.shape
    q_width = HEADS * HD
    kv_width = KV * HD
    total_rows = lengths.shape[0]
    scale_factor = 1.0 / math.sqrt(HD)
    shards = lax.axis_size("shard")
    devices = lax.axis_size("dp") * shards
    part_len = attn_gain.shape[0]
    shard_at = lax.axis_index("shard")
    me = (lax.axis_index("dp") * shards + shard_at).astype(jnp.int32).reshape(1)
    row_valid = jnp.sum(
        jnp.where(
            slot_sequence[:, None] == jnp.arange(total_rows, dtype=jnp.int32)[None, :],
            lengths[None, :],
            0,
        ),
        axis=1,
    )
    start = (shard_at * piece_len).astype(jnp.int32)
    positions = start + jnp.arange(piece_len, dtype=jnp.int32)
    live_mask = (positions[None, :] < row_valid[:, None]).astype(jnp.float32)
    cos_t, sin_t = tables(positions)
    cos_h = cos_t[None, None]
    sin_h = sin_t[None, None]
    q_gain_h = q_gain[None, None, :, None]
    k_gain_h = k_gain[None, None, :, None]

    gain_columns = jnp.concatenate(
        [attn_gain[:, None], ffn_gain[:, None], jnp.zeros((part_len, 126), jnp.float32)], axis=1
    )
    wqkv, gains = gather_rows([w_qkv.astype(LOW), gain_columns.astype(LOW)], me, devices)
    wout, wgate = gather_rows([w_out.astype(LOW).T, w_gate.astype(LOW)], me, devices)
    wup, wdown = gather_rows([w_up.astype(LOW), w_down.astype(LOW).T], me, devices)
    gain_attn = gains[:, 0].astype(jnp.float32)
    gain_ffn = gains[:, 1].astype(jnp.float32)

    x_float = tokens.astype(jnp.float32)
    normed_one, inverse_one = normalize(x_float)
    normed_low = (normed_one * gain_attn).astype(LOW)
    projected = jnp.einsum("rtd,de->ret", normed_low, wqkv, preferred_element_type=jnp.float32)
    q_raw = projected[:, :q_width].reshape(row_count, HEADS, HD, piece_len)
    k_raw = projected[:, q_width : q_width + kv_width].reshape(row_count, KV, HD, piece_len)
    v_raw = projected[:, q_width + kv_width :]
    q_unit, q_inverse = normalize(q_raw, 2)
    k_unit, k_inverse = normalize(k_raw, 2)
    q_low = (
        rotate(q_unit * q_gain_h, cos_h, sin_h).astype(LOW) * jnp.array(scale_factor, LOW)
    ).reshape(row_count, q_width, piece_len)
    k_low = rotate(k_unit * k_gain_h, cos_h, sin_h).astype(LOW).reshape(row_count, kv_width, piece_len)
    own_kv = jnp.concatenate([k_low, v_raw.astype(LOW)], axis=1)
    pieces, piece_at = gather_pieces(own_kv, devices, shards)
    info = jnp.concatenate([start.reshape(1), piece_at * piece_len, row_valid]).astype(jnp.int32)
    o_heads, att_low, sums = attention(info, q_low, pieces)
    x_mid = x_float + jnp.einsum("rct,dc->rtd", att_low, wout, preferred_element_type=jnp.float32)
    normed_two, inverse_two = normalize(x_mid)
    ffn_in = (normed_two * gain_ffn).astype(LOW)
    gate_proj = jnp.einsum("rtd,df->rtf", ffn_in, wgate, preferred_element_type=jnp.float32)
    up_proj = jnp.einsum("rtd,df->rtf", ffn_in, wup, preferred_element_type=jnp.float32)
    gate_sig = jax.nn.sigmoid(gate_proj)
    silu_gate = gate_proj * gate_sig
    activated = (silu_gate * up_proj).astype(LOW)
    output = (
        x_mid + jnp.einsum("rtf,df->rtd", activated, wdown, preferred_element_type=jnp.float32)
    ).astype(LOW)

    grad_out = cotangent.astype(jnp.float32) * live_mask[..., None]
    grad_low = grad_out.astype(LOW)
    grad_down = jnp.einsum("rtd,rtf->df", grad_low, activated, preferred_element_type=jnp.float32)
    grad_act = jnp.einsum("rtd,df->rtf", grad_low, wdown, preferred_element_type=jnp.float32)
    grad_gate = (grad_act * up_proj * gate_sig * (1.0 + gate_proj * (1.0 - gate_sig))).astype(LOW)
    grad_up = (grad_act * silu_gate).astype(LOW)
    grad_wgate = jnp.einsum("rtd,rtf->df", ffn_in, grad_gate, preferred_element_type=jnp.float32)
    grad_wup = jnp.einsum("rtd,rtf->df", ffn_in, grad_up, preferred_element_type=jnp.float32)
    one = reduce_rows([grad_down.astype(LOW), grad_wgate.astype(LOW)], me, devices)
    width = grad_down.shape[1]
    summed_down, summed_wgate = one[:, :width].T, one[:, width:]
    grad_ffn_in = jnp.einsum(
        "rtf,df->rtd", grad_gate, wgate, preferred_element_type=jnp.float32
    ) + jnp.einsum("rtf,df->rtd", grad_up, wup, preferred_element_type=jnp.float32)
    grad_gain_two = jnp.sum(grad_ffn_in * normed_two, axis=(0, 1))
    grad_mid = grad_out + norm_back(x_mid, inverse_two, grad_ffn_in * gain_ffn)
    mid_low = grad_mid.astype(LOW)
    grad_wout = jnp.einsum("rtd,rct->dc", mid_low, att_low, preferred_element_type=jnp.float32)
    two = reduce_rows([grad_wup.astype(LOW), grad_wout.astype(LOW)], me, devices)
    summed_wup, summed_wout = two[:, :width], two[:, width:].T
    grad_att = jnp.einsum("rtd,dc->rct", mid_low, wout, preferred_element_type=jnp.float32)
    dq_parts, dk_parts, dv_parts = [], [], []
    for group in range(KV):
        dq, dk, dv = attention_back(info, q_low, pieces, o_heads, sums, grad_att, group, 1)
        dq_parts.append(dq)
        dk_parts.append(dk)
        dv_parts.append(dv)
    grad_query = jnp.concatenate(dq_parts, axis=1)
    grad_pieces = jnp.concatenate(dk_parts + dv_parts, axis=2)
    grad_kv = reduce_pieces(grad_pieces, devices, shards)
    grad_q_scaled = rotate_back(
        scale_factor * grad_query.reshape(row_count, HEADS, HD, piece_len), cos_h, sin_h
    )
    grad_qgain = jnp.sum(grad_q_scaled * q_unit, axis=(0, 1, 3))
    grad_q_raw = norm_back(q_raw, q_inverse, grad_q_scaled * q_gain_h, 2)
    grad_k_scaled = rotate_back(
        grad_kv[:, :kv_width].reshape(row_count, KV, HD, piece_len), cos_h, sin_h
    )
    grad_kgain = jnp.sum(grad_k_scaled * k_unit, axis=(0, 1, 3))
    grad_k_raw = norm_back(k_raw, k_inverse, grad_k_scaled * k_gain_h, 2)
    shared = sum_over_devices(jnp.concatenate([grad_qgain, grad_kgain])[None], devices)
    grad_projected = jnp.concatenate(
        [
            grad_q_raw.reshape(row_count, q_width, piece_len),
            grad_k_raw.reshape(row_count, kv_width, piece_len),
            grad_kv[:, kv_width:],
        ],
        axis=1,
    ).astype(LOW)
    grad_wqkv = jnp.einsum("rtd,ret->de", normed_low, grad_projected, preferred_element_type=jnp.float32)
    grad_normed = jnp.einsum("ret,de->rtd", grad_projected, wqkv, preferred_element_type=jnp.float32)
    grad_gain_one = jnp.sum(grad_normed * normed_one, axis=(0, 1))
    input_grad = grad_mid + norm_back(x_float, inverse_one, grad_normed * gain_attn)
    grad_gains = jnp.concatenate(
        [grad_gain_one[:, None], grad_gain_two[:, None], jnp.zeros((model_width, 126), jnp.float32)],
        axis=1,
    )
    three = reduce_rows([grad_wqkv.astype(LOW), grad_gains.astype(LOW)], me, devices)
    qkv_width = w_qkv.shape[1]
    return (
        output,
        input_grad,
        three[:, qkv_width],
        three[:, :qkv_width],
        shared[0, :HD],
        shared[0, HD:],
        summed_wout,
        three[:, qkv_width + 1],
        summed_wgate,
        summed_wup,
        summed_down,
    )


def solution(mesh):
    in_specs = (
        P("dp", "shard", None),
        P("dp", "shard", None),
        P(),
        P("dp"),
        P(("dp", "shard")),
        P(("dp", "shard"), None),
        P(),
        P(),
        P(None, ("dp", "shard")),
        P(("dp", "shard")),
        P(("dp", "shard"), None),
        P(("dp", "shard"), None),
        P(None, ("dp", "shard")),
    )
    out_specs = (
        P("dp", "shard", None),
        P("dp", "shard", None),
        P(("dp", "shard")),
        P(("dp", "shard"), None),
        P(),
        P(),
        P(None, ("dp", "shard")),
        P(("dp", "shard")),
        P(("dp", "shard"), None),
        P(("dp", "shard"), None),
        P(None, ("dp", "shard")),
    )
    return jax.shard_map(local, mesh=mesh, in_specs=in_specs, out_specs=out_specs, check_vma=False)
```

```python
import functools
import math

import jax
import jax.numpy as jnp
from jax import lax
from jax.experimental import pallas as pl
from jax.experimental.pallas import tpu as pltpu
from jax.sharding import PartitionSpec as P

HEADS = 16
KV = 4
HD = 64
GROUP = HEADS // KV
EPS = 1e-06
LOW = jnp.bfloat16
ANY = pl.BlockSpec(memory_space=pl.ANY)
VMEM = pl.BlockSpec(memory_space=pltpu.VMEM)
SMEM = pl.BlockSpec(memory_space=pltpu.SMEM)
FIRST_FIRST = (((0,), (0,)), ((), ()))
LAST_FIRST = (((1,), (0,)), ((), ()))
LAST_LAST = (((1,), (1,)), ((), ()))


def dot(left, right, dims):
    return lax.dot_general(left, right, dims, preferred_element_type=jnp.float32)


def normalize(values, axis=-1):
    inverse = lax.rsqrt(jnp.mean(values * values, axis=axis, keepdims=True) + EPS)
    return (values * inverse, inverse)


def norm_back(values, inverse, grad_normed, axis=-1):
    cubed = inverse * inverse * inverse
    return inverse * grad_normed - values * cubed * jnp.mean(
        grad_normed * values, axis=axis, keepdims=True
    )


def rotate(values, cos_t, sin_t):
    half_len = HD // 2
    turned = jnp.concatenate([-values[:, :, half_len:], values[:, :, :half_len]], axis=2)
    return values * cos_t + turned * sin_t


def rotate_back(grad_in, cos_t, sin_t):
    half_len = HD // 2
    along = grad_in * sin_t
    return grad_in * cos_t + jnp.concatenate([along[:, :, half_len:], -along[:, :, :half_len]], axis=2)


def tables(positions):
    freq = 10000.0 ** (-(2.0 * jnp.arange(HD // 2, dtype=jnp.float32)) / HD)
    angles = freq[:, None] * positions.astype(jnp.float32)[None, :]
    angles = jnp.concatenate([angles, angles], axis=0)
    return (jnp.cos(angles), jnp.sin(angles))


def swap(values, mask, devices):
    return lax.ppermute(values, ("dp", "shard"), [(i, i ^ mask) for i in range(devices)])


def place(blocks, masks, widths, me, total_rows):
    count = len(blocks)
    size = blocks[0].shape[0] // len(masks[0])
    copies = sum(len(own) for own in masks) * len(widths)

    def kernel(me_ref, *refs):
        sources, outs, sems = refs[:count], refs[count:-1], refs[-1]
        started = []
        for array, own in zip(sources, masks):
            for at, mask in enumerate(own):
                row = pl.multiple_of((me_ref[0] ^ mask) * size, size)
                column = 0
                for out, width in zip(outs, widths):
                    copy = pltpu.make_async_copy(
                        array.at[pl.ds(at * size, size), pl.ds(column, width)],
                        out.at[pl.ds(row, size)],
                        sems.at[len(started)],
                    )
                    copy.start()
                    started.append(copy)
                    column += width
        for copy in started:
            copy.wait()

    return pl.pallas_call(
        kernel,
        out_shape=[jax.ShapeDtypeStruct((total_rows, width), blocks[0].dtype) for width in widths],
        in_specs=[SMEM] + [ANY] * count,
        out_specs=[VMEM] * len(widths),
        scratch_shapes=[pltpu.SemaphoreType.DMA((copies,))],
        compiler_params=pltpu.CompilerParams(vmem_limit_bytes=24 << 20),
    )(me, *blocks)


def pick(arrays, orders, me, size):
    count = len(arrays)
    copies = sum(len(own) for own in orders) * count
    width = sum(array.shape[1] for array in arrays)

    def kernel(me_ref, *refs):
        sources, outs, sems = refs[:count], refs[count:-1], refs[-1]
        started = []
        for out, own in zip(outs, orders):
            for at, mask in enumerate(own):
                row = pl.multiple_of((me_ref[0] ^ mask) * size, size)
                column = 0
                for array in sources:
                    copy = pltpu.make_async_copy(
                        array.at[pl.ds(row, size)],
                        out.at[pl.ds(at * size, size), pl.ds(column, array.shape[1])],
                        sems.at[len(started)],
                    )
                    copy.start()
                    started.append(copy)
                    column += array.shape[1]
        for copy in started:
            copy.wait()

    return pl.pallas_call(
        kernel,
        out_shape=[jax.ShapeDtypeStruct((len(own) * size, width), arrays[0].dtype) for own in orders],
        in_specs=[SMEM] + [VMEM] * count,
        out_specs=[ANY] * len(orders),
        scratch_shapes=[pltpu.SemaphoreType.DMA((copies,))],
        compiler_params=pltpu.CompilerParams(vmem_limit_bytes=24 << 20),
    )(me, *arrays)


def after(value, *others):
    others = [one for one in others if one is not None]
    return lax.optimization_barrier((value, *others))[0] if others else value


class Gather:
    def __init__(self, parts, me, devices):
        self.part = jnp.concatenate(parts, axis=1)
        self.widths = [one.shape[1] for one in parts]
        self.me, self.devices, self.staged = me, devices, devices == 32

    def along_z(self, *others):
        if self.staged:
            part = after(self.part, *others)
            one, two, three = (swap(part, mask, self.devices) for mask in (8, 16, 24))
            self.near, self.far = jnp.concatenate([part, one]), jnp.concatenate([two, three])
            return self.near, self.far
        return ()

    def first_half(self, *others):
        if self.staged:
            near, far = after(self.near, *others), after(self.far, *others)
            self.near = jnp.concatenate([near, swap(near, 4, self.devices)])
            self.far = jnp.concatenate([far, swap(far, 2, self.devices)])
            return self.near, self.far
        return ()

    def second_half(self, *others):
        if self.staged:
            near, far = after(self.near, *others), after(self.far, *others)
            self.blocks = [near, far, swap(near, 2, self.devices), swap(far, 4, self.devices)]
            return tuple(self.blocks[2:])
        return ()

    def whole(self, *others):
        if not self.staged:
            whole = lax.all_gather(self.part, ("dp", "shard"), axis=0, tiled=True)
            ends = [sum(self.widths[:i]) for i in range(1, len(self.widths))]
            return jnp.split(whole, ends, axis=1)
        masks = [(0, 8, 4, 12), (16, 24, 18, 26), (2, 10, 6, 14), (20, 28, 22, 30)]
        blocks = self.blocks + [swap(block, 1, self.devices) for block in self.blocks]
        masks += [tuple(m | 1 for m in own) for own in masks]
        return place(blocks, masks, self.widths, self.me, self.part.shape[0] * self.devices)


class Reduce:
    def __init__(self, grads, me, devices):
        self.grads, self.me, self.devices, self.staged = grads, me, devices, devices == 32
        self.size = grads[0].shape[0] // devices

    def send(self, values, mask):
        return swap(values, mask, self.devices).astype(jnp.float32)

    def between_cores(self):
        if not self.staged:
            grad = jnp.concatenate([one.astype(jnp.float32) for one in self.grads], axis=1)
            self.total = lax.psum_scatter(grad, ("dp", "shard"), scatter_dimension=0, tiled=True)
            return ()
        order = [2, 10, 6, 14, 20, 28, 22, 30, 0, 8, 4, 12, 16, 24, 18, 26]
        self.keep, send = pick(self.grads, [order, [m | 1 for m in order]], self.me, self.size)
        self.came = swap(send, 1, self.devices)
        return (send,)

    def both(self, low, high):
        rows = slice(low * self.size, high * self.size)
        return self.keep[rows].astype(jnp.float32) + self.came[rows].astype(jnp.float32)

    def second_half(self):
        if not self.staged:
            return ()
        sent = self.both(0, 4).astype(LOW), self.both(4, 8).astype(LOW)
        self.from_y, self.from_x = self.send(sent[0], 2), self.send(sent[1], 4)
        return sent

    def first_half(self):
        if not self.staged:
            return ()
        near, far, size = self.both(8, 12) + self.from_y, self.both(12, 16) + self.from_x, self.size
        sent = near[2 * size :].astype(LOW), far[2 * size :].astype(LOW)
        self.near, self.far = near[: 2 * size], far[: 2 * size]
        self.from_x, self.from_y = self.send(sent[0], 4), self.send(sent[1], 2)
        return sent

    def along_z(self):
        if not self.staged:
            return ()
        near, far, size = self.near + self.from_x, self.far + self.from_y, self.size
        sent = near[size:].astype(LOW), far[:size].astype(LOW), far[size:].astype(LOW)
        self.own = near[:size]
        self.others = [self.send(one, mask) for one, mask in zip(sent, (8, 16, 24))]
        return sent

    def result(self):
        if not self.staged:
            return self.total
        return (self.own + self.others[0]) + (self.others[1] + self.others[2])


def gather_pieces(part, devices, shards):
    at = lax.axis_index("shard")
    if shards != 4 or devices != 32:
        return lax.all_gather(part, "shard", axis=0), jnp.arange(shards, dtype=jnp.int32)
    over = swap(part, 2, devices)
    pieces = jnp.stack([part, swap(part, 1, devices), over, swap(over, 1, devices)])
    return pieces, jnp.arange(4, dtype=jnp.int32) ^ at


def reduce_pieces(grad, devices, shards):
    if shards != 4 or devices != 32:
        return lax.psum_scatter(grad, "shard", scatter_dimension=0)
    came = swap(jnp.stack([grad[1], grad[3]]).astype(LOW), 1, devices).astype(jnp.float32)
    over = swap((grad[2] + came[1]).astype(LOW), 2, devices)
    return grad[0] + came[0] + over.astype(jnp.float32)


def sum_over_devices(values, devices):
    if devices != 32:
        return lax.psum(values, ("dp", "shard"))
    for mask in (16, 8, 4, 2, 1):
        values = values + swap(values, mask, devices)
    return values


def allowed(base, start, valid, key_axis, shape):
    key = base + lax.broadcasted_iota(jnp.int32, shape, key_axis)
    query = start + lax.broadcasted_iota(jnp.int32, shape, 1 - key_axis)
    return (key <= query) & (key < valid)


def over_pieces(info_ref, pieces, length, row, tile, before=None, after=None):
    start, valid = info_ref[0], info_ref[1 + pieces + row]

    def one(piece, carry):
        base = info_ref[1 + piece]
        if before is not None:
            before()
        used = (base < start + length) & (base < valid)
        full = (base + length <= start) & (base + length <= valid)
        pl.when(used & full)(lambda: tile(piece, None))
        pl.when(used & jnp.logical_not(full))(lambda: tile(piece, (base, start, valid)))
        if after is not None:
            after(piece)
        return carry

    lax.fori_loop(0, pieces, one, 0)


def attention(info, queries, keys_values):
    rows, _, length = queries.shape
    pieces = keys_values.shape[0]
    group_width = GROUP * HD

    def kernel(info_ref, q_ref, k_ref, v_ref, out_ref, low_ref, sums_ref, accum_ref, part_ref):
        accum_ref[...] = jnp.zeros_like(accum_ref)
        part_ref[...] = jnp.zeros_like(part_ref)

        def tile(piece, bounds):
            key_t, value_t = k_ref[piece, 0], v_ref[piece, 0]
            if bounds is not None:
                mask = allowed(*bounds, 1, (length, length))
            for head in range(GROUP):
                exps = jnp.exp(dot(q_ref[0, head * HD : (head + 1) * HD, :], key_t, FIRST_FIRST))
                if bounds is not None:
                    exps = jnp.where(mask, exps, 0.0)
                width = min(128, length)
                part = exps[:, :width]
                for at in range(width, length, width):
                    part = part + exps[:, at : at + width]
                part_ref[head] += part
                accum_ref[head] += dot(exps.astype(LOW), value_t, LAST_LAST)

        over_pieces(info_ref, pieces, length, pl.program_id(0), tile)
        for head in range(GROUP):
            own = slice(head * HD, (head + 1) * HD)
            sums = jnp.sum(part_ref[head].T, axis=0, keepdims=True)
            sums_ref[0, 0, head : head + 1, :] = sums
            out = accum_ref[head].T / sums
            out_ref[0, own, :] = out
            low_ref[0, own, :] = out.astype(LOW)

    q_spec = pl.BlockSpec((1, group_width, length), lambda row, group, *_: (row, group, 0))
    k_spec = pl.BlockSpec((pieces, 1, HD, length), lambda row, group, *_: (0, row, group, 0))
    v_spec = pl.BlockSpec((pieces, 1, HD, length), lambda row, group, *_: (0, row, group + KV, 0))
    s_spec = pl.BlockSpec((1, 1, GROUP, length), lambda row, group, *_: (row, group, 0, 0))
    work = rows * HEADS * length * length * pieces
    return pl.pallas_call(
        kernel,
        out_shape=[
            jax.ShapeDtypeStruct(queries.shape, jnp.float32),
            jax.ShapeDtypeStruct(queries.shape, LOW),
            jax.ShapeDtypeStruct((rows, KV, GROUP, length), jnp.float32),
        ],
        grid_spec=pltpu.PrefetchScalarGridSpec(
            num_scalar_prefetch=1,
            grid=(rows, KV),
            in_specs=[q_spec, k_spec, v_spec],
            out_specs=[q_spec, q_spec, s_spec],
            scratch_shapes=[
                pltpu.VMEM((GROUP, length, HD), jnp.float32),
                pltpu.VMEM((GROUP, length, min(128, length)), jnp.float32),
            ],
        ),
        compiler_params=pltpu.CompilerParams(vmem_limit_bytes=40 << 20),
        cost_estimate=pl.CostEstimate(flops=work * 1000, transcendentals=work, bytes_accessed=10 << 20),
    )(info, queries, keys_values, keys_values)


def attention_back(info, queries, keys_values, out, sums, grad_out, first, groups):
    rows, _, length = queries.shape
    pieces = keys_values.shape[0]
    group_width = GROUP * HD

    def kernel(
        info_ref, q_ref, k_ref, v_ref, out_ref, sums_ref, grad_ref, dq_ref, dk_ref, dv_ref,
        grad_low, grad_sums, q_rows, grad_rows, k_accum, v_accum,
    ):
        dq_ref[...] = jnp.zeros_like(dq_ref)
        for head in range(GROUP):
            own = slice(head * HD, (head + 1) * HD)
            inverse = 1.0 / sums_ref[0, 0, head : head + 1, :]
            grad = grad_ref[0, own, :]
            grad_sums[head] = -jnp.sum(grad * out_ref[0, own, :], axis=0, keepdims=True) * inverse
            scaled = grad * inverse
            grad_low[own, :] = scaled.astype(LOW)
            grad_rows[head] = scaled.T.astype(LOW)
            q_rows[head] = q_ref[0, own, :].T

        def tile(piece, bounds):
            key_t, value_t = k_ref[piece, 0], v_ref[piece, 0]
            if bounds is not None:
                mask = allowed(*bounds, 0, (length, length))
            for head in range(GROUP):
                own = slice(head * HD, (head + 1) * HD)
                exps = jnp.exp(dot(key_t, q_ref[0, own, :], FIRST_FIRST))
                if bounds is not None:
                    exps = jnp.where(mask, exps, 0.0)
                grad_exps = dot(value_t, grad_low[own, :], FIRST_FIRST) + grad_sums[head]
                grad_scores = (exps * grad_exps).astype(LOW)
                v_accum[...] += dot(exps.astype(LOW), grad_rows[head], LAST_FIRST)
                k_accum[...] += dot(grad_scores, q_rows[head], LAST_FIRST)
                dq_ref[0, own, :] += dot(key_t, grad_scores, LAST_FIRST)

        def before():
            k_accum[...] = jnp.zeros_like(k_accum)
            v_accum[...] = jnp.zeros_like(v_accum)

        def after(piece):
            dk_ref[piece, 0] = k_accum[...].T
            dv_ref[piece, 0] = v_accum[...].T

        over_pieces(info_ref, pieces, length, pl.program_id(0), tile, before, after)

    q_spec = pl.BlockSpec((1, group_width, length), lambda row, group, *_: (row, group + first, 0))
    k_spec = pl.BlockSpec((pieces, 1, HD, length), lambda row, group, *_: (0, row, group + first, 0))
    v_spec = pl.BlockSpec(
        (pieces, 1, HD, length), lambda row, group, *_: (0, row, group + first + KV, 0)
    )
    s_spec = pl.BlockSpec((1, 1, GROUP, length), lambda row, group, *_: (row, group + first, 0, 0))
    dq_spec = pl.BlockSpec((1, group_width, length), lambda row, group, *_: (row, group, 0))
    dk_spec = pl.BlockSpec((pieces, 1, HD, length), lambda row, group, *_: (0, row, group, 0))
    work = rows * groups * GROUP * length * length * pieces
    pieces_shape = jax.ShapeDtypeStruct((pieces, rows, groups * HD, length), jnp.float32)
    return pl.pallas_call(
        kernel,
        out_shape=[
            jax.ShapeDtypeStruct((rows, groups * group_width, length), jnp.float32),
            pieces_shape,
            pieces_shape,
        ],
        grid_spec=pltpu.PrefetchScalarGridSpec(
            num_scalar_prefetch=1,
            grid=(rows, groups),
            in_specs=[q_spec, k_spec, v_spec, q_spec, s_spec, q_spec],
            out_specs=[dq_spec, dk_spec, dk_spec],
            scratch_shapes=[
                pltpu.VMEM((group_width, length), LOW),
                pltpu.VMEM((GROUP, 1, length), jnp.float32),
                pltpu.VMEM((GROUP, length, HD), LOW),
                pltpu.VMEM((GROUP, length, HD), LOW),
                pltpu.VMEM((length, HD), jnp.float32),
                pltpu.VMEM((length, HD), jnp.float32),
            ],
        ),
        compiler_params=pltpu.CompilerParams(vmem_limit_bytes=40 << 20),
        cost_estimate=pl.CostEstimate(flops=work * 2500, transcendentals=work, bytes_accessed=10 << 20),
    )(info, queries, keys_values, keys_values, out, sums, grad_out)


def local(
    tokens,
    cotangent,
    lengths,
    slot_sequence,
    attn_gain,
    w_qkv,
    q_gain,
    k_gain,
    w_out,
    ffn_gain,
    w_gate,
    w_up,
    w_down,
):
    row_count, piece_len, model_width = tokens.shape
    q_width = HEADS * HD
    kv_width = KV * HD
    total_rows = lengths.shape[0]
    scale_factor = 1.0 / math.sqrt(HD)
    shards = lax.axis_size("shard")
    devices = lax.axis_size("dp") * shards
    part_len = attn_gain.shape[0]
    shard_at = lax.axis_index("shard")
    me = (lax.axis_index("dp") * shards + shard_at).astype(jnp.int32).reshape(1)
    row_valid = jnp.sum(
        jnp.where(
            slot_sequence[:, None] == jnp.arange(total_rows, dtype=jnp.int32)[None, :],
            lengths[None, :],
            0,
        ),
        axis=1,
    )
    start = (shard_at * piece_len).astype(jnp.int32)
    positions = start + jnp.arange(piece_len, dtype=jnp.int32)
    live_mask = (positions[None, :] < row_valid[:, None]).astype(jnp.float32)
    cos_t, sin_t = tables(positions)
    cos_h = cos_t[None, None]
    sin_h = sin_t[None, None]
    q_gain_h = q_gain[None, None, :, None]
    k_gain_h = k_gain[None, None, :, None]

    gain_columns = jnp.concatenate(
        [attn_gain[:, None], ffn_gain[:, None], jnp.zeros((part_len, 126), jnp.float32)], axis=1
    )
    w_kv = Gather([w_qkv[:, q_width:].astype(LOW), gain_columns.astype(LOW)], me, devices)
    w_q = Gather([w_qkv[:, :q_width].astype(LOW)], me, devices)
    w_og = Gather([w_out.astype(LOW).T, w_gate.astype(LOW)], me, devices)
    w_ud = Gather([w_up.astype(LOW), w_down.astype(LOW).T], me, devices)
    z_kv = w_kv.along_z()
    one_kv = w_kv.first_half()
    z_q = w_q.along_z(*z_kv)
    two_kv = w_kv.second_half()
    one_q = w_q.first_half(*two_kv)
    z_og = w_og.along_z(*z_q)
    wkv, gains = w_kv.whole()
    two_q = w_q.second_half()
    one_og = w_og.first_half(*two_q)
    z_ud = w_ud.along_z(*z_og)
    (wq,) = w_q.whole()
    gain_attn = gains[:, 0].astype(jnp.float32)
    gain_ffn = gains[:, 1].astype(jnp.float32)

    x_float = tokens.astype(jnp.float32)
    normed_one, inverse_one = normalize(x_float)
    normed_low = (normed_one * gain_attn).astype(LOW)
    kv_raw = jnp.einsum("rtd,de->ret", normed_low, wkv, preferred_element_type=jnp.float32)
    k_raw = kv_raw[:, :kv_width].reshape(row_count, KV, HD, piece_len)
    v_raw = kv_raw[:, kv_width:]
    q_raw = jnp.einsum("rtd,de->ret", normed_low, wq, preferred_element_type=jnp.float32).reshape(
        row_count, HEADS, HD, piece_len
    )
    q_unit, q_inverse = normalize(q_raw, 2)
    k_unit, k_inverse = normalize(k_raw, 2)
    q_low = (
        rotate(q_unit * q_gain_h, cos_h, sin_h).astype(LOW) * jnp.array(scale_factor, LOW)
    ).reshape(row_count, q_width, piece_len)
    k_low = rotate(k_unit * k_gain_h, cos_h, sin_h).astype(LOW).reshape(row_count, kv_width, piece_len)
    own_kv = jnp.concatenate([k_low, v_raw.astype(LOW)], axis=1)
    pieces, piece_at = gather_pieces(own_kv, devices, shards)
    info = jnp.concatenate([start.reshape(1), piece_at * piece_len, row_valid]).astype(jnp.int32)
    two_og = w_og.second_half()
    q_low = after(q_low, *one_og)
    o_heads, att_low, sums = attention(info, q_low, pieces)
    wout, wgate = w_og.whole()
    one_ud = w_ud.first_half(att_low, *two_og)
    two_ud = w_ud.second_half()
    wup, wdown = w_ud.whole()
    x_mid = x_float + jnp.einsum("rct,dc->rtd", att_low, wout, preferred_element_type=jnp.float32)
    normed_two, inverse_two = normalize(x_mid)
    ffn_in = (normed_two * gain_ffn).astype(LOW)
    gate_proj = jnp.einsum("rtd,df->rtf", ffn_in, wgate, preferred_element_type=jnp.float32)
    up_proj = jnp.einsum("rtd,df->rtf", ffn_in, wup, preferred_element_type=jnp.float32)
    gate_sig = jax.nn.sigmoid(gate_proj)
    silu_gate = gate_proj * gate_sig
    activated = (silu_gate * up_proj).astype(LOW)
    output = (
        x_mid + jnp.einsum("rtf,df->rtd", activated, wdown, preferred_element_type=jnp.float32)
    ).astype(LOW)

    grad_out = cotangent.astype(jnp.float32) * live_mask[..., None]
    grad_low = grad_out.astype(LOW)
    grad_down = jnp.einsum("rtd,rtf->df", grad_low, activated, preferred_element_type=jnp.float32)
    grad_act = jnp.einsum("rtd,df->rtf", grad_low, wdown, preferred_element_type=jnp.float32)
    grad_gate = (grad_act * up_proj * gate_sig * (1.0 + gate_proj * (1.0 - gate_sig))).astype(LOW)
    grad_up = (grad_act * silu_gate).astype(LOW)
    grad_wgate = jnp.einsum("rtd,rtf->df", ffn_in, grad_gate, preferred_element_type=jnp.float32)
    grad_wup = jnp.einsum("rtd,rtf->df", ffn_in, grad_up, preferred_element_type=jnp.float32)
    red_one = Reduce([grad_down.astype(LOW), grad_wgate.astype(LOW)], me, devices)
    sent = red_one.between_cores()
    grad_gate, grad_up = after(grad_gate, *sent), after(grad_up, *sent)
    grad_ffn_in = jnp.einsum(
        "rtf,df->rtd", grad_gate, wgate, preferred_element_type=jnp.float32
    ) + jnp.einsum("rtf,df->rtd", grad_up, wup, preferred_element_type=jnp.float32)
    grad_gain_two = jnp.sum(grad_ffn_in * normed_two, axis=(0, 1))
    grad_mid = grad_out + norm_back(x_mid, inverse_two, grad_ffn_in * gain_ffn)
    mid_low = grad_mid.astype(LOW)
    grad_wout = jnp.einsum("rtd,rct->dc", mid_low, att_low, preferred_element_type=jnp.float32)
    red_two = Reduce([grad_wup.astype(LOW), grad_wout.astype(LOW)], me, devices)
    sent_two = red_two.between_cores()
    sent_one = red_one.second_half()
    mid_after = after(mid_low, *sent_two, *sent_one)
    grad_att = jnp.einsum("rtd,dc->rct", mid_after, wout, preferred_element_type=jnp.float32)
    dq_parts, dk_parts, dv_parts = [], [], []
    for group in range(KV):
        if group == 1:
            grad_att = after(grad_att, dq_parts[-1], *red_two.second_half())
        if group == 2:
            grad_att = after(grad_att, dq_parts[-1], *red_one.first_half())
        if group == 3:
            grad_att = after(grad_att, dq_parts[-1])
        dq, dk, dv = attention_back(info, q_low, pieces, o_heads, sums, grad_att, group, 1)
        dq_parts.append(dq)
        dk_parts.append(dk)
        dv_parts.append(dv)
    sent = red_two.first_half() + red_one.along_z()
    dq_parts[-1] = after(dq_parts[-1], *sent)
    grad_query = jnp.concatenate(dq_parts, axis=1)
    grad_pieces = jnp.concatenate(dk_parts + dv_parts, axis=2)
    grad_kv = reduce_pieces(grad_pieces, devices, shards)
    grad_q_scaled = rotate_back(
        scale_factor * grad_query.reshape(row_count, HEADS, HD, piece_len), cos_h, sin_h
    )
    grad_qgain = jnp.sum(grad_q_scaled * q_unit, axis=(0, 1, 3))
    grad_q_raw = norm_back(q_raw, q_inverse, grad_q_scaled * q_gain_h, 2)
    grad_k_scaled = rotate_back(
        grad_kv[:, :kv_width].reshape(row_count, KV, HD, piece_len), cos_h, sin_h
    )
    grad_kgain = jnp.sum(grad_k_scaled * k_unit, axis=(0, 1, 3))
    grad_k_raw = norm_back(k_raw, k_inverse, grad_k_scaled * k_gain_h, 2)
    shared = sum_over_devices(jnp.concatenate([grad_qgain, grad_kgain])[None], devices)
    grad_q_low = grad_q_raw.reshape(row_count, q_width, piece_len).astype(LOW)
    grad_kv_low = jnp.concatenate(
        [grad_k_raw.reshape(row_count, kv_width, piece_len), grad_kv[:, kv_width:]], axis=1
    ).astype(LOW)
    grad_wq = jnp.einsum("rtd,ret->de", normed_low, grad_q_low, preferred_element_type=jnp.float32)
    red_q = Reduce([grad_wq.astype(LOW)], me, devices)
    sent = red_q.between_cores() + red_two.along_z()
    grad_kv_low = after(grad_kv_low, *sent)
    grad_wkv = jnp.einsum("rtd,ret->de", normed_low, grad_kv_low, preferred_element_type=jnp.float32)
    grad_normed = jnp.einsum(
        "ret,de->rtd", grad_q_low, wq, preferred_element_type=jnp.float32
    ) + jnp.einsum("ret,de->rtd", grad_kv_low, wkv, preferred_element_type=jnp.float32)
    grad_gain_one = jnp.sum(grad_normed * normed_one, axis=(0, 1))
    grad_gains = jnp.concatenate(
        [grad_gain_one[:, None], grad_gain_two[:, None], jnp.zeros((model_width, 126), jnp.float32)],
        axis=1,
    )
    red_q.second_half()
    red_kv = Reduce([grad_wkv.astype(LOW), grad_gains.astype(LOW)], me, devices)
    sent = red_kv.between_cores()
    input_grad = grad_mid + norm_back(
        x_float, inverse_one, after(grad_normed, *sent) * gain_attn
    )
    red_q.first_half()
    red_kv.second_half()
    red_q.along_z()
    red_kv.first_half()
    red_kv.along_z()
    one, two, three, four = red_one.result(), red_two.result(), red_q.result(), red_kv.result()
    width = grad_down.shape[1]
    summed_down, summed_wgate = one[:, :width].T, one[:, width:]
    summed_wup, summed_wout = two[:, :width], two[:, width:].T
    tail_width = 2 * kv_width
    return (
        output,
        input_grad,
        four[:, tail_width],
        jnp.concatenate([three, four[:, :tail_width]], axis=1),
        shared[0, :HD],
        shared[0, HD:],
        summed_wout,
        four[:, tail_width + 1],
        summed_wgate,
        summed_wup,
        summed_down,
    )


def solution(mesh):
    in_specs = (
        P("dp", "shard", None),
        P("dp", "shard", None),
        P(),
        P("dp"),
        P(("dp", "shard")),
        P(("dp", "shard"), None),
        P(),
        P(),
        P(None, ("dp", "shard")),
        P(("dp", "shard")),
        P(("dp", "shard"), None),
        P(("dp", "shard"), None),
        P(None, ("dp", "shard")),
    )
    out_specs = (
        P("dp", "shard", None),
        P("dp", "shard", None),
        P(("dp", "shard")),
        P(("dp", "shard"), None),
        P(),
        P(),
        P(None, ("dp", "shard")),
        P(("dp", "shard")),
        P(("dp", "shard"), None),
        P(("dp", "shard"), None),
        P(None, ("dp", "shard")),
    )
    return jax.shard_map(local, mesh=mesh, in_specs=in_specs, out_specs=out_specs, check_vma=False)
```

```python
import functools
import math

import jax
import jax.numpy as jnp
from jax import lax
from jax.experimental import pallas as pl
from jax.experimental.pallas import tpu as pltpu
from jax.sharding import PartitionSpec as P

HEADS = 16
KV = 4
HD = 64
GROUP = HEADS // KV
EPS = 1e-06
LOW = jnp.bfloat16
ANY = pl.BlockSpec(memory_space=pl.ANY)
VMEM = pl.BlockSpec(memory_space=pltpu.VMEM)
SMEM = pl.BlockSpec(memory_space=pltpu.SMEM)
FIRST_FIRST = (((0,), (0,)), ((), ()))
LAST_FIRST = (((1,), (0,)), ((), ()))
LAST_LAST = (((1,), (1,)), ((), ()))


def dot(left, right, dims):
    return lax.dot_general(left, right, dims, preferred_element_type=jnp.float32)


def normalize(values, axis=-1):
    inverse = lax.rsqrt(jnp.mean(values * values, axis=axis, keepdims=True) + EPS)
    return (values * inverse, inverse)


def norm_back(values, inverse, grad_normed, axis=-1):
    cubed = inverse * inverse * inverse
    return inverse * grad_normed - values * cubed * jnp.mean(
        grad_normed * values, axis=axis, keepdims=True
    )


def rotate(values, cos_t, sin_t):
    half_len = HD // 2
    turned = jnp.concatenate([-values[:, :, half_len:], values[:, :, :half_len]], axis=2)
    return values * cos_t + turned * sin_t


def rotate_back(grad_in, cos_t, sin_t):
    half_len = HD // 2
    along = grad_in * sin_t
    return grad_in * cos_t + jnp.concatenate([along[:, :, half_len:], -along[:, :, :half_len]], axis=2)


def tables(positions):
    freq = 10000.0 ** (-(2.0 * jnp.arange(HD // 2, dtype=jnp.float32)) / HD)
    angles = freq[:, None] * positions.astype(jnp.float32)[None, :]
    angles = jnp.concatenate([angles, angles], axis=0)
    return (jnp.cos(angles), jnp.sin(angles))


def swap(values, mask, devices):
    return lax.ppermute(values, ("dp", "shard"), [(i, i ^ mask) for i in range(devices)])


def place(blocks, masks, widths, me, total_rows):
    count = len(blocks)
    size = blocks[0].shape[0] // len(masks[0])
    copies = sum(len(own) for own in masks) * len(widths)

    def kernel(me_ref, *refs):
        sources, outs, sems = refs[:count], refs[count:-1], refs[-1]
        started = []
        for array, own in zip(sources, masks):
            for at, mask in enumerate(own):
                row = pl.multiple_of((me_ref[0] ^ mask) * size, size)
                column = 0
                for out, width in zip(outs, widths):
                    copy = pltpu.make_async_copy(
                        array.at[pl.ds(at * size, size), pl.ds(column, width)],
                        out.at[pl.ds(row, size)],
                        sems.at[len(started)],
                    )
                    copy.start()
                    started.append(copy)
                    column += width
        for copy in started:
            copy.wait()

    return pl.pallas_call(
        kernel,
        out_shape=[jax.ShapeDtypeStruct((total_rows, width), blocks[0].dtype) for width in widths],
        in_specs=[SMEM] + [ANY] * count,
        out_specs=[VMEM] * len(widths),
        scratch_shapes=[pltpu.SemaphoreType.DMA((copies,))],
        compiler_params=pltpu.CompilerParams(vmem_limit_bytes=24 << 20),
    )(me, *blocks)


def pick(arrays, orders, me, size):
    count = len(arrays)
    copies = sum(len(own) for own in orders) * count
    width = sum(array.shape[1] for array in arrays)

    def kernel(me_ref, *refs):
        sources, outs, sems = refs[:count], refs[count:-1], refs[-1]
        started = []
        for out, own in zip(outs, orders):
            for at, mask in enumerate(own):
                row = pl.multiple_of((me_ref[0] ^ mask) * size, size)
                column = 0
                for array in sources:
                    copy = pltpu.make_async_copy(
                        array.at[pl.ds(row, size)],
                        out.at[pl.ds(at * size, size), pl.ds(column, array.shape[1])],
                        sems.at[len(started)],
                    )
                    copy.start()
                    started.append(copy)
                    column += array.shape[1]
        for copy in started:
            copy.wait()

    return pl.pallas_call(
        kernel,
        out_shape=[jax.ShapeDtypeStruct((len(own) * size, width), arrays[0].dtype) for own in orders],
        in_specs=[SMEM] + [VMEM] * count,
        out_specs=[ANY] * len(orders),
        scratch_shapes=[pltpu.SemaphoreType.DMA((copies,))],
        compiler_params=pltpu.CompilerParams(vmem_limit_bytes=24 << 20),
    )(me, *arrays)


class Gather:
    def __init__(self, parts, me, devices):
        self.part = jnp.concatenate(parts, axis=1)
        self.widths = [one.shape[1] for one in parts]
        self.me, self.devices, self.staged = me, devices, devices == 32
        self.stage, self.outgoing, self.incoming = 0, (), ()

    def prepare(self):
        stage = self.stage
        self.stage += 1
        if not self.staged:
            return
        if stage == 0:
            self.outgoing, self.masks = (self.part,), ((8, 16, 24),)
        elif stage == 1:
            one, two, three = self.incoming
            self.outgoing = jnp.concatenate([self.part, one]), jnp.concatenate([two, three])
            self.masks = (4,), (2,)
        elif stage == 2:
            self.outgoing = tuple(
                jnp.concatenate([own, came]) for own, came in zip(self.outgoing, self.incoming)
            )
            self.masks = (2,), (4,)
        else:
            self.outgoing, self.masks = (jnp.concatenate([*self.outgoing, *self.incoming]),), ((1,),)

    def launch(self):
        if self.staged:
            self.incoming = tuple(
                swap(one, mask, self.devices) for one, own in zip(self.outgoing, self.masks) for mask in own
            )

    def whole(self):
        if not self.staged:
            whole = lax.all_gather(self.part, ("dp", "shard"), axis=0, tiled=True)
            ends = [sum(self.widths[:i]) for i in range(1, len(self.widths))]
            return jnp.split(whole, ends, axis=1)
        near, far = (0, 8, 4, 12), (16, 24, 18, 26)
        masks = [*near, *far, *(m | 2 for m in near), *(m | 4 for m in far)]
        masks = masks, [m | 1 for m in masks]
        blocks = self.outgoing + self.incoming
        return place(blocks, masks, self.widths, self.me, self.part.shape[0] * self.devices)


class Reduce:
    def __init__(self, grads, me, devices):
        self.grads, self.me, self.devices, self.staged = grads, me, devices, devices == 32
        self.size = grads[0].shape[0] // devices
        self.stage, self.outgoing, self.incoming = 0, (), ()

    def both(self, low, high):
        rows = slice(low * self.size, high * self.size)
        return self.keep[rows].astype(jnp.float32) + self.came[rows].astype(jnp.float32)

    def prepare(self):
        stage, size = self.stage, self.size
        self.stage += 1
        if not self.staged:
            if stage == 0:
                grad = jnp.concatenate([one.astype(jnp.float32) for one in self.grads], axis=1)
                self.total = lax.psum_scatter(grad, ("dp", "shard"), scatter_dimension=0, tiled=True)
            return
        incoming = [one.astype(jnp.float32) for one in self.incoming]
        if stage == 0:
            order = [2, 10, 6, 14, 20, 28, 22, 30, 0, 8, 4, 12, 16, 24, 18, 26]
            self.keep, send = pick(self.grads, [order, [m | 1 for m in order]], self.me, size)
            self.outgoing, self.masks = (send,), (1,)
        elif stage == 1:
            (self.came,) = self.incoming
            self.outgoing = self.both(0, 4).astype(LOW), self.both(4, 8).astype(LOW)
            self.masks = 2, 4
        elif stage == 2:
            near, far = self.both(8, 12) + incoming[0], self.both(12, 16) + incoming[1]
            self.outgoing = near[2 * size :].astype(LOW), far[2 * size :].astype(LOW)
            self.near, self.far = near[: 2 * size], far[: 2 * size]
            self.masks = 4, 2
        elif stage == 3:
            near, far = self.near + incoming[0], self.far + incoming[1]
            self.outgoing = near[size:].astype(LOW), far[:size].astype(LOW), far[size:].astype(LOW)
            self.own, self.masks = near[:size], (8, 16, 24)
        else:
            self.total = (self.own + incoming[0]) + (incoming[1] + incoming[2])

    def launch(self):
        if self.staged:
            self.incoming = tuple(
                swap(one, mask, self.devices) for one, mask in zip(self.outgoing, self.masks)
            )


class Sum:
    def __init__(self, values, devices):
        self.values, self.devices, self.staged = values, devices, devices == 32
        self.stage, self.outgoing, self.incoming = 0, (), ()

    def prepare(self):
        stage = self.stage
        self.stage += 1
        if not self.staged:
            if stage == 0:
                self.values = lax.psum(self.values, ("dp", "shard"))
            return
        if stage in (1, 2, 3):
            self.values = self.values + self.incoming[0]
        if stage == 4:
            one, two, three = self.incoming
            self.values = (self.values + one) + (two + three)
            return
        self.outgoing, self.masks = (self.values,), ((1,), (2,), (4,), (8, 16, 24))[stage]

    def launch(self):
        if self.staged:
            self.incoming = tuple(swap(self.outgoing[0], mask, self.devices) for mask in self.masks)


def open_slot(travellers, *values):
    for one in travellers:
        one.prepare()
    travellers = [one for one in travellers if one.staged]
    if not travellers:
        return values
    outgoing, values = lax.optimization_barrier((tuple(one.outgoing for one in travellers), values))
    for one, sent in zip(travellers, outgoing):
        one.outgoing = sent
        one.launch()
    return values


def close_slot(travellers, *values):
    travellers = [one for one in travellers if one.staged]
    if not travellers:
        return values
    incoming, values = lax.optimization_barrier((tuple(one.incoming for one in travellers), values))
    for one, came in zip(travellers, incoming):
        one.incoming = came
    return values


class Pieces:
    def __init__(self, part, devices, shards):
        self.part, self.devices, self.shards = part, devices, shards
        self.staged = devices == 32 and shards == 4
        self.stage, self.outgoing, self.incoming = 0, (), ()

    def prepare(self):
        stage = self.stage
        self.stage += 1
        if stage == 0:
            self.outgoing, self.mask = (self.part,), 2
        elif self.staged:
            self.outgoing, self.mask = (jnp.stack([self.part, *self.incoming]),), 1

    def launch(self):
        if self.staged:
            self.incoming = (swap(self.outgoing[0], self.mask, self.devices),)

    def whole(self):
        if not self.staged:
            return lax.all_gather(self.part, "shard", axis=0), jnp.arange(self.shards, dtype=jnp.int32)
        at = jnp.array([0, 2, 1, 3], jnp.int32) ^ lax.axis_index("shard")
        return jnp.concatenate([self.outgoing[0], self.incoming[0]]), at


class PiecesBack:
    def __init__(self, grad, devices, shards):
        self.grad, self.devices, self.staged = grad, devices, devices == 32 and shards == 4
        self.stage, self.outgoing, self.incoming = 0, (), ()

    def prepare(self):
        stage, grad = self.stage, self.grad
        self.stage += 1
        if not self.staged:
            if stage == 0:
                self.total = lax.psum_scatter(grad, "shard", scatter_dimension=0)
        elif stage == 0:
            self.outgoing, self.mask = (grad[2:].astype(LOW),), 1
        elif stage == 1:
            self.came = self.incoming[0].astype(jnp.float32)
            self.outgoing, self.mask = ((grad[1] + self.came[1]).astype(LOW),), 2
        else:
            self.total = grad[0] + self.came[0] + self.incoming[0].astype(jnp.float32)

    def launch(self):
        if self.staged:
            self.incoming = (swap(self.outgoing[0], self.mask, self.devices),)


def allowed(base, start, valid, key_axis, shape):
    key = base + lax.broadcasted_iota(jnp.int32, shape, key_axis)
    query = start + lax.broadcasted_iota(jnp.int32, shape, 1 - key_axis)
    return (key <= query) & (key < valid)


def over_pieces(info_ref, pieces, length, row, tile, before=None, after=None):
    start, valid = info_ref[0], info_ref[1 + pieces + row]

    def one(piece, carry):
        base = info_ref[1 + piece]
        if before is not None:
            before()
        used = (base < start + length) & (base < valid)
        full = (base + length <= start) & (base + length <= valid)
        pl.when(used & full)(lambda: tile(piece, None))
        pl.when(used & jnp.logical_not(full))(lambda: tile(piece, (base, start, valid)))
        if after is not None:
            after(piece)
        return carry

    lax.fori_loop(0, pieces, one, 0)


def attention(info, queries, keys_values, first, groups):
    rows, _, length = queries.shape
    pieces = keys_values.shape[0]
    group_width = GROUP * HD

    def kernel(info_ref, q_ref, k_ref, v_ref, out_ref, low_ref, sums_ref, accum_ref, part_ref):
        accum_ref[...] = jnp.zeros_like(accum_ref)
        part_ref[...] = jnp.zeros_like(part_ref)

        def tile(piece, bounds):
            key_t, value_t = k_ref[piece, 0], v_ref[piece, 0]
            if bounds is not None:
                mask = allowed(*bounds, 1, (length, length))
            for head in range(GROUP):
                exps = jnp.exp(dot(q_ref[0, head * HD : (head + 1) * HD, :], key_t, FIRST_FIRST))
                if bounds is not None:
                    exps = jnp.where(mask, exps, 0.0)
                width = min(128, length)
                part = exps[:, :width]
                for at in range(width, length, width):
                    part = part + exps[:, at : at + width]
                part_ref[head] += part
                accum_ref[head] += dot(exps.astype(LOW), value_t, LAST_LAST)

        over_pieces(info_ref, pieces, length, pl.program_id(0), tile)
        for head in range(GROUP):
            own = slice(head * HD, (head + 1) * HD)
            sums = jnp.sum(part_ref[head].T, axis=0, keepdims=True)
            sums_ref[0, 0, head : head + 1, :] = sums
            out = accum_ref[head].T / sums
            out_ref[0, own, :] = out
            low_ref[0, own, :] = out.astype(LOW)

    q_spec = pl.BlockSpec((1, group_width, length), lambda row, group, *_: (row, group + first, 0))
    o_spec = pl.BlockSpec((1, group_width, length), lambda row, group, *_: (row, group, 0))
    k_spec = pl.BlockSpec((pieces, 1, HD, length), lambda row, group, *_: (0, row, group + first, 0))
    v_spec = pl.BlockSpec(
        (pieces, 1, HD, length), lambda row, group, *_: (0, row, group + first + KV, 0)
    )
    s_spec = pl.BlockSpec((1, 1, GROUP, length), lambda row, group, *_: (row, group, 0, 0))
    work = rows * groups * GROUP * length * length * pieces
    return pl.pallas_call(
        kernel,
        out_shape=[
            jax.ShapeDtypeStruct((rows, groups * group_width, length), jnp.float32),
            jax.ShapeDtypeStruct((rows, groups * group_width, length), LOW),
            jax.ShapeDtypeStruct((rows, groups, GROUP, length), jnp.float32),
        ],
        grid_spec=pltpu.PrefetchScalarGridSpec(
            num_scalar_prefetch=1,
            grid=(rows, groups),
            in_specs=[q_spec, k_spec, v_spec],
            out_specs=[o_spec, o_spec, s_spec],
            scratch_shapes=[
                pltpu.VMEM((GROUP, length, HD), jnp.float32),
                pltpu.VMEM((GROUP, length, min(128, length)), jnp.float32),
            ],
        ),
        compiler_params=pltpu.CompilerParams(vmem_limit_bytes=40 << 20),
        cost_estimate=pl.CostEstimate(flops=work, transcendentals=0, bytes_accessed=1 << 20),
    )(info, queries, keys_values, keys_values)


def attention_back(info, queries, keys_values, out, sums, grad_out, first, groups, part_first):
    rows, _, length = queries.shape
    pieces = keys_values.shape[0]
    group_width = GROUP * HD

    def kernel(
        info_ref, q_ref, k_ref, v_ref, out_ref, sums_ref, grad_ref, dq_ref, dk_ref, dv_ref,
        grad_low, grad_sums, q_rows, grad_rows, k_accum, v_accum,
    ):
        dq_ref[...] = jnp.zeros_like(dq_ref)
        for head in range(GROUP):
            own = slice(head * HD, (head + 1) * HD)
            inverse = 1.0 / sums_ref[0, 0, head : head + 1, :]
            grad = grad_ref[0, own, :]
            grad_sums[head] = -jnp.sum(grad * out_ref[0, own, :], axis=0, keepdims=True) * inverse
            scaled = grad * inverse
            grad_low[own, :] = scaled.astype(LOW)
            grad_rows[head] = scaled.T.astype(LOW)
            q_rows[head] = q_ref[0, own, :].T

        def tile(piece, bounds):
            key_t, value_t = k_ref[piece, 0], v_ref[piece, 0]
            if bounds is not None:
                mask = allowed(*bounds, 0, (length, length))
            for head in range(GROUP):
                own = slice(head * HD, (head + 1) * HD)
                exps = jnp.exp(dot(key_t, q_ref[0, own, :], FIRST_FIRST))
                if bounds is not None:
                    exps = jnp.where(mask, exps, 0.0)
                grad_exps = dot(value_t, grad_low[own, :], FIRST_FIRST) + grad_sums[head]
                grad_scores = (exps * grad_exps).astype(LOW)
                v_accum[...] += dot(exps.astype(LOW), grad_rows[head], LAST_FIRST)
                k_accum[...] += dot(grad_scores, q_rows[head], LAST_FIRST)
                dq_ref[0, own, :] += dot(key_t, grad_scores, LAST_FIRST)

        def before():
            k_accum[...] = jnp.zeros_like(k_accum)
            v_accum[...] = jnp.zeros_like(v_accum)

        def after(piece):
            dk_ref[piece, 0] = k_accum[...].T
            dv_ref[piece, 0] = v_accum[...].T

        over_pieces(info_ref, pieces, length, pl.program_id(0), tile, before, after)

    q_spec = pl.BlockSpec((1, group_width, length), lambda row, group, *_: (row, group + first, 0))
    k_spec = pl.BlockSpec((pieces, 1, HD, length), lambda row, group, *_: (0, row, group + first, 0))
    v_spec = pl.BlockSpec(
        (pieces, 1, HD, length), lambda row, group, *_: (0, row, group + first + KV, 0)
    )
    o_spec = pl.BlockSpec((1, group_width, length), lambda row, group, *_: (row, group + part_first, 0))
    s_spec = pl.BlockSpec(
        (1, 1, GROUP, length), lambda row, group, *_: (row, group + part_first, 0, 0)
    )
    dq_spec = pl.BlockSpec((1, group_width, length), lambda row, group, *_: (row, group, 0))
    dk_spec = pl.BlockSpec((pieces, 1, HD, length), lambda row, group, *_: (0, row, group, 0))
    work = rows * groups * GROUP * length * length * pieces
    pieces_shape = jax.ShapeDtypeStruct((pieces, rows, groups * HD, length), jnp.float32)
    return pl.pallas_call(
        kernel,
        out_shape=[
            jax.ShapeDtypeStruct((rows, groups * group_width, length), jnp.float32),
            pieces_shape,
            pieces_shape,
        ],
        grid_spec=pltpu.PrefetchScalarGridSpec(
            num_scalar_prefetch=1,
            grid=(rows, groups),
            in_specs=[q_spec, k_spec, v_spec, o_spec, s_spec, q_spec],
            out_specs=[dq_spec, dk_spec, dk_spec],
            scratch_shapes=[
                pltpu.VMEM((group_width, length), LOW),
                pltpu.VMEM((GROUP, 1, length), jnp.float32),
                pltpu.VMEM((GROUP, length, HD), LOW),
                pltpu.VMEM((GROUP, length, HD), LOW),
                pltpu.VMEM((length, HD), jnp.float32),
                pltpu.VMEM((length, HD), jnp.float32),
            ],
        ),
        compiler_params=pltpu.CompilerParams(vmem_limit_bytes=40 << 20),
        cost_estimate=pl.CostEstimate(flops=work, transcendentals=0, bytes_accessed=1 << 20),
    )(info, queries, keys_values, keys_values, out, sums, grad_out)


def local(
    tokens,
    cotangent,
    lengths,
    slot_sequence,
    attn_gain,
    w_qkv,
    q_gain,
    k_gain,
    w_out,
    ffn_gain,
    w_gate,
    w_up,
    w_down,
):
    row_count, piece_len, model_width = tokens.shape
    q_width = HEADS * HD
    kv_width = KV * HD
    total_rows = lengths.shape[0]
    scale_factor = 1.0 / math.sqrt(HD)
    shards = lax.axis_size("shard")
    devices = lax.axis_size("dp") * shards
    part_len = attn_gain.shape[0]
    shard_at = lax.axis_index("shard")
    me = (lax.axis_index("dp") * shards + shard_at).astype(jnp.int32).reshape(1)
    row_valid = jnp.sum(
        jnp.where(
            slot_sequence[:, None] == jnp.arange(total_rows, dtype=jnp.int32)[None, :],
            lengths[None, :],
            0,
        ),
        axis=1,
    )
    start = (shard_at * piece_len).astype(jnp.int32)
    positions = start + jnp.arange(piece_len, dtype=jnp.int32)
    live_mask = (positions[None, :] < row_valid[:, None]).astype(jnp.float32)
    cos_t, sin_t = tables(positions)
    cos_h = cos_t[None, None]
    sin_h = sin_t[None, None]
    q_gain_h = q_gain[None, None, :, None]
    k_gain_h = k_gain[None, None, :, None]

    gain_columns = jnp.concatenate(
        [attn_gain[:, None], ffn_gain[:, None], jnp.zeros((part_len, 126), jnp.float32)], axis=1
    ).astype(LOW)
    w_qkv_low, w_gate_low, w_up_low = w_qkv.astype(LOW), w_gate.astype(LOW), w_up.astype(LOW)
    gather_a = Gather([w_qkv_low, gain_columns], me, devices)
    gather_b = Gather([w_out.astype(LOW).T], me, devices)
    w_down_low = w_down.astype(LOW).T
    units = w_down_low.shape[1] // 2
    halves = slice(0, units), slice(units, 2 * units)
    gather_c = [
        Gather([w_gate_low[:, own], w_up_low[:, own], w_down_low[:, own]], me, devices) for own in halves
    ]
    (tokens,) = open_slot([gather_a], tokens)
    x_float = tokens.astype(jnp.float32)
    normed_one, inverse_one = normalize(x_float)
    (normed_one,) = close_slot([gather_a], normed_one)
    (normed_one,) = open_slot([gather_a, gather_b], normed_one)
    (normed_one,) = close_slot([gather_a, gather_b], normed_one)
    (normed_one,) = open_slot([gather_a, gather_b], normed_one)
    (normed_one,) = close_slot([gather_a, gather_b], normed_one)
    (normed_one,) = open_slot([gather_a, gather_b, gather_c[0]], normed_one)
    (normed_one,) = close_slot([gather_a], normed_one)
    wqkv, gains = gather_a.whole()
    gain_attn = gains[:, 0].astype(jnp.float32)
    gain_ffn = gains[:, 1].astype(jnp.float32)
    normed_low = (normed_one * gain_attn).astype(LOW)
    projected = jnp.einsum("rtd,de->ret", normed_low, wqkv, preferred_element_type=jnp.float32)
    q_raw = projected[:, :q_width].reshape(row_count, HEADS, HD, piece_len)
    k_raw = projected[:, q_width : q_width + kv_width].reshape(row_count, KV, HD, piece_len)
    v_raw = projected[:, q_width + kv_width :]
    k_unit, k_inverse = normalize(k_raw, 2)
    k_low = rotate(k_unit * k_gain_h, cos_h, sin_h).astype(LOW).reshape(row_count, kv_width, piece_len)
    own_kv = jnp.concatenate([k_low, v_raw.astype(LOW)], axis=1)
    own_kv, q_raw = close_slot([gather_b, gather_c[0]], own_kv, q_raw)
    row_pieces = Pieces(own_kv, devices, shards)
    (q_raw,) = open_slot([row_pieces, gather_b, gather_c[0]], q_raw)
    q_unit, q_inverse = normalize(q_raw, 2)
    q_low = (
        rotate(q_unit * q_gain_h, cos_h, sin_h).astype(LOW) * jnp.array(scale_factor, LOW)
    ).reshape(row_count, q_width, piece_len)
    (q_low,) = close_slot([row_pieces, gather_b, gather_c[0]], q_low)
    (q_low,) = open_slot([row_pieces, *gather_c], q_low)
    (q_low,) = close_slot([row_pieces], q_low)
    pieces, piece_at = row_pieces.whole()
    info = jnp.concatenate([start.reshape(1), piece_at * piece_len, row_valid]).astype(jnp.int32)
    o_heads, att_low, sums = attention(info, q_low, pieces, 0, KV)
    o_heads, att_low, sums = close_slot(gather_c, o_heads, att_low, sums)
    (att_low,) = open_slot(gather_c, att_low)
    (wout,) = gather_b.whole()
    x_mid = x_float + jnp.einsum("rct,dc->rtd", att_low, wout, preferred_element_type=jnp.float32)
    normed_two, inverse_two = normalize(x_mid)
    ffn_in = (normed_two * gain_ffn).astype(LOW)
    grad_out = cotangent.astype(jnp.float32) * live_mask[..., None]
    grad_low = grad_out.astype(LOW)

    def feed_forward(ffn_in, grad_low, wgate, wup, wdown):
        gate_proj = jnp.einsum("rtd,df->rtf", ffn_in, wgate, preferred_element_type=jnp.float32)
        up_proj = jnp.einsum("rtd,df->rtf", ffn_in, wup, preferred_element_type=jnp.float32)
        gate_sig = jax.nn.sigmoid(gate_proj)
        silu_gate = gate_proj * gate_sig
        activated = (silu_gate * up_proj).astype(LOW)
        grad_down = jnp.einsum("rtd,rtf->df", grad_low, activated, preferred_element_type=jnp.float32)
        grad_act = jnp.einsum("rtd,df->rtf", grad_low, wdown, preferred_element_type=jnp.float32)
        grad_gate = (grad_act * up_proj * gate_sig * (1.0 + gate_proj * (1.0 - gate_sig))).astype(LOW)
        grad_up = (grad_act * silu_gate).astype(LOW)
        grad_wgate = jnp.einsum("rtd,rtf->df", ffn_in, grad_gate, preferred_element_type=jnp.float32)
        grad_wup = jnp.einsum("rtd,rtf->df", ffn_in, grad_up, preferred_element_type=jnp.float32)
        grads = [grad_down.astype(LOW), grad_wgate.astype(LOW), grad_wup.astype(LOW)]
        return activated, grad_gate, grad_up, grads

    ffn_in, x_mid = close_slot(gather_c, ffn_in, x_mid)
    (ffn_in,) = open_slot([gather_c[1]], ffn_in)
    one = gather_c[0].whole()
    act_one, gate_one, up_one, grads = feed_forward(ffn_in, grad_low, *one)
    ffn_in, grads, act_one, gate_one, up_one = close_slot(
        [gather_c[1]], ffn_in, grads, act_one, gate_one, up_one
    )
    red_one = Reduce(grads, me, devices)
    (ffn_in,) = open_slot([gather_c[1], red_one], ffn_in)
    (ffn_in,) = close_slot([gather_c[1], red_one], ffn_in)
    (ffn_in,) = open_slot([red_one], ffn_in)
    two = gather_c[1].whole()
    act_two, gate_two, up_two, grads = feed_forward(ffn_in, grad_low, *two)
    ffn_in, grads, act_two, gate_two, up_two = close_slot(
        [red_one], ffn_in, grads, act_two, gate_two, up_two
    )
    red_two = Reduce(grads, me, devices)
    gate_two, up_two, act_two = open_slot([red_one, red_two], gate_two, up_two, act_two)
    grad_ffn_in = jnp.einsum(
        "rtf,df->rtd",
        jnp.concatenate([gate_one, up_one, gate_two, up_two], axis=2),
        jnp.concatenate([*one[:2], *two[:2]], axis=1),
        preferred_element_type=jnp.float32,
    )
    grad_mid = grad_out + norm_back(x_mid, inverse_two, grad_ffn_in * gain_ffn)
    mid_low = grad_mid.astype(LOW)
    grad_wout = jnp.einsum("rtd,rct->dc", mid_low, att_low, preferred_element_type=jnp.float32)
    grad_att = jnp.einsum("rtd,dc->rct", mid_low, wout, preferred_element_type=jnp.float32)
    red_out = Reduce([grad_wout.astype(LOW)], me, devices)
    grad_att, red_out.grads = close_slot([red_one, red_two], grad_att, red_out.grads)
    grad_att, act_two = open_slot([red_one, red_two], grad_att, act_two)

    def back(group, grad_att):
        return attention_back(info, q_low, pieces, o_heads, sums, grad_att, group, 1, group)

    output = (
        x_mid
        + jnp.einsum(
            "rtf,df->rtd",
            jnp.concatenate([act_one, act_two], axis=2),
            jnp.concatenate([one[2], two[2]], axis=1),
            preferred_element_type=jnp.float32,
        )
    ).astype(LOW)
    parts = [back(0, grad_att)]
    parts[0], grad_att, output = close_slot([red_one, red_two], parts[0], grad_att, output)
    red_one.prepare()
    (grad_att,) = open_slot([red_two, red_out], grad_att)
    parts.append(back(1, grad_att))
    parts[1], grad_att = close_slot([red_two, red_out], parts[1], grad_att)
    (grad_att,) = open_slot([red_two, red_out], grad_att)
    parts.append(back(2, grad_att))
    parts[2], grad_att = close_slot([red_two, red_out], parts[2], grad_att)
    red_two.prepare()
    (grad_att,) = open_slot([red_out], grad_att)
    parts.append(back(3, grad_att))
    (parts,) = close_slot([red_out], parts)
    grad_query = jnp.concatenate([one_part[0] for one_part in parts], axis=1)
    grad_pieces = jnp.concatenate(
        [one_part[1] for one_part in parts] + [one_part[2] for one_part in parts], axis=2
    )
    kv_back = PiecesBack(grad_pieces, devices, shards)
    (grad_query,) = open_slot([kv_back, red_out], grad_query)
    (grad_query,) = close_slot([kv_back], grad_query)
    (grad_query,) = open_slot([kv_back], grad_query)
    grad_q_scaled = rotate_back(
        scale_factor * grad_query.reshape(row_count, HEADS, HD, piece_len), cos_h, sin_h
    )
    grad_qgain = jnp.sum(grad_q_scaled * q_unit, axis=(0, 1, 3))
    grad_q_raw = norm_back(q_raw, q_inverse, grad_q_scaled * q_gain_h, 2)
    grad_q_low = grad_q_raw.reshape(row_count, q_width, piece_len).astype(LOW)
    grad_wq = jnp.einsum("rtd,ret->de", normed_low, grad_q_low, preferred_element_type=jnp.float32)
    grad_wq, grad_q_low = close_slot([kv_back, red_out], grad_wq, grad_q_low)
    red_out.prepare()
    kv_back.prepare()
    red_q = Reduce([grad_wq.astype(LOW)], me, devices)
    grad_kv, grad_q_low = open_slot([red_q], kv_back.total, grad_q_low)
    grad_k_scaled = rotate_back(
        grad_kv[:, :kv_width].reshape(row_count, KV, HD, piece_len), cos_h, sin_h
    )
    grad_kgain = jnp.sum(grad_k_scaled * k_unit, axis=(0, 1, 3))
    grad_k_raw = norm_back(k_raw, k_inverse, grad_k_scaled * k_gain_h, 2)
    grad_kv_low = jnp.concatenate(
        [grad_k_raw.reshape(row_count, kv_width, piece_len), grad_kv[:, kv_width:]], axis=1
    ).astype(LOW)
    grad_wkv = jnp.einsum("rtd,ret->de", normed_low, grad_kv_low, preferred_element_type=jnp.float32)
    grad_wkv, grad_kv_low, grad_q_low = close_slot([red_q], grad_wkv, grad_kv_low, grad_q_low)
    shared = Sum(jnp.concatenate([grad_qgain, grad_kgain])[None], devices)
    red_kv = Reduce([grad_wkv.astype(LOW)], me, devices)
    grad_kv_low, grad_q_low = open_slot([red_q, red_kv, shared], grad_kv_low, grad_q_low)
    grad_normed = jnp.einsum(
        "ret,de->rtd",
        jnp.concatenate([grad_q_low, grad_kv_low], axis=1),
        wqkv,
        preferred_element_type=jnp.float32,
    )
    input_grad = grad_mid + norm_back(x_float, inverse_one, grad_normed * gain_attn)
    (input_grad,) = close_slot([red_q, red_kv, shared], input_grad)
    open_slot([red_q, red_kv, shared])
    close_slot([red_q, red_kv, shared])
    open_slot([red_q, red_kv, shared])
    close_slot([red_q, red_kv, shared])
    open_slot([red_kv, shared])
    red_q.prepare()
    close_slot([red_kv, shared])
    red_kv.prepare()
    shared.prepare()
    shared = shared.values
    three, four = red_q.total, red_kv.total
    summed = [jnp.split(one_red.total, 3, axis=1) for one_red in (red_one, red_two)]
    summed_down, summed_wgate, summed_wup = (
        jnp.concatenate([summed[0][at], summed[1][at]], axis=1) for at in range(3)
    )
    summed_down, summed_wout = summed_down.T, red_out.total.T
    summed_wqkv = jnp.concatenate([three, four], axis=1)
    grad_gain_one = jnp.sum(summed_wqkv * w_qkv_low, axis=1) / attn_gain.astype(LOW)
    grad_gain_two = jnp.sum(summed_wgate * w_gate_low + summed_wup * w_up_low, axis=1) / ffn_gain.astype(LOW)
    return (
        output,
        input_grad,
        grad_gain_one,
        summed_wqkv,
        shared[0, :HD],
        shared[0, HD:],
        summed_wout,
        grad_gain_two,
        summed_wgate,
        summed_wup,
        summed_down,
    )


def solution(mesh):
    in_specs = (
        P("dp", "shard", None),
        P("dp", "shard", None),
        P(),
        P("dp"),
        P(("dp", "shard")),
        P(("dp", "shard"), None),
        P(),
        P(),
        P(None, ("dp", "shard")),
        P(("dp", "shard")),
        P(("dp", "shard"), None),
        P(("dp", "shard"), None),
        P(None, ("dp", "shard")),
    )
    out_specs = (
        P("dp", "shard", None),
        P("dp", "shard", None),
        P(("dp", "shard")),
        P(("dp", "shard"), None),
        P(),
        P(),
        P(None, ("dp", "shard")),
        P(("dp", "shard")),
        P(("dp", "shard"), None),
        P(("dp", "shard"), None),
        P(None, ("dp", "shard")),
    )
    return jax.shard_map(local, mesh=mesh, in_specs=in_specs, out_specs=out_specs, check_vma=False)
```

```python
import functools
import math

import jax
import jax.numpy as jnp
from jax import lax
from jax.experimental import pallas as pl
from jax.experimental.pallas import tpu as pltpu
from jax.sharding import PartitionSpec as P

HEADS = 16
KV = 4
HD = 64
GROUP = HEADS // KV
EPS = 1e-06
LOW = jnp.bfloat16
ANY = pl.BlockSpec(memory_space=pl.ANY)
VMEM = pl.BlockSpec(memory_space=pltpu.VMEM)
SMEM = pl.BlockSpec(memory_space=pltpu.SMEM)
FIRST_FIRST = (((0,), (0,)), ((), ()))
LAST_FIRST = (((1,), (0,)), ((), ()))
LAST_LAST = (((1,), (1,)), ((), ()))


def dot(left, right, dims):
    return lax.dot_general(left, right, dims, preferred_element_type=jnp.float32)


def normalize(values, axis=-1):
    inverse = lax.rsqrt(jnp.mean(values * values, axis=axis, keepdims=True) + EPS)
    return (values * inverse, inverse)


def norm_back(values, inverse, grad_normed, axis=-1):
    cubed = inverse * inverse * inverse
    return inverse * grad_normed - values * cubed * jnp.mean(
        grad_normed * values, axis=axis, keepdims=True
    )


def rotate(values, cos_t, sin_t):
    half_len = HD // 2
    turned = jnp.concatenate([-values[:, :, half_len:], values[:, :, :half_len]], axis=2)
    return values * cos_t + turned * sin_t


def rotate_back(grad_in, cos_t, sin_t):
    half_len = HD // 2
    along = grad_in * sin_t
    return grad_in * cos_t + jnp.concatenate([along[:, :, half_len:], -along[:, :, :half_len]], axis=2)


def tables(positions):
    freq = 10000.0 ** (-(2.0 * jnp.arange(HD // 2, dtype=jnp.float32)) / HD)
    angles = freq[:, None] * positions.astype(jnp.float32)[None, :]
    angles = jnp.concatenate([angles, angles], axis=0)
    return (jnp.cos(angles), jnp.sin(angles))


def swap(values, mask, devices):
    return lax.ppermute(values, ("dp", "shard"), [(i, i ^ mask) for i in range(devices)])


def place(blocks, masks, widths, me, total_rows):
    count = len(blocks)
    size = blocks[0].shape[0] // len(masks[0])
    copies = sum(len(own) for own in masks) * len(widths)

    def kernel(me_ref, *refs):
        sources, outs, sems = refs[:count], refs[count:-1], refs[-1]
        started = []
        for array, own in zip(sources, masks):
            for at, mask in enumerate(own):
                row = pl.multiple_of((me_ref[0] ^ mask) * size, size)
                column = 0
                for out, width in zip(outs, widths):
                    copy = pltpu.make_async_copy(
                        array.at[pl.ds(at * size, size), pl.ds(column, width)],
                        out.at[pl.ds(row, size)],
                        sems.at[len(started)],
                    )
                    copy.start()
                    started.append(copy)
                    column += width
        for copy in started:
            copy.wait()

    return pl.pallas_call(
        kernel,
        out_shape=[jax.ShapeDtypeStruct((total_rows, width), blocks[0].dtype) for width in widths],
        in_specs=[SMEM] + [ANY] * count,
        out_specs=[VMEM] * len(widths),
        scratch_shapes=[pltpu.SemaphoreType.DMA((copies,))],
        compiler_params=pltpu.CompilerParams(vmem_limit_bytes=24 << 20),
        cost_estimate=pl.CostEstimate(flops=0, transcendentals=0, bytes_accessed=1 << 16),
    )(me, *blocks)


def pick(arrays, orders, me, size):
    count = len(arrays)
    copies = sum(len(own) for own in orders) * count
    width = sum(array.shape[1] for array in arrays)

    def kernel(me_ref, *refs):
        sources, outs, sems = refs[:count], refs[count:-1], refs[-1]
        started = []
        for out, own in zip(outs, orders):
            for at, mask in enumerate(own):
                row = pl.multiple_of((me_ref[0] ^ mask) * size, size)
                column = 0
                for array in sources:
                    copy = pltpu.make_async_copy(
                        array.at[pl.ds(row, size)],
                        out.at[pl.ds(at * size, size), pl.ds(column, array.shape[1])],
                        sems.at[len(started)],
                    )
                    copy.start()
                    started.append(copy)
                    column += array.shape[1]
        for copy in started:
            copy.wait()

    return pl.pallas_call(
        kernel,
        out_shape=[jax.ShapeDtypeStruct((len(own) * size, width), arrays[0].dtype) for own in orders],
        in_specs=[SMEM] + [VMEM] * count,
        out_specs=[ANY] * len(orders),
        scratch_shapes=[pltpu.SemaphoreType.DMA((copies,))],
        compiler_params=pltpu.CompilerParams(vmem_limit_bytes=24 << 20),
        cost_estimate=pl.CostEstimate(flops=0, transcendentals=0, bytes_accessed=1 << 16),
    )(me, *arrays)


class Gather:
    def __init__(self, parts, me, devices, first=False):
        self.part = jnp.concatenate(parts, axis=1)
        self.widths = [one.shape[1] for one in parts]
        self.me, self.devices, self.staged, self.first = me, devices, devices == 32, first
        self.stage, self.outgoing, self.incoming = 0, (), ()

    def prepare(self):
        stage = self.stage
        self.stage += 1
        if not self.staged:
            return
        if stage == 0:
            self.outgoing, self.masks = (self.part,), ((8, 16, 24),)
        elif stage == 1:
            one, two, three = self.incoming
            self.outgoing = jnp.concatenate([self.part, one]), jnp.concatenate([two, three])
            self.masks = (4,), (2,)
        elif stage == 2:
            self.outgoing = tuple(
                jnp.concatenate([own, came]) for own, came in zip(self.outgoing, self.incoming)
            )
            self.masks = (2,), (4,)
        elif self.first:
            self.outgoing, self.masks = self.outgoing + self.incoming, ((1,),) * 4
        else:
            self.outgoing, self.masks = (jnp.concatenate([*self.outgoing, *self.incoming]),), ((1,),)

    def launch(self):
        if self.staged:
            self.incoming = tuple(
                swap(one, mask, self.devices) for one, own in zip(self.outgoing, self.masks) for mask in own
            )

    def whole(self):
        if not self.staged:
            whole = lax.all_gather(self.part, ("dp", "shard"), axis=0, tiled=True)
            ends = [sum(self.widths[:i]) for i in range(1, len(self.widths))]
            return jnp.split(whole, ends, axis=1)
        near, far = (0, 8, 4, 12), (16, 24, 18, 26)
        masks = [near, far, [m | 2 for m in near], [m | 4 for m in far]]
        if not self.first:
            masks = [[m for own in masks for m in own]]
        masks += [[m | 1 for m in own] for own in masks]
        blocks = self.outgoing + self.incoming
        return place(blocks, masks, self.widths, self.me, self.part.shape[0] * self.devices)


class Reduce:
    def __init__(self, grads, me, devices):
        self.grads, self.me, self.devices, self.staged = grads, me, devices, devices == 32
        self.size = grads[0].shape[0] // devices
        self.stage, self.outgoing, self.incoming = 0, (), ()

    def both(self, low, high):
        rows = slice(low * self.size, high * self.size)
        return self.keep[rows].astype(jnp.float32) + self.came[rows].astype(jnp.float32)

    def prepare(self):
        stage, size = self.stage, self.size
        self.stage += 1
        if not self.staged:
            if stage == 0:
                grad = jnp.concatenate([one.astype(jnp.float32) for one in self.grads], axis=1)
                self.total = lax.psum_scatter(grad, ("dp", "shard"), scatter_dimension=0, tiled=True)
            return
        incoming = [one.astype(jnp.float32) for one in self.incoming]
        if stage == 0:
            order = [2, 10, 6, 14, 20, 28, 22, 30, 0, 8, 4, 12, 16, 24, 18, 26]
            self.keep, send = pick(self.grads, [order, [m | 1 for m in order]], self.me, size)
            self.outgoing, self.masks = (send,), (1,)
        elif stage == 1:
            (self.came,) = self.incoming
            self.outgoing = self.both(0, 4).astype(LOW), self.both(4, 8).astype(LOW)
            self.masks = 2, 4
        elif stage == 2:
            near, far = self.both(8, 12) + incoming[0], self.both(12, 16) + incoming[1]
            self.outgoing = near[2 * size :].astype(LOW), far[2 * size :].astype(LOW)
            self.near, self.far = near[: 2 * size], far[: 2 * size]
            self.masks = 4, 2
        elif stage == 3:
            near, far = self.near + incoming[0], self.far + incoming[1]
            self.outgoing = near[size:].astype(LOW), far[:size].astype(LOW), far[size:].astype(LOW)
            self.own, self.masks = near[:size], (8, 16, 24)
        else:
            self.total = (self.own + incoming[0]) + (incoming[1] + incoming[2])

    def launch(self):
        if self.staged:
            self.incoming = tuple(
                swap(one, mask, self.devices) for one, mask in zip(self.outgoing, self.masks)
            )


class Sum:
    def __init__(self, values, devices):
        self.values, self.devices, self.staged = values, devices, devices == 32
        self.stage, self.outgoing, self.incoming = 0, (), ()

    def prepare(self):
        stage = self.stage
        self.stage += 1
        if not self.staged:
            if stage == 0:
                self.values = lax.psum(self.values, ("dp", "shard"))
            return
        if stage:
            self.values = self.values + self.incoming[0]
        if stage < 5:
            self.outgoing, self.masks = (self.values,), ((1,), (2,), (4,), (8,), (16,))[stage]

    def launch(self):
        if self.staged:
            self.incoming = tuple(swap(self.outgoing[0], mask, self.devices) for mask in self.masks)


def open_slot(travellers, *values, ready=()):
    for one in travellers:
        if one not in ready:
            one.prepare()
    travellers = [one for one in travellers if one.staged]
    if not travellers:
        return values
    outgoing, values = lax.optimization_barrier((tuple(one.outgoing for one in travellers), values))
    for one, sent in zip(travellers, outgoing):
        one.outgoing = sent
        one.launch()
    return values


def close_slot(travellers, *values):
    travellers = [one for one in travellers if one.staged]
    if not travellers:
        return values
    incoming, values = lax.optimization_barrier((tuple(one.incoming for one in travellers), values))
    for one, came in zip(travellers, incoming):
        one.incoming = came
    return values


class Pieces:
    def __init__(self, part, devices, shards):
        self.part, self.devices, self.shards = part, devices, shards
        self.staged = devices == 32 and shards == 4
        self.stage, self.outgoing, self.incoming = 0, (), ()

    def prepare(self):
        stage = self.stage
        self.stage += 1
        if stage == 0:
            self.outgoing, self.mask = (self.part,), 2
        elif self.staged:
            self.outgoing, self.mask = (jnp.stack([self.part, *self.incoming]),), 1

    def launch(self):
        if self.staged:
            self.incoming = (swap(self.outgoing[0], self.mask, self.devices),)

    def whole(self):
        if not self.staged:
            return lax.all_gather(self.part, "shard", axis=0), jnp.arange(self.shards, dtype=jnp.int32)
        at = jnp.array([0, 2, 1, 3], jnp.int32) ^ lax.axis_index("shard")
        return jnp.concatenate([self.outgoing[0], self.incoming[0]]), at


class PiecesBack:
    def __init__(self, grad, devices, shards):
        self.grad, self.devices, self.staged = grad, devices, devices == 32 and shards == 4
        self.stage, self.outgoing, self.incoming = 0, (), ()

    def prepare(self):
        stage, grad = self.stage, self.grad
        self.stage += 1
        if not self.staged:
            if stage == 0:
                self.shares = lax.psum_scatter(grad, "shard", scatter_dimension=0)[None], ()
        elif stage == 0:
            self.outgoing, self.mask = (grad[2:].astype(LOW),), 1
        elif stage == 1:
            (self.came,) = self.incoming
            self.outgoing, self.mask = ((grad[1:2] + self.came[1:].astype(jnp.float32)).astype(LOW),), 2
        else:
            self.shares = grad, (self.came, *self.incoming)

    def launch(self):
        if self.staged:
            self.incoming = (swap(self.outgoing[0], self.mask, self.devices),)


def allowed(base, start, valid, key_axis, shape):
    key = base + lax.broadcasted_iota(jnp.int32, shape, key_axis)
    query = start + lax.broadcasted_iota(jnp.int32, shape, 1 - key_axis)
    return (key <= query) & (key < valid)


def over_pieces(info_ref, pieces, length, row, tile, before=None, after=None):
    start, valid = info_ref[0], info_ref[1 + pieces + row]

    def one(piece, carry):
        base = info_ref[1 + piece]
        if before is not None:
            before()
        used = (base < start + length) & (base < valid)
        full = (base + length <= start) & (base + length <= valid)
        pl.when(used & full)(lambda: tile(piece, None))
        pl.when(used & jnp.logical_not(full))(lambda: tile(piece, (base, start, valid)))
        if after is not None:
            after(piece)
        return carry

    lax.fori_loop(0, pieces, one, 0)


def attention(info, queries, keys_values, first, groups):
    rows, _, length = queries.shape
    pieces = keys_values.shape[0]
    group_width = GROUP * HD

    def kernel(info_ref, q_ref, k_ref, v_ref, out_ref, low_ref, sums_ref, accum_ref, part_ref):
        accum_ref[...] = jnp.zeros_like(accum_ref)
        part_ref[...] = jnp.zeros_like(part_ref)

        def tile(piece, bounds):
            key_t, value_t = k_ref[piece, 0], v_ref[piece, 0]
            if bounds is not None:
                mask = allowed(*bounds, 1, (length, length))
            for head in range(GROUP):
                exps = jnp.exp(dot(q_ref[0, head * HD : (head + 1) * HD, :], key_t, FIRST_FIRST))
                if bounds is not None:
                    exps = jnp.where(mask, exps, 0.0)
                width = min(128, length)
                part = exps[:, :width]
                for at in range(width, length, width):
                    part = part + exps[:, at : at + width]
                part_ref[head] += part
                accum_ref[head] += dot(exps.astype(LOW), value_t, LAST_LAST)

        over_pieces(info_ref, pieces, length, pl.program_id(0), tile)
        for head in range(GROUP):
            own = slice(head * HD, (head + 1) * HD)
            sums = jnp.sum(part_ref[head].T, axis=0, keepdims=True)
            sums_ref[0, 0, head : head + 1, :] = sums
            out = accum_ref[head].T / sums
            out_ref[0, own, :] = out
            low_ref[0, own, :] = out.astype(LOW)

    q_spec = pl.BlockSpec((1, group_width, length), lambda row, group, *_: (row, group + first, 0))
    o_spec = pl.BlockSpec((1, group_width, length), lambda row, group, *_: (row, group, 0))
    k_spec = pl.BlockSpec((pieces, 1, HD, length), lambda row, group, *_: (0, row, group + first, 0))
    v_spec = pl.BlockSpec(
        (pieces, 1, HD, length), lambda row, group, *_: (0, row, group + first + KV, 0)
    )
    s_spec = pl.BlockSpec((1, 1, GROUP, length), lambda row, group, *_: (row, group, 0, 0))
    work = rows * groups * GROUP * length * length * pieces
    return pl.pallas_call(
        kernel,
        out_shape=[
            jax.ShapeDtypeStruct((rows, groups * group_width, length), jnp.float32),
            jax.ShapeDtypeStruct((rows, groups * group_width, length), LOW),
            jax.ShapeDtypeStruct((rows, groups, GROUP, length), jnp.float32),
        ],
        grid_spec=pltpu.PrefetchScalarGridSpec(
            num_scalar_prefetch=1,
            grid=(rows, groups),
            in_specs=[q_spec, k_spec, v_spec],
            out_specs=[o_spec, o_spec, s_spec],
            scratch_shapes=[
                pltpu.VMEM((GROUP, length, HD), jnp.float32),
                pltpu.VMEM((GROUP, length, min(128, length)), jnp.float32),
            ],
        ),
        compiler_params=pltpu.CompilerParams(vmem_limit_bytes=40 << 20),
        cost_estimate=pl.CostEstimate(flops=work, transcendentals=0, bytes_accessed=1 << 20),
    )(info, queries, keys_values, keys_values)


def head_back(grad, raw, gain, cos_t, sin_t):
    half_len = HD // 2
    along = grad * sin_t
    grad = grad * cos_t + jnp.concatenate([along[half_len:], -along[:half_len]], axis=0)
    inverse = lax.rsqrt(jnp.mean(raw * raw, axis=0, keepdims=True) + EPS)
    products = grad * (raw * inverse)
    grad = grad * gain
    cubed = inverse * inverse * inverse
    return inverse * grad - raw * cubed * jnp.mean(grad * raw, axis=0, keepdims=True), products


def fold(values):
    total = values[:, :128]
    for at in range(128, values.shape[1], 128):
        total = total + values[:, at : at + 128]
    return total


def attention_back(
    info, queries, keys_values, out, sums, grad_out, q_raw, gain, cos_t, sin_t, group, carried
):
    rows, _, length = queries.shape
    pieces = keys_values.shape[0]
    group_width = GROUP * HD
    scale_factor = 1.0 / math.sqrt(HD)

    def kernel(
        info_ref, q_ref, k_ref, v_ref, out_ref, sums_ref, grad_ref, raw_ref, gain_ref, cos_ref, sin_ref, *refs
    ):
        refs = refs[len(carried) :]
        dq_ref, dkv_ref, gain_grad_ref = refs[:3]
        grad_low, grad_sums, q_rows, grad_rows, k_accum, v_accum, q_accum = refs[3:]
        q_accum[...] = jnp.zeros_like(q_accum)
        for head in range(GROUP):
            own = slice(head * HD, (head + 1) * HD)
            inverse = 1.0 / sums_ref[0, 0, head : head + 1, :]
            grad = grad_ref[0, own, :]
            grad_sums[head] = -jnp.sum(grad * out_ref[0, own, :], axis=0, keepdims=True) * inverse
            scaled = grad * inverse
            grad_low[own, :] = scaled.astype(LOW)
            grad_rows[head] = scaled.T.astype(LOW)
            q_rows[head] = q_ref[0, own, :].T

        def tile(piece, bounds):
            key_t, value_t = k_ref[piece, 0], v_ref[piece, 0]
            if bounds is not None:
                mask = allowed(*bounds, 0, (length, length))
            for head in range(GROUP):
                own = slice(head * HD, (head + 1) * HD)
                exps = jnp.exp(dot(key_t, q_ref[0, own, :], FIRST_FIRST))
                if bounds is not None:
                    exps = jnp.where(mask, exps, 0.0)
                grad_exps = dot(value_t, grad_low[own, :], FIRST_FIRST) + grad_sums[head]
                grad_scores = (exps * grad_exps).astype(LOW)
                v_accum[...] += dot(exps.astype(LOW), grad_rows[head], LAST_FIRST)
                k_accum[...] += dot(grad_scores, q_rows[head], LAST_FIRST)
                q_accum[own, :] += dot(key_t, grad_scores, LAST_FIRST)

        def before():
            k_accum[...] = jnp.zeros_like(k_accum)
            v_accum[...] = jnp.zeros_like(v_accum)

        def after(piece):
            dkv_ref[piece, 0, 0] = k_accum[...].T
            dkv_ref[piece, 0, 1] = v_accum[...].T

        over_pieces(info_ref, pieces, length, pl.program_id(0), tile, before, after)
        total = jnp.zeros((HD, 128), jnp.float32)
        for head in range(GROUP):
            own = slice(head * HD, (head + 1) * HD)
            grad, products = head_back(
                scale_factor * q_accum[own, :], raw_ref[0, own, :], gain_ref[...], cos_ref[...], sin_ref[...]
            )
            dq_ref[0, own, :] = grad.astype(LOW)
            total = total + fold(products)
        gain_grad_ref[0] = total

    q_spec = pl.BlockSpec((1, group_width, length), lambda row, *_: (row, group, 0))
    k_spec = pl.BlockSpec((pieces, 1, HD, length), lambda row, *_: (0, row, group, 0))
    v_spec = pl.BlockSpec((pieces, 1, HD, length), lambda row, *_: (0, row, group + KV, 0))
    s_spec = pl.BlockSpec((1, 1, GROUP, length), lambda row, *_: (row, group, 0, 0))
    table_spec = pl.BlockSpec((HD, length), lambda row, *_: (0, 0))
    gain_spec = pl.BlockSpec((HD, 1), lambda row, *_: (0, 0))
    dkv_spec = pl.BlockSpec((pieces, 1, 2, HD, length), lambda row, *_: (0, row, 0, group, 0))
    work = rows * GROUP * length * length * pieces
    inputs = [info, queries, keys_values, keys_values, out, sums, grad_out, q_raw, gain, cos_t, sin_t]
    return pl.pallas_call(
        kernel,
        out_shape=[
            jax.ShapeDtypeStruct(queries.shape, LOW),
            jax.ShapeDtypeStruct((pieces, rows, 2, KV * HD, length), jnp.float32),
            jax.ShapeDtypeStruct((rows, HD, 128), jnp.float32),
        ],
        grid_spec=pltpu.PrefetchScalarGridSpec(
            num_scalar_prefetch=1,
            grid=(rows,),
            in_specs=[
                q_spec, k_spec, v_spec, q_spec, s_spec, q_spec, q_spec, gain_spec, table_spec, table_spec,
                *[ANY] * len(carried),
            ],
            out_specs=[q_spec, dkv_spec, pl.BlockSpec((1, HD, 128), lambda row, *_: (row, 0, 0))],
            scratch_shapes=[
                pltpu.VMEM((group_width, length), LOW),
                pltpu.VMEM((GROUP, 1, length), jnp.float32),
                pltpu.VMEM((GROUP, length, HD), LOW),
                pltpu.VMEM((GROUP, length, HD), LOW),
                pltpu.VMEM((length, HD), jnp.float32),
                pltpu.VMEM((length, HD), jnp.float32),
                pltpu.VMEM((group_width, length), jnp.float32),
            ],
        ),
        input_output_aliases={len(inputs) + at: at for at in range(len(carried))},
        compiler_params=pltpu.CompilerParams(vmem_limit_bytes=40 << 20),
        cost_estimate=pl.CostEstimate(flops=work, transcendentals=0, bytes_accessed=1 << 20),
    )(*inputs, *carried)


def finish_keys(own, others, k_raw, gain, cos_t, sin_t):
    _, rows, _, width, length = own.shape

    def kernel(own_ref, *refs):
        shares, (raw_ref, gain_ref, cos_ref, sin_ref, out_ref, gain_grad_ref) = refs[:-6], refs[-6:]

        def share(which, rows_of):
            total = own_ref[0, 0, which, rows_of, :]
            for ref in shares:
                total = total + ref[0, 0, which, rows_of, :].astype(jnp.float32)
            return total

        total = jnp.zeros((HD, 128), jnp.float32)
        for head in range(KV):
            rows_of = slice(head * HD, (head + 1) * HD)
            grad, products = head_back(
                share(0, rows_of), raw_ref[0, rows_of, :], gain_ref[...], cos_ref[...], sin_ref[...]
            )
            out_ref[0, rows_of, :] = grad.astype(LOW)
            out_ref[0, slice(width + head * HD, width + (head + 1) * HD), :] = share(1, rows_of).astype(LOW)
            total = total + fold(products)
        gain_grad_ref[0] = total

    piece_spec = pl.BlockSpec((1, 1, 2, width, length), lambda row: (0, row, 0, 0, 0))
    table_spec = pl.BlockSpec((HD, length), lambda row: (0, 0))
    return pl.pallas_call(
        kernel,
        out_shape=[
            jax.ShapeDtypeStruct((rows, 2 * width, length), LOW),
            jax.ShapeDtypeStruct((rows, HD, 128), jnp.float32),
        ],
        grid=(rows,),
        in_specs=[
            *[piece_spec] * (1 + len(others)),
            pl.BlockSpec((1, width, length), lambda row: (row, 0, 0)),
            pl.BlockSpec((HD, 1), lambda row: (0, 0)),
            table_spec,
            table_spec,
        ],
        out_specs=[
            pl.BlockSpec((1, 2 * width, length), lambda row: (row, 0, 0)),
            pl.BlockSpec((1, HD, 128), lambda row: (row, 0, 0)),
        ],
        compiler_params=pltpu.CompilerParams(vmem_limit_bytes=40 << 20),
    )(own, *others, k_raw, gain, cos_t, sin_t)


def local(
    tokens,
    cotangent,
    lengths,
    slot_sequence,
    attn_gain,
    w_qkv,
    q_gain,
    k_gain,
    w_out,
    ffn_gain,
    w_gate,
    w_up,
    w_down,
):
    row_count, piece_len, model_width = tokens.shape
    q_width = HEADS * HD
    kv_width = KV * HD
    total_rows = lengths.shape[0]
    scale_factor = 1.0 / math.sqrt(HD)
    shards = lax.axis_size("shard")
    devices = lax.axis_size("dp") * shards
    part_len = attn_gain.shape[0]
    shard_at = lax.axis_index("shard")
    me = (lax.axis_index("dp") * shards + shard_at).astype(jnp.int32).reshape(1)
    row_valid = jnp.sum(
        jnp.where(
            slot_sequence[:, None] == jnp.arange(total_rows, dtype=jnp.int32)[None, :],
            lengths[None, :],
            0,
        ),
        axis=1,
    )
    start = (shard_at * piece_len).astype(jnp.int32)
    positions = start + jnp.arange(piece_len, dtype=jnp.int32)
    live_mask = (positions[None, :] < row_valid[:, None]).astype(jnp.float32)
    cos_t, sin_t = tables(positions)
    cos_h = cos_t[None, None]
    sin_h = sin_t[None, None]
    q_gain_h = q_gain[None, None, :, None]
    k_gain_h = k_gain[None, None, :, None]

    gain_columns = jnp.concatenate(
        [attn_gain[:, None], ffn_gain[:, None], jnp.zeros((part_len, 126), jnp.float32)], axis=1
    ).astype(LOW)
    w_qkv_low, w_gate_low, w_up_low = w_qkv.astype(LOW), w_gate.astype(LOW), w_up.astype(LOW)
    gather_a = Gather([w_qkv_low[:, :q_width], w_qkv_low[:, q_width:], gain_columns], me, devices, True)
    gather_b = Gather([w_out.astype(LOW).T], me, devices)
    w_down_low = w_down.astype(LOW).T
    units = w_down_low.shape[1] // 2
    halves = slice(0, units), slice(units, 2 * units)
    gather_c = [
        Gather(
            [jnp.concatenate([w_gate_low[:, own], w_up_low[:, own]], axis=1), w_down_low[:, own]],
            me,
            devices,
        )
        for own in halves
    ]
    (tokens,) = open_slot([gather_a], tokens)
    x_float = tokens.astype(jnp.float32)
    normed_one, inverse_one = normalize(x_float)
    (normed_one,) = close_slot([gather_a], normed_one)
    (normed_one,) = open_slot([gather_a, gather_b], normed_one)
    (normed_one,) = close_slot([gather_a, gather_b], normed_one)
    (normed_one,) = open_slot([gather_a, gather_b], normed_one)
    (normed_one,) = close_slot([gather_a, gather_b], normed_one)
    (normed_one,) = open_slot([gather_a, gather_b, gather_c[0]], normed_one)
    (normed_one,) = close_slot([gather_a], normed_one)
    wq, wkv, gains = gather_a.whole()
    gain_attn = gains[:, 0].astype(jnp.float32)
    gain_ffn = gains[:, 1].astype(jnp.float32)
    normed_low = (normed_one * gain_attn).astype(LOW)
    kv_raw = jnp.einsum("rtd,de->ret", normed_low, wkv, preferred_element_type=jnp.float32)
    k_raw = kv_raw[:, :kv_width].reshape(row_count, KV, HD, piece_len)
    v_raw = kv_raw[:, kv_width:]
    k_unit, k_inverse = normalize(k_raw, 2)
    k_low = rotate(k_unit * k_gain_h, cos_h, sin_h).astype(LOW).reshape(row_count, kv_width, piece_len)
    own_kv = jnp.concatenate([k_low, v_raw.astype(LOW)], axis=1)
    own_kv, normed_low = close_slot([gather_b, gather_c[0]], own_kv, normed_low)
    row_pieces = Pieces(own_kv, devices, shards)
    (normed_low,) = open_slot([row_pieces, gather_b, gather_c[0]], normed_low)
    q_raw = jnp.einsum("rtd,de->ret", normed_low, wq, preferred_element_type=jnp.float32).reshape(
        row_count, HEADS, HD, piece_len
    )
    q_unit, q_inverse = normalize(q_raw, 2)
    q_low = (
        rotate(q_unit * q_gain_h, cos_h, sin_h).astype(LOW) * jnp.array(scale_factor, LOW)
    ).reshape(row_count, q_width, piece_len)
    (q_low,) = close_slot([row_pieces, gather_b, gather_c[0]], q_low)
    (q_low,) = open_slot([row_pieces, *gather_c], q_low)
    (q_low,) = close_slot([row_pieces], q_low)
    pieces, piece_at = row_pieces.whole()
    info = jnp.concatenate([start.reshape(1), piece_at * piece_len, row_valid]).astype(jnp.int32)
    o_heads, att_low, sums = attention(info, q_low, pieces, 0, KV)
    o_heads, att_low, sums = close_slot(gather_c, o_heads, att_low, sums)
    (att_low,) = open_slot(gather_c, att_low)
    (wout,) = gather_b.whole()
    x_mid = x_float + jnp.einsum("rct,dc->rtd", att_low, wout, preferred_element_type=jnp.float32)
    normed_two, inverse_two = normalize(x_mid)
    ffn_in = (normed_two * gain_ffn).astype(LOW)
    grad_out = cotangent.astype(jnp.float32) * live_mask[..., None]
    grad_low = grad_out.astype(LOW)

    def feed_forward(ffn_in, grad_low, wgu, wdown):
        both = jnp.einsum("rtd,df->rtf", ffn_in, wgu, preferred_element_type=jnp.float32)
        gate_proj, up_proj = both[..., :units], both[..., units:]
        gate_sig = jax.nn.sigmoid(gate_proj)
        silu_gate = gate_proj * gate_sig
        activated = (silu_gate * up_proj).astype(LOW)
        grad_down = jnp.einsum("rtd,rtf->df", grad_low, activated, preferred_element_type=jnp.float32)
        grad_act = jnp.einsum("rtd,df->rtf", grad_low, wdown, preferred_element_type=jnp.float32)
        grad_gate = (grad_act * up_proj * gate_sig * (1.0 + gate_proj * (1.0 - gate_sig))).astype(LOW)
        grad_up = (grad_act * silu_gate).astype(LOW)
        grad_both = jnp.concatenate([grad_gate, grad_up], axis=2)
        grad_wgu = jnp.einsum("rtd,rtf->df", ffn_in, grad_both, preferred_element_type=jnp.float32)
        return activated, grad_both, [grad_wgu.astype(LOW), grad_down.astype(LOW)]

    ffn_in, x_mid = close_slot(gather_c, ffn_in, x_mid)
    (ffn_in,) = open_slot([gather_c[1]], ffn_in)
    wgu_one, wdown_one = gather_c[0].whole()
    act_one, both_one, grads = feed_forward(ffn_in, grad_low, wgu_one, wdown_one)
    red_one = Reduce(grads, me, devices)
    red_one.prepare()
    ffn_in, red_one.outgoing, act_one, both_one = close_slot(
        [gather_c[1]], ffn_in, red_one.outgoing, act_one, both_one
    )
    (ffn_in,) = open_slot([gather_c[1]], ffn_in)
    (ffn_in,) = open_slot([red_one], ffn_in, ready=[red_one])
    (ffn_in,) = close_slot([gather_c[1]], ffn_in)
    wgu_two, wdown_two = gather_c[1].whole()
    ffn_in, wgu_two, wdown_two = close_slot([red_one], ffn_in, wgu_two, wdown_two)
    (ffn_in,) = open_slot([red_one], ffn_in)
    act_two, both_two, grads = feed_forward(ffn_in, grad_low, wgu_two, wdown_two)
    red_two = Reduce(grads, me, devices)
    red_two.prepare()
    ffn_in, red_two.outgoing, act_two, both_two = close_slot(
        [red_one], ffn_in, red_two.outgoing, act_two, both_two
    )
    both_two, act_two = open_slot([red_one, red_two], both_two, act_two, ready=[red_two])
    grad_ffn_in = jnp.einsum(
        "rtf,df->rtd", both_one, wgu_one, preferred_element_type=jnp.float32
    ) + jnp.einsum("rtf,df->rtd", both_two, wgu_two, preferred_element_type=jnp.float32)
    grad_mid = grad_out + norm_back(x_mid, inverse_two, grad_ffn_in * gain_ffn)
    mid_low = grad_mid.astype(LOW)
    grad_wout = jnp.einsum("rtd,rct->dc", mid_low, att_low, preferred_element_type=jnp.float32)
    grad_att = jnp.einsum("rtd,dc->rct", mid_low, wout, preferred_element_type=jnp.float32)
    red_out = Reduce([grad_wout.astype(LOW)], me, devices)
    red_out.prepare()
    grad_att, red_out.outgoing = close_slot([red_one, red_two], grad_att, red_out.outgoing)
    grad_att, act_two = open_slot([red_one, red_two], grad_att, act_two)

    q_gain_c, k_gain_c = q_gain[:, None], k_gain[:, None]
    q_raw_flat = q_raw.reshape(row_count, q_width, piece_len)
    k_raw_flat = k_raw.reshape(row_count, kv_width, piece_len)

    def back(group, grad_att, carried=()):
        return attention_back(
            info, q_low, pieces, o_heads, sums, grad_att, q_raw_flat, q_gain_c, cos_t, sin_t, group, carried
        )

    output = (
        x_mid
        + jnp.einsum("rtf,df->rtd", act_one, wdown_one, preferred_element_type=jnp.float32)
        + jnp.einsum("rtf,df->rtd", act_two, wdown_two, preferred_element_type=jnp.float32)
    ).astype(LOW)
    gain_parts = []

    def more(group, grad_att, carried=()):
        *carried, gain_part = back(group, grad_att, carried)
        gain_parts.append(gain_part)
        return tuple(carried)

    carried = more(0, grad_att)
    carried, grad_att, output = close_slot([red_one, red_two], carried, grad_att, output)
    red_one.prepare()
    (grad_att,) = open_slot([red_two, red_out], grad_att, ready=[red_out])
    carried = more(1, grad_att, carried)
    carried, grad_att = close_slot([red_two, red_out], carried, grad_att)
    (grad_att,) = open_slot([red_two, red_out], grad_att)
    carried = more(2, grad_att, carried)
    carried, grad_att = close_slot([red_two, red_out], carried, grad_att)
    red_two.prepare()
    (grad_att,) = open_slot([red_out], grad_att)
    carried = more(3, grad_att, carried)
    grad_q_low, grad_pieces = close_slot([red_out], carried)[0]
    kv_back = PiecesBack(grad_pieces, devices, shards)
    (grad_q_low,) = open_slot([kv_back], grad_q_low)
    grad_wq = jnp.einsum("rtd,ret->de", normed_low, grad_q_low, preferred_element_type=jnp.float32)
    red_q = Reduce([grad_wq.astype(LOW)], me, devices)
    red_q.prepare()
    red_q.outgoing, grad_q_low = close_slot([kv_back], red_q.outgoing, grad_q_low)
    (grad_q_low,) = open_slot([kv_back, red_q], grad_q_low, ready=[red_q])
    grad_normed_q = jnp.einsum("ret,de->rtd", grad_q_low, wq, preferred_element_type=jnp.float32)
    (grad_normed_q,) = close_slot([kv_back, red_q], grad_normed_q)
    kv_back.prepare()
    grad_kv_low, k_gain_part = finish_keys(*kv_back.shares, k_raw_flat, k_gain_c, cos_t, sin_t)
    shared = Sum(
        jnp.concatenate([jnp.sum(sum(gain_parts), axis=(0, 2)), jnp.sum(k_gain_part, axis=(0, 2))])[None],
        devices,
    )
    (grad_kv_low,) = open_slot([red_q, shared, red_out], grad_kv_low)
    grad_wkv = jnp.einsum("rtd,ret->de", normed_low, grad_kv_low, preferred_element_type=jnp.float32)
    red_kv = Reduce([grad_wkv.astype(LOW)], me, devices)
    red_kv.prepare()
    red_kv.outgoing, grad_kv_low = close_slot([red_q, red_out, shared], red_kv.outgoing, grad_kv_low)
    red_out.prepare()
    (grad_kv_low,) = open_slot([red_q, red_kv, shared], grad_kv_low, ready=[red_kv])
    grad_normed = grad_normed_q + jnp.einsum(
        "ret,de->rtd", grad_kv_low, wkv, preferred_element_type=jnp.float32
    )
    input_grad = grad_mid + norm_back(x_float, inverse_one, grad_normed * gain_attn)
    (input_grad,) = close_slot([red_q, red_kv, shared], input_grad)
    open_slot([red_q, red_kv, shared])
    close_slot([red_q, red_kv, shared])
    red_q.prepare()
    open_slot([red_kv, shared])
    close_slot([red_kv, shared])
    open_slot([red_kv, shared])
    close_slot([red_kv, shared])
    red_kv.prepare()
    shared.prepare()
    shared = shared.values
    three, four = red_q.total, red_kv.total
    summed = red_one.total, red_two.total
    summed_wgate, summed_wup, summed_down = (
        jnp.concatenate([one[:, at * units : (at + 1) * units] for one in summed], axis=1) for at in range(3)
    )
    summed_down, summed_wout = summed_down.T, red_out.total.T
    summed_wqkv = jnp.concatenate([three, four], axis=1)
    grad_gain_one = jnp.sum(summed_wqkv * w_qkv_low, axis=1) / attn_gain.astype(LOW)
    grad_gain_two = jnp.sum(summed_wgate * w_gate_low + summed_wup * w_up_low, axis=1) / ffn_gain.astype(LOW)
    return (
        output,
        input_grad,
        grad_gain_one,
        summed_wqkv,
        shared[0, :HD],
        shared[0, HD:],
        summed_wout,
        grad_gain_two,
        summed_wgate,
        summed_wup,
        summed_down,
    )


def solution(mesh):
    in_specs = (
        P("dp", "shard", None),
        P("dp", "shard", None),
        P(),
        P("dp"),
        P(("dp", "shard")),
        P(("dp", "shard"), None),
        P(),
        P(),
        P(None, ("dp", "shard")),
        P(("dp", "shard")),
        P(("dp", "shard"), None),
        P(("dp", "shard"), None),
        P(None, ("dp", "shard")),
    )
    out_specs = (
        P("dp", "shard", None),
        P("dp", "shard", None),
        P(("dp", "shard")),
        P(("dp", "shard"), None),
        P(),
        P(),
        P(None, ("dp", "shard")),
        P(("dp", "shard")),
        P(("dp", "shard"), None),
        P(("dp", "shard"), None),
        P(None, ("dp", "shard")),
    )
    return jax.shard_map(local, mesh=mesh, in_specs=in_specs, out_specs=out_specs, check_vma=False)
```

```python
import functools
import math

import jax
import jax.numpy as jnp
from jax import lax
from jax.experimental import pallas as pl
from jax.experimental.pallas import tpu as pltpu
from jax.sharding import PartitionSpec as P

HEADS = 16
KV = 4
HD = 64
GROUP = HEADS // KV
EPS = 1e-06
LOW = jnp.bfloat16
ANY = pl.BlockSpec(memory_space=pl.ANY)
VMEM = pl.BlockSpec(memory_space=pltpu.VMEM)
SMEM = pl.BlockSpec(memory_space=pltpu.SMEM)
FIRST_FIRST = (((0,), (0,)), ((), ()))
LAST_FIRST = (((1,), (0,)), ((), ()))
LAST_LAST = (((1,), (1,)), ((), ()))


def dot(left, right, dims):
    return lax.dot_general(left, right, dims, preferred_element_type=jnp.float32)


def normalize(values, axis=-1):
    inverse = lax.rsqrt(jnp.mean(values * values, axis=axis, keepdims=True) + EPS)
    return (values * inverse, inverse)


def norm_back(values, inverse, grad_normed, axis=-1):
    cubed = inverse * inverse * inverse
    return inverse * grad_normed - values * cubed * jnp.mean(
        grad_normed * values, axis=axis, keepdims=True
    )


def rotate(values, cos_t, sin_t):
    half_len = HD // 2
    turned = jnp.concatenate([-values[:, :, half_len:], values[:, :, :half_len]], axis=2)
    return values * cos_t + turned * sin_t


def rotate_back(grad_in, cos_t, sin_t):
    half_len = HD // 2
    along = grad_in * sin_t
    return grad_in * cos_t + jnp.concatenate([along[:, :, half_len:], -along[:, :, :half_len]], axis=2)


def tables(positions):
    freq = 10000.0 ** (-(2.0 * jnp.arange(HD // 2, dtype=jnp.float32)) / HD)
    angles = freq[:, None] * positions.astype(jnp.float32)[None, :]
    angles = jnp.concatenate([angles, angles], axis=0)
    return (jnp.cos(angles), jnp.sin(angles))


def swap(values, mask, devices):
    return lax.ppermute(values, ("dp", "shard"), [(i, i ^ mask) for i in range(devices)])


def place(blocks, masks, widths, me, total_rows):
    count = len(blocks)
    size = blocks[0].shape[0] // len(masks[0])
    copies = sum(len(own) for own in masks) * len(widths)

    def kernel(me_ref, *refs):
        sources, outs, sems = refs[:count], refs[count:-1], refs[-1]
        started = []
        for array, own in zip(sources, masks):
            for at, mask in enumerate(own):
                row = pl.multiple_of((me_ref[0] ^ mask) * size, size)
                column = 0
                for out, width in zip(outs, widths):
                    copy = pltpu.make_async_copy(
                        array.at[pl.ds(at * size, size), pl.ds(column, width)],
                        out.at[pl.ds(row, size)],
                        sems.at[len(started)],
                    )
                    copy.start()
                    started.append(copy)
                    column += width
        for copy in started:
            copy.wait()

    return pl.pallas_call(
        kernel,
        out_shape=[jax.ShapeDtypeStruct((total_rows, width), blocks[0].dtype) for width in widths],
        in_specs=[SMEM] + [ANY] * count,
        out_specs=[VMEM] * len(widths),
        scratch_shapes=[pltpu.SemaphoreType.DMA((copies,))],
        compiler_params=pltpu.CompilerParams(vmem_limit_bytes=24 << 20),
        cost_estimate=pl.CostEstimate(flops=0, transcendentals=0, bytes_accessed=1 << 16),
    )(me, *blocks)


def pick(arrays, orders, me, size):
    count = len(arrays)
    copies = sum(len(own) for own in orders) * count
    width = sum(array.shape[1] for array in arrays)

    def kernel(me_ref, *refs):
        sources, outs, sems = refs[:count], refs[count:-1], refs[-1]
        started = []
        for out, own in zip(outs, orders):
            for at, mask in enumerate(own):
                row = pl.multiple_of((me_ref[0] ^ mask) * size, size)
                column = 0
                for array in sources:
                    copy = pltpu.make_async_copy(
                        array.at[pl.ds(row, size)],
                        out.at[pl.ds(at * size, size), pl.ds(column, array.shape[1])],
                        sems.at[len(started)],
                    )
                    copy.start()
                    started.append(copy)
                    column += array.shape[1]
        for copy in started:
            copy.wait()

    return pl.pallas_call(
        kernel,
        out_shape=[jax.ShapeDtypeStruct((len(own) * size, width), arrays[0].dtype) for own in orders],
        in_specs=[SMEM] + [VMEM] * count,
        out_specs=[ANY] * len(orders),
        scratch_shapes=[pltpu.SemaphoreType.DMA((copies,))],
        compiler_params=pltpu.CompilerParams(vmem_limit_bytes=24 << 20),
        cost_estimate=pl.CostEstimate(flops=0, transcendentals=0, bytes_accessed=1 << 16),
    )(me, *arrays)


class Gather:
    def __init__(self, parts, me, devices, first=False, spread=False):
        self.part = jnp.concatenate(parts, axis=1)
        self.widths = [one.shape[1] for one in parts]
        self.me, self.devices, self.staged, self.first = me, devices, devices == 32, first
        self.stage, self.outgoing, self.incoming = -1 if spread else 0, (), ()
        self.spread = spread

    def prepare(self):
        stage = self.stage
        self.stage += 1
        if not self.staged:
            return
        if stage == -1:
            self.outgoing, self.masks = (self.part,), ((8,),)
        elif stage == 0 and self.spread:
            self.outgoing, self.masks = (jnp.concatenate([self.part, *self.incoming]),), ((16,),)
        elif stage == 0:
            self.outgoing, self.masks = (self.part,), ((8, 16, 24),)
        elif stage == 1:
            if self.spread:
                self.outgoing += self.incoming
            else:
                one, two, three = self.incoming
                self.outgoing = jnp.concatenate([self.part, one]), jnp.concatenate([two, three])
            self.masks = (4,), (2,)
        elif stage == 2:
            self.outgoing = tuple(
                jnp.concatenate([own, came]) for own, came in zip(self.outgoing, self.incoming)
            )
            self.masks = (2,), (4,)
        elif self.first:
            self.outgoing, self.masks = self.outgoing + self.incoming, ((1,),) * 4
        else:
            self.outgoing, self.masks = (jnp.concatenate([*self.outgoing, *self.incoming]),), ((1,),)

    def launch(self):
        if self.staged:
            self.incoming = tuple(
                swap(one, mask, self.devices) for one, own in zip(self.outgoing, self.masks) for mask in own
            )

    def whole(self):
        if not self.staged:
            whole = lax.all_gather(self.part, ("dp", "shard"), axis=0, tiled=True)
            ends = [sum(self.widths[:i]) for i in range(1, len(self.widths))]
            return jnp.split(whole, ends, axis=1)
        near, far = (0, 8, 4, 12), (16, 24, 18, 26)
        masks = [near, far, [m | 2 for m in near], [m | 4 for m in far]]
        if not self.first:
            masks = [[m for own in masks for m in own]]
        masks += [[m | 1 for m in own] for own in masks]
        blocks = self.outgoing + self.incoming
        return place(blocks, masks, self.widths, self.me, self.part.shape[0] * self.devices)


class Reduce:
    def __init__(self, grads, me, devices, spread=False):
        self.grads, self.me, self.devices, self.staged = grads, me, devices, devices == 32
        self.spread = spread
        self.size = grads[0].shape[0] // devices
        self.stage, self.outgoing, self.incoming = 0, (), ()

    def both(self, low, high):
        rows = slice(low * self.size, high * self.size)
        return self.keep[rows].astype(jnp.float32) + self.came[rows].astype(jnp.float32)

    def prepare(self):
        stage, size = self.stage, self.size
        self.stage += 1
        if not self.staged:
            if stage == 0:
                grad = jnp.concatenate([one.astype(jnp.float32) for one in self.grads], axis=1)
                self.total = lax.psum_scatter(grad, ("dp", "shard"), scatter_dimension=0, tiled=True)
            return
        incoming = [one.astype(jnp.float32) for one in self.incoming]
        if stage == 0:
            order = [2, 10, 6, 14, 20, 28, 22, 30, 0, 8, 4, 12, 16, 24, 18, 26]
            self.keep, send = pick(self.grads, [order, [m | 1 for m in order]], self.me, size)
            self.outgoing, self.masks = (send,), (1,)
        elif stage == 1:
            (self.came,) = self.incoming
            self.outgoing = self.both(0, 4).astype(LOW), self.both(4, 8).astype(LOW)
            self.masks = 2, 4
        elif stage == 2:
            near, far = self.both(8, 12) + incoming[0], self.both(12, 16) + incoming[1]
            self.outgoing = near[2 * size :].astype(LOW), far[2 * size :].astype(LOW)
            self.near, self.far = near[: 2 * size], far[: 2 * size]
            self.masks = 4, 2
        elif stage == 3 and self.spread:
            self.near = self.near + incoming[0]
            self.outgoing, self.masks = ((self.far + incoming[1]).astype(LOW),), (16,)
        elif stage == 4 and self.spread:
            near = self.near + incoming[0]
            self.own = near[:size]
            self.outgoing, self.masks = (near[size:].astype(LOW),), (8,)
        elif self.spread and stage > 4:
            self.total = self.own + incoming[0]
        elif stage == 3:
            near, far = self.near + incoming[0], self.far + incoming[1]
            self.outgoing = near[size:].astype(LOW), far[:size].astype(LOW), far[size:].astype(LOW)
            self.own, self.masks = near[:size], (8, 16, 24)
        else:
            self.total = (self.own + incoming[0]) + (incoming[1] + incoming[2])

    def launch(self):
        if self.staged:
            self.incoming = tuple(
                swap(one, mask, self.devices) for one, mask in zip(self.outgoing, self.masks)
            )


class Sum:
    def __init__(self, values, devices):
        self.values, self.devices, self.staged = values, devices, devices == 32
        self.stage, self.outgoing, self.incoming = 0, (), ()

    def prepare(self):
        stage = self.stage
        self.stage += 1
        if not self.staged:
            if stage == 0:
                self.values = lax.psum(self.values, ("dp", "shard"))
            return
        if stage:
            self.values = self.values + self.incoming[0]
        if stage < 5:
            self.outgoing, self.masks = (self.values,), ((1,), (2,), (4,), (8,), (16,))[stage]

    def launch(self):
        if self.staged:
            self.incoming = tuple(swap(self.outgoing[0], mask, self.devices) for mask in self.masks)


def open_slot(travellers, *values, ready=()):
    for one in travellers:
        if one not in ready:
            one.prepare()
    travellers = [one for one in travellers if one.staged]
    if not travellers:
        return values
    outgoing, values = lax.optimization_barrier((tuple(one.outgoing for one in travellers), values))
    for one, sent in zip(travellers, outgoing):
        one.outgoing = sent
        one.launch()
    return values


def close_slot(travellers, *values):
    travellers = [one for one in travellers if one.staged]
    if not travellers:
        return values
    incoming, values = lax.optimization_barrier((tuple(one.incoming for one in travellers), values))
    for one, came in zip(travellers, incoming):
        one.incoming = came
    return values


class Pieces:
    def __init__(self, part, devices, shards):
        self.part, self.devices, self.shards = part, devices, shards
        self.staged = devices == 32 and shards == 4
        self.stage, self.outgoing, self.incoming = 0, (), ()

    def prepare(self):
        stage = self.stage
        self.stage += 1
        if stage == 0:
            self.outgoing, self.mask = (self.part,), 2
        elif self.staged:
            self.outgoing, self.mask = (jnp.stack([self.part, *self.incoming]),), 1

    def launch(self):
        if self.staged:
            self.incoming = (swap(self.outgoing[0], self.mask, self.devices),)

    def whole(self):
        if not self.staged:
            return lax.all_gather(self.part, "shard", axis=0), jnp.arange(self.shards, dtype=jnp.int32)
        at = jnp.array([0, 2, 1, 3], jnp.int32) ^ lax.axis_index("shard")
        return jnp.concatenate([self.outgoing[0], self.incoming[0]]), at


class PiecesBack:
    def __init__(self, grad, devices, shards):
        self.grad, self.devices, self.staged = grad, devices, devices == 32 and shards == 4
        self.stage, self.outgoing, self.incoming = 0, (), ()

    def prepare(self):
        stage, grad = self.stage, self.grad
        self.stage += 1
        if not self.staged:
            if stage == 0:
                self.shares = lax.psum_scatter(grad, "shard", scatter_dimension=0)[None], ()
        elif stage == 0:
            self.outgoing, self.mask = (grad[2:].astype(LOW),), 1
        elif stage == 1:
            (self.came,) = self.incoming
            self.over = (grad[1:2] + self.came[1:].astype(jnp.float32)).astype(LOW)
            self.outgoing, self.mask = (self.over[:, :, :1],), 2
        elif stage == 2:
            (self.keys,) = self.incoming
            self.outgoing = (self.over[:, :, 1:],)
        else:
            self.shares = grad, (self.came, jnp.concatenate([self.keys, *self.incoming], axis=2))

    def launch(self):
        if self.staged:
            self.incoming = (swap(self.outgoing[0], self.mask, self.devices),)


def allowed(base, start, valid, key_axis, shape):
    key = base + lax.broadcasted_iota(jnp.int32, shape, key_axis)
    query = start + lax.broadcasted_iota(jnp.int32, shape, 1 - key_axis)
    return (key <= query) & (key < valid)


def over_pieces(info_ref, pieces, length, row, tile, before=None, after=None):
    start, valid = info_ref[0], info_ref[1 + pieces + row]

    def one(piece, carry):
        base = info_ref[1 + piece]
        if before is not None:
            before()
        used = (base < start + length) & (base < valid)
        full = (base + length <= start) & (base + length <= valid)
        pl.when(used & full)(lambda: tile(piece, None))
        pl.when(used & jnp.logical_not(full))(lambda: tile(piece, (base, start, valid)))
        if after is not None:
            after(piece)
        return carry

    lax.fori_loop(0, pieces, one, 0)


def attention(info, queries, keys_values, first, groups):
    rows, _, length = queries.shape
    pieces = keys_values.shape[0]
    group_width = GROUP * HD

    def kernel(info_ref, q_ref, k_ref, v_ref, out_ref, low_ref, sums_ref, accum_ref, part_ref):
        accum_ref[...] = jnp.zeros_like(accum_ref)
        part_ref[...] = jnp.zeros_like(part_ref)

        def tile(piece, bounds):
            key_t, value_t = k_ref[piece, 0], v_ref[piece, 0]
            if bounds is not None:
                mask = allowed(*bounds, 1, (length, length))
            for head in range(GROUP):
                exps = jnp.exp(dot(q_ref[0, head * HD : (head + 1) * HD, :], key_t, FIRST_FIRST))
                if bounds is not None:
                    exps = jnp.where(mask, exps, 0.0)
                width = min(128, length)
                part = exps[:, :width]
                for at in range(width, length, width):
                    part = part + exps[:, at : at + width]
                part_ref[head] += part
                accum_ref[head] += dot(exps.astype(LOW), value_t, LAST_LAST)

        over_pieces(info_ref, pieces, length, pl.program_id(0), tile)
        for head in range(GROUP):
            own = slice(head * HD, (head + 1) * HD)
            sums = jnp.sum(part_ref[head].T, axis=0, keepdims=True)
            sums_ref[0, 0, head : head + 1, :] = sums
            out = accum_ref[head].T / sums
            out_ref[0, own, :] = out
            low_ref[0, own, :] = out.astype(LOW)

    q_spec = pl.BlockSpec((1, group_width, length), lambda row, group, *_: (row, group + first, 0))
    o_spec = pl.BlockSpec((1, group_width, length), lambda row, group, *_: (row, group, 0))
    k_spec = pl.BlockSpec((pieces, 1, HD, length), lambda row, group, *_: (0, row, group + first, 0))
    v_spec = pl.BlockSpec(
        (pieces, 1, HD, length), lambda row, group, *_: (0, row, group + first + KV, 0)
    )
    s_spec = pl.BlockSpec((1, 1, GROUP, length), lambda row, group, *_: (row, group, 0, 0))
    work = rows * groups * GROUP * length * length * pieces
    return pl.pallas_call(
        kernel,
        out_shape=[
            jax.ShapeDtypeStruct((rows, groups * group_width, length), jnp.float32),
            jax.ShapeDtypeStruct((rows, groups * group_width, length), LOW),
            jax.ShapeDtypeStruct((rows, groups, GROUP, length), jnp.float32),
        ],
        grid_spec=pltpu.PrefetchScalarGridSpec(
            num_scalar_prefetch=1,
            grid=(rows, groups),
            in_specs=[q_spec, k_spec, v_spec],
            out_specs=[o_spec, o_spec, s_spec],
            scratch_shapes=[
                pltpu.VMEM((GROUP, length, HD), jnp.float32),
                pltpu.VMEM((GROUP, length, min(128, length)), jnp.float32),
            ],
        ),
        compiler_params=pltpu.CompilerParams(vmem_limit_bytes=16 << 20),
        cost_estimate=pl.CostEstimate(flops=work, transcendentals=0, bytes_accessed=1 << 20),
    )(info, queries, keys_values, keys_values)


def head_back(grad, raw, gain, cos_t, sin_t):
    half_len = HD // 2
    along = grad * sin_t
    grad = grad * cos_t + jnp.concatenate([along[half_len:], -along[:half_len]], axis=0)
    inverse = lax.rsqrt(jnp.mean(raw * raw, axis=0, keepdims=True) + EPS)
    products = grad * (raw * inverse)
    grad = grad * gain
    cubed = inverse * inverse * inverse
    return inverse * grad - raw * cubed * jnp.mean(grad * raw, axis=0, keepdims=True), products


def fold(values):
    total = values[:, :128]
    for at in range(128, values.shape[1], 128):
        total = total + values[:, at : at + 128]
    return total


def attention_back(
    info, queries, keys_values, out, sums, grad_out, q_raw, gain, cos_t, sin_t, group, carried
):
    rows, _, length = queries.shape
    pieces = keys_values.shape[0]
    group_width = GROUP * HD
    scale_factor = 1.0 / math.sqrt(HD)

    def kernel(
        info_ref, q_ref, k_ref, v_ref, out_ref, sums_ref, grad_ref, raw_ref, gain_ref, cos_ref, sin_ref, *refs
    ):
        refs = refs[len(carried) :]
        dq_ref, dkv_ref, gain_grad_ref = refs[:3]
        grad_low, grad_sums, q_rows, grad_rows, k_accum, v_accum, q_accum = refs[3:]
        q_accum[...] = jnp.zeros_like(q_accum)
        for head in range(GROUP):
            own = slice(head * HD, (head + 1) * HD)
            inverse = 1.0 / sums_ref[0, 0, head : head + 1, :]
            grad = grad_ref[0, own, :]
            grad_sums[head] = -jnp.sum(grad * out_ref[0, own, :], axis=0, keepdims=True) * inverse
            scaled = grad * inverse
            grad_low[own, :] = scaled.astype(LOW)
            grad_rows[head] = scaled.T.astype(LOW)
            q_rows[head] = q_ref[0, own, :].T

        def tile(piece, bounds):
            key_t, value_t = k_ref[piece, 0], v_ref[piece, 0]
            if bounds is not None:
                mask = allowed(*bounds, 0, (length, length))
            for head in range(GROUP):
                own = slice(head * HD, (head + 1) * HD)
                exps = jnp.exp(dot(key_t, q_ref[0, own, :], FIRST_FIRST))
                if bounds is not None:
                    exps = jnp.where(mask, exps, 0.0)
                grad_exps = dot(value_t, grad_low[own, :], FIRST_FIRST) + grad_sums[head]
                grad_scores = (exps * grad_exps).astype(LOW)
                v_accum[...] += dot(exps.astype(LOW), grad_rows[head], LAST_FIRST)
                k_accum[...] += dot(grad_scores, q_rows[head], LAST_FIRST)
                q_accum[own, :] += dot(key_t, grad_scores, LAST_FIRST)

        def before():
            k_accum[...] = jnp.zeros_like(k_accum)
            v_accum[...] = jnp.zeros_like(v_accum)

        def after(piece):
            dkv_ref[piece, 0, 0] = k_accum[...].T
            dkv_ref[piece, 0, 1] = v_accum[...].T

        over_pieces(info_ref, pieces, length, pl.program_id(0), tile, before, after)
        total = jnp.zeros((HD, 128), jnp.float32)
        for head in range(GROUP):
            own = slice(head * HD, (head + 1) * HD)
            grad, products = head_back(
                scale_factor * q_accum[own, :], raw_ref[0, own, :], gain_ref[...], cos_ref[...], sin_ref[...]
            )
            dq_ref[0, own, :] = grad.astype(LOW)
            total = total + fold(products)
        gain_grad_ref[0] = total

    q_spec = pl.BlockSpec((1, group_width, length), lambda row, *_: (row, group, 0))
    k_spec = pl.BlockSpec((pieces, 1, HD, length), lambda row, *_: (0, row, group, 0))
    v_spec = pl.BlockSpec((pieces, 1, HD, length), lambda row, *_: (0, row, group + KV, 0))
    s_spec = pl.BlockSpec((1, 1, GROUP, length), lambda row, *_: (row, group, 0, 0))
    table_spec = pl.BlockSpec((HD, length), lambda row, *_: (0, 0))
    gain_spec = pl.BlockSpec((HD, 1), lambda row, *_: (0, 0))
    dkv_spec = pl.BlockSpec((pieces, 1, 2, HD, length), lambda row, *_: (0, row, 0, group, 0))
    work = rows * GROUP * length * length * pieces
    inputs = [info, queries, keys_values, keys_values, out, sums, grad_out, q_raw, gain, cos_t, sin_t]
    return pl.pallas_call(
        kernel,
        out_shape=[
            jax.ShapeDtypeStruct(queries.shape, LOW),
            jax.ShapeDtypeStruct((pieces, rows, 2, KV * HD, length), jnp.float32),
            jax.ShapeDtypeStruct((rows, HD, 128), jnp.float32),
        ],
        grid_spec=pltpu.PrefetchScalarGridSpec(
            num_scalar_prefetch=1,
            grid=(rows,),
            in_specs=[
                q_spec, k_spec, v_spec, q_spec, s_spec, q_spec, q_spec, gain_spec, table_spec, table_spec,
                *[ANY] * len(carried),
            ],
            out_specs=[q_spec, dkv_spec, pl.BlockSpec((1, HD, 128), lambda row, *_: (row, 0, 0))],
            scratch_shapes=[
                pltpu.VMEM((group_width, length), LOW),
                pltpu.VMEM((GROUP, 1, length), jnp.float32),
                pltpu.VMEM((GROUP, length, HD), LOW),
                pltpu.VMEM((GROUP, length, HD), LOW),
                pltpu.VMEM((length, HD), jnp.float32),
                pltpu.VMEM((length, HD), jnp.float32),
                pltpu.VMEM((group_width, length), jnp.float32),
            ],
        ),
        input_output_aliases={len(inputs) + at: at for at in range(len(carried))},
        compiler_params=pltpu.CompilerParams(vmem_limit_bytes=16 << 20),
        cost_estimate=pl.CostEstimate(flops=work, transcendentals=0, bytes_accessed=1 << 20),
    )(*inputs, *carried)


def finish_keys(own, others, k_raw, gain, cos_t, sin_t):
    _, rows, _, width, length = own.shape

    def kernel(own_ref, *refs):
        shares, (raw_ref, gain_ref, cos_ref, sin_ref, out_ref, gain_grad_ref) = refs[:-6], refs[-6:]

        def share(which, rows_of):
            total = own_ref[0, 0, which, rows_of, :]
            for ref in shares:
                total = total + ref[0, 0, which, rows_of, :].astype(jnp.float32)
            return total

        total = jnp.zeros((HD, 128), jnp.float32)
        for head in range(KV):
            rows_of = slice(head * HD, (head + 1) * HD)
            grad, products = head_back(
                share(0, rows_of), raw_ref[0, rows_of, :], gain_ref[...], cos_ref[...], sin_ref[...]
            )
            out_ref[0, rows_of, :] = grad.astype(LOW)
            out_ref[0, slice(width + head * HD, width + (head + 1) * HD), :] = share(1, rows_of).astype(LOW)
            total = total + fold(products)
        gain_grad_ref[0] = total

    piece_spec = pl.BlockSpec((1, 1, 2, width, length), lambda row: (0, row, 0, 0, 0))
    table_spec = pl.BlockSpec((HD, length), lambda row: (0, 0))
    return pl.pallas_call(
        kernel,
        out_shape=[
            jax.ShapeDtypeStruct((rows, 2 * width, length), LOW),
            jax.ShapeDtypeStruct((rows, HD, 128), jnp.float32),
        ],
        grid=(rows,),
        in_specs=[
            *[piece_spec] * (1 + len(others)),
            pl.BlockSpec((1, width, length), lambda row: (row, 0, 0)),
            pl.BlockSpec((HD, 1), lambda row: (0, 0)),
            table_spec,
            table_spec,
        ],
        out_specs=[
            pl.BlockSpec((1, 2 * width, length), lambda row: (row, 0, 0)),
            pl.BlockSpec((1, HD, 128), lambda row: (row, 0, 0)),
        ],
        compiler_params=pltpu.CompilerParams(vmem_limit_bytes=16 << 20),
    )(own, *others, k_raw, gain, cos_t, sin_t)


def local(
    tokens,
    cotangent,
    lengths,
    slot_sequence,
    attn_gain,
    w_qkv,
    q_gain,
    k_gain,
    w_out,
    ffn_gain,
    w_gate,
    w_up,
    w_down,
):
    row_count, piece_len, model_width = tokens.shape
    q_width = HEADS * HD
    kv_width = KV * HD
    total_rows = lengths.shape[0]
    scale_factor = 1.0 / math.sqrt(HD)
    shards = lax.axis_size("shard")
    devices = lax.axis_size("dp") * shards
    part_len = attn_gain.shape[0]
    shard_at = lax.axis_index("shard")
    me = (lax.axis_index("dp") * shards + shard_at).astype(jnp.int32).reshape(1)
    row_valid = jnp.sum(
        jnp.where(
            slot_sequence[:, None] == jnp.arange(total_rows, dtype=jnp.int32)[None, :],
            lengths[None, :],
            0,
        ),
        axis=1,
    )
    start = (shard_at * piece_len).astype(jnp.int32)
    positions = start + jnp.arange(piece_len, dtype=jnp.int32)
    live_mask = (positions[None, :] < row_valid[:, None]).astype(jnp.float32)
    cos_t, sin_t = tables(positions)
    cos_h = cos_t[None, None]
    sin_h = sin_t[None, None]
    q_gain_h = q_gain[None, None, :, None]
    k_gain_h = k_gain[None, None, :, None]

    gain_columns = jnp.concatenate(
        [attn_gain[:, None], ffn_gain[:, None], jnp.zeros((part_len, 126), jnp.float32)], axis=1
    ).astype(LOW)
    w_qkv_low, w_gate_low, w_up_low = w_qkv.astype(LOW), w_gate.astype(LOW), w_up.astype(LOW)
    gather_a = Gather([w_qkv_low[:, :q_width], w_qkv_low[:, q_width:], gain_columns], me, devices, True)
    gather_b = Gather([w_out.astype(LOW).T], me, devices)
    w_down_low = w_down.astype(LOW).T
    units = w_down_low.shape[1] // 2
    halves = slice(0, units), slice(units, 2 * units)
    gather_c = [
        Gather(
            [jnp.concatenate([w_gate_low[:, own], w_up_low[:, own]], axis=1), w_down_low[:, own]],
            me,
            devices,
            spread=own is halves[1],
        )
        for own in halves
    ]
    (tokens,) = open_slot([gather_a], tokens)
    x_float = tokens.astype(jnp.float32)
    normed_one, inverse_one = normalize(x_float)
    (normed_one,) = close_slot([gather_a], normed_one)
    (normed_one,) = open_slot([gather_a, gather_c[0]], normed_one)
    (normed_one,) = close_slot([gather_a, gather_c[0]], normed_one)
    (normed_one,) = open_slot([gather_a, gather_b], normed_one)
    (normed_one,) = close_slot([gather_a, gather_b], normed_one)
    (normed_one,) = open_slot([gather_a, gather_c[0]], normed_one)
    (normed_one,) = close_slot([gather_a], normed_one)
    wq, wkv, gains = gather_a.whole()
    gain_attn = gains[:, 0].astype(jnp.float32)
    gain_ffn = gains[:, 1].astype(jnp.float32)
    normed_low = (normed_one * gain_attn).astype(LOW)
    kv_raw = jnp.einsum("rtd,de->ret", normed_low, wkv, preferred_element_type=jnp.float32)
    k_raw = kv_raw[:, :kv_width].reshape(row_count, KV, HD, piece_len)
    v_raw = kv_raw[:, kv_width:]
    k_unit, k_inverse = normalize(k_raw, 2)
    k_low = rotate(k_unit * k_gain_h, cos_h, sin_h).astype(LOW).reshape(row_count, kv_width, piece_len)
    own_kv = jnp.concatenate([k_low, v_raw.astype(LOW)], axis=1)
    own_kv, normed_low = close_slot([gather_c[0]], own_kv, normed_low)
    row_pieces = Pieces(own_kv, devices, shards)
    (normed_low,) = open_slot([row_pieces, gather_b, gather_c[1]], normed_low)
    q_raw = jnp.einsum("rtd,de->ret", normed_low, wq, preferred_element_type=jnp.float32).reshape(
        row_count, HEADS, HD, piece_len
    )
    q_unit, q_inverse = normalize(q_raw, 2)
    q_low = (
        rotate(q_unit * q_gain_h, cos_h, sin_h).astype(LOW) * jnp.array(scale_factor, LOW)
    ).reshape(row_count, q_width, piece_len)
    (q_low,) = close_slot([row_pieces, gather_b, gather_c[1]], q_low)
    (q_low,) = open_slot([row_pieces, gather_b, *gather_c], q_low)
    (q_low,) = close_slot([row_pieces], q_low)
    pieces, piece_at = row_pieces.whole()
    info = jnp.concatenate([start.reshape(1), piece_at * piece_len, row_valid]).astype(jnp.int32)
    o_heads, att_low, sums = attention(info, q_low, pieces, 0, KV)
    o_heads, att_low, sums = close_slot([gather_b, *gather_c], o_heads, att_low, sums)
    (att_low,) = open_slot([gather_b, *gather_c], att_low)
    (att_low,) = close_slot([gather_b], att_low)
    (wout,) = gather_b.whole()
    x_mid = x_float + jnp.einsum("rct,dc->rtd", att_low, wout, preferred_element_type=jnp.float32)
    normed_two, inverse_two = normalize(x_mid)
    ffn_in = (normed_two * gain_ffn).astype(LOW)
    grad_out = cotangent.astype(jnp.float32) * live_mask[..., None]
    grad_low = grad_out.astype(LOW)

    def feed_forward(ffn_in, grad_low, wgu, wdown):
        both = jnp.einsum("rtd,df->rtf", ffn_in, wgu, preferred_element_type=jnp.float32)
        gate_proj, up_proj = both[..., :units], both[..., units:]
        gate_sig = jax.nn.sigmoid(gate_proj)
        silu_gate = gate_proj * gate_sig
        activated = (silu_gate * up_proj).astype(LOW)
        grad_down = jnp.einsum("rtd,rtf->df", grad_low, activated, preferred_element_type=jnp.float32)
        grad_act = jnp.einsum("rtd,df->rtf", grad_low, wdown, preferred_element_type=jnp.float32)
        grad_gate = (grad_act * up_proj * gate_sig * (1.0 + gate_proj * (1.0 - gate_sig))).astype(LOW)
        grad_up = (grad_act * silu_gate).astype(LOW)
        grad_both = jnp.concatenate([grad_gate, grad_up], axis=2)
        grad_wgu = jnp.einsum("rtd,rtf->df", ffn_in, grad_both, preferred_element_type=jnp.float32)
        return activated, grad_both, [grad_wgu.astype(LOW), grad_down.astype(LOW)]

    ffn_in, x_mid = close_slot(gather_c, ffn_in, x_mid)
    (ffn_in,) = open_slot([gather_c[1]], ffn_in)
    wgu_one, wdown_one = gather_c[0].whole()
    act_one, both_one, grads = feed_forward(ffn_in, grad_low, wgu_one, wdown_one)
    red_one = Reduce(grads, me, devices)
    red_one.prepare()
    ffn_in, red_one.outgoing, act_one, both_one = close_slot(
        [gather_c[1]], ffn_in, red_one.outgoing, act_one, both_one
    )
    (ffn_in,) = open_slot([gather_c[1]], ffn_in)
    (ffn_in,) = close_slot([gather_c[1]], ffn_in)
    (ffn_in,) = open_slot([red_one], ffn_in, ready=[red_one])
    wgu_two, wdown_two = gather_c[1].whole()
    act_two, both_two, grads = feed_forward(ffn_in, grad_low, wgu_two, wdown_two)
    red_two = Reduce(grads, me, devices)
    red_two.prepare()
    ffn_in, red_two.outgoing, act_two, both_two = close_slot(
        [red_one], ffn_in, red_two.outgoing, act_two, both_two
    )
    both_two, act_two = open_slot([red_one], both_two, act_two)
    grad_ffn_in = jnp.einsum(
        "rtf,df->rtd", both_one, wgu_one, preferred_element_type=jnp.float32
    ) + jnp.einsum("rtf,df->rtd", both_two, wgu_two, preferred_element_type=jnp.float32)
    grad_mid = grad_out + norm_back(x_mid, inverse_two, grad_ffn_in * gain_ffn)
    mid_low = grad_mid.astype(LOW)
    grad_wout = jnp.einsum("rtd,rct->dc", mid_low, att_low, preferred_element_type=jnp.float32)
    grad_att = jnp.einsum("rtd,dc->rct", mid_low, wout, preferred_element_type=jnp.float32)
    red_out = Reduce([grad_wout.astype(LOW)], me, devices, True)
    red_out.prepare()
    grad_att, red_out.outgoing = close_slot([red_one], grad_att, red_out.outgoing)
    grad_att, act_two = open_slot([red_one, red_two], grad_att, act_two, ready=[red_two])

    q_gain_c, k_gain_c = q_gain[:, None], k_gain[:, None]
    q_raw_flat = q_raw.reshape(row_count, q_width, piece_len)
    k_raw_flat = k_raw.reshape(row_count, kv_width, piece_len)

    def back(group, grad_att, carried=()):
        return attention_back(
            info, q_low, pieces, o_heads, sums, grad_att, q_raw_flat, q_gain_c, cos_t, sin_t, group, carried
        )

    output = (
        x_mid
        + jnp.einsum("rtf,df->rtd", act_one, wdown_one, preferred_element_type=jnp.float32)
        + jnp.einsum("rtf,df->rtd", act_two, wdown_two, preferred_element_type=jnp.float32)
    ).astype(LOW)
    gain_parts = []

    def more(group, grad_att, carried=()):
        *carried, gain_part = back(group, grad_att, carried)
        gain_parts.append(gain_part)
        return tuple(carried)

    carried = more(0, grad_att)
    carried, grad_att, output = close_slot([red_one, red_two], carried, grad_att, output)
    (grad_att,) = open_slot([red_one, red_two], grad_att)
    carried = more(1, grad_att, carried)
    carried, grad_att = close_slot([red_one, red_two], carried, grad_att)
    red_one.prepare()
    (grad_att,) = open_slot([red_two, red_out], grad_att, ready=[red_out])
    carried = more(2, grad_att, carried)
    carried, grad_att = close_slot([red_two, red_out], carried, grad_att)
    (grad_att,) = open_slot([red_two, red_out], grad_att)
    carried = more(3, grad_att, carried)
    grad_q_low, grad_pieces = close_slot([red_two, red_out], carried)[0]
    red_two.prepare()
    kv_back = PiecesBack(grad_pieces, devices, shards)
    (grad_q_low,) = open_slot([kv_back, red_out], grad_q_low)
    (grad_q_low,) = close_slot([kv_back], grad_q_low)
    (grad_q_low,) = open_slot([kv_back], grad_q_low)
    grad_wq = jnp.einsum("rtd,ret->de", normed_low, grad_q_low, preferred_element_type=jnp.float32)
    red_q = Reduce([grad_wq.astype(LOW)], me, devices)
    red_q.prepare()
    red_q.outgoing, grad_q_low = close_slot([kv_back, red_out], red_q.outgoing, grad_q_low)
    (grad_q_low,) = open_slot([kv_back, red_q, red_out], grad_q_low, ready=[red_q])
    grad_normed_q = jnp.einsum("ret,de->rtd", grad_q_low, wq, preferred_element_type=jnp.float32)
    (grad_normed_q,) = close_slot([kv_back, red_q, red_out], grad_normed_q)
    kv_back.prepare()
    grad_kv_low, k_gain_part = finish_keys(*kv_back.shares, k_raw_flat, k_gain_c, cos_t, sin_t)
    shared = Sum(
        jnp.concatenate([jnp.sum(sum(gain_parts), axis=(0, 2)), jnp.sum(k_gain_part, axis=(0, 2))])[None],
        devices,
    )
    (grad_kv_low,) = open_slot([red_q, shared, red_out], grad_kv_low)
    grad_wkv = jnp.einsum("rtd,ret->de", normed_low, grad_kv_low, preferred_element_type=jnp.float32)
    red_kv = Reduce([grad_wkv.astype(LOW)], me, devices)
    red_kv.prepare()
    red_kv.outgoing, grad_kv_low = close_slot([red_q, red_out, shared], red_kv.outgoing, grad_kv_low)
    red_out.prepare()
    (grad_kv_low,) = open_slot([red_q, red_kv, shared], grad_kv_low, ready=[red_kv])
    grad_normed = grad_normed_q + jnp.einsum(
        "ret,de->rtd", grad_kv_low, wkv, preferred_element_type=jnp.float32
    )
    input_grad = grad_mid + norm_back(x_float, inverse_one, grad_normed * gain_attn)
    (input_grad,) = close_slot([red_q, red_kv, shared], input_grad)
    open_slot([red_q, red_kv, shared])
    close_slot([red_q, red_kv, shared])
    red_q.prepare()
    open_slot([red_kv, shared])
    close_slot([red_kv, shared])
    open_slot([red_kv, shared])
    close_slot([red_kv, shared])
    red_kv.prepare()
    shared.prepare()
    shared = shared.values
    three, four = red_q.total, red_kv.total
    summed = red_one.total, red_two.total
    summed_wgate, summed_wup, summed_down = (
        jnp.concatenate([one[:, at * units : (at + 1) * units] for one in summed], axis=1) for at in range(3)
    )
    summed_down, summed_wout = summed_down.T, red_out.total.T
    summed_wqkv = jnp.concatenate([three, four], axis=1)
    grad_gain_one = jnp.sum(summed_wqkv * w_qkv_low, axis=1) / attn_gain.astype(LOW)
    grad_gain_two = jnp.sum(summed_wgate * w_gate_low + summed_wup * w_up_low, axis=1) / ffn_gain.astype(LOW)
    return (
        output,
        input_grad,
        grad_gain_one,
        summed_wqkv,
        shared[0, :HD],
        shared[0, HD:],
        summed_wout,
        grad_gain_two,
        summed_wgate,
        summed_wup,
        summed_down,
    )


def solution(mesh):
    in_specs = (
        P("dp", "shard", None),
        P("dp", "shard", None),
        P(),
        P("dp"),
        P(("dp", "shard")),
        P(("dp", "shard"), None),
        P(),
        P(),
        P(None, ("dp", "shard")),
        P(("dp", "shard")),
        P(("dp", "shard"), None),
        P(("dp", "shard"), None),
        P(None, ("dp", "shard")),
    )
    out_specs = (
        P("dp", "shard", None),
        P("dp", "shard", None),
        P(("dp", "shard")),
        P(("dp", "shard"), None),
        P(),
        P(),
        P(None, ("dp", "shard")),
        P(("dp", "shard")),
        P(("dp", "shard"), None),
        P(("dp", "shard"), None),
        P(None, ("dp", "shard")),
    )
    return jax.shard_map(local, mesh=mesh, in_specs=in_specs, out_specs=out_specs, check_vma=False)
```

```python
import functools
import math

import jax
import jax.numpy as jnp
from jax import lax
from jax.experimental import pallas as pl
from jax.experimental.pallas import tpu as pltpu
from jax.sharding import PartitionSpec as P

HEADS = 16
KV = 4
HD = 64
GROUP = HEADS // KV
EPS = 1e-06
LOW = jnp.bfloat16
ANY = pl.BlockSpec(memory_space=pl.ANY)
VMEM = pl.BlockSpec(memory_space=pltpu.VMEM)
SMEM = pl.BlockSpec(memory_space=pltpu.SMEM)
FIRST_FIRST = (((0,), (0,)), ((), ()))
LAST_FIRST = (((1,), (0,)), ((), ()))
LAST_LAST = (((1,), (1,)), ((), ()))


def dot(left, right, dims):
    return lax.dot_general(left, right, dims, preferred_element_type=jnp.float32)


def normalize(values, axis=-1):
    inverse = lax.rsqrt(jnp.mean(values * values, axis=axis, keepdims=True) + EPS)
    return (values * inverse, inverse)


def norm_back(values, inverse, grad_normed, axis=-1):
    cubed = inverse * inverse * inverse
    return inverse * grad_normed - values * cubed * jnp.mean(
        grad_normed * values, axis=axis, keepdims=True
    )


def rotate(values, cos_t, sin_t):
    half_len = HD // 2
    turned = jnp.concatenate([-values[:, :, half_len:], values[:, :, :half_len]], axis=2)
    return values * cos_t + turned * sin_t


def rotate_back(grad_in, cos_t, sin_t):
    half_len = HD // 2
    along = grad_in * sin_t
    return grad_in * cos_t + jnp.concatenate([along[:, :, half_len:], -along[:, :, :half_len]], axis=2)


def tables(positions):
    freq = 10000.0 ** (-(2.0 * jnp.arange(HD // 2, dtype=jnp.float32)) / HD)
    angles = freq[:, None] * positions.astype(jnp.float32)[None, :]
    angles = jnp.concatenate([angles, angles], axis=0)
    return (jnp.cos(angles), jnp.sin(angles))


def swap(values, mask, devices):
    return lax.ppermute(values, ("dp", "shard"), [(i, i ^ mask) for i in range(devices)])


def place(blocks, masks, widths, me, total_rows):
    count = len(blocks)
    size = blocks[0].shape[0] // len(masks[0])
    copies = sum(len(own) for own in masks) * len(widths)

    def kernel(me_ref, *refs):
        sources, outs, sems = refs[:count], refs[count:-1], refs[-1]
        started = []
        for array, own in zip(sources, masks):
            for at, mask in enumerate(own):
                row = pl.multiple_of((me_ref[0] ^ mask) * size, size)
                column = 0
                for out, width in zip(outs, widths):
                    copy = pltpu.make_async_copy(
                        array.at[pl.ds(at * size, size), pl.ds(column, width)],
                        out.at[pl.ds(row, size)],
                        sems.at[len(started)],
                    )
                    copy.start()
                    started.append(copy)
                    column += width
        for copy in started:
            copy.wait()

    return pl.pallas_call(
        kernel,
        out_shape=[jax.ShapeDtypeStruct((total_rows, width), blocks[0].dtype) for width in widths],
        in_specs=[SMEM] + [ANY] * count,
        out_specs=[VMEM] * len(widths),
        scratch_shapes=[pltpu.SemaphoreType.DMA((copies,))],
        compiler_params=pltpu.CompilerParams(vmem_limit_bytes=24 << 20),
        cost_estimate=pl.CostEstimate(flops=0, transcendentals=0, bytes_accessed=1 << 16),
    )(me, *blocks)


def pick(arrays, orders, me, size):
    count = len(arrays)
    copies = sum(len(own) for own in orders) * count
    width = sum(array.shape[1] for array in arrays)

    def kernel(me_ref, *refs):
        sources, outs, sems = refs[:count], refs[count:-1], refs[-1]
        started = []
        for out, own in zip(outs, orders):
            for at, mask in enumerate(own):
                row = pl.multiple_of((me_ref[0] ^ mask) * size, size)
                column = 0
                for array in sources:
                    copy = pltpu.make_async_copy(
                        array.at[pl.ds(row, size)],
                        out.at[pl.ds(at * size, size), pl.ds(column, array.shape[1])],
                        sems.at[len(started)],
                    )
                    copy.start()
                    started.append(copy)
                    column += array.shape[1]
        for copy in started:
            copy.wait()

    return pl.pallas_call(
        kernel,
        out_shape=[jax.ShapeDtypeStruct((len(own) * size, width), arrays[0].dtype) for own in orders],
        in_specs=[SMEM] + [VMEM] * count,
        out_specs=[ANY] * len(orders),
        scratch_shapes=[pltpu.SemaphoreType.DMA((copies,))],
        compiler_params=pltpu.CompilerParams(vmem_limit_bytes=24 << 20),
        cost_estimate=pl.CostEstimate(flops=0, transcendentals=0, bytes_accessed=1 << 16),
    )(me, *arrays)


class Gather:
    def __init__(self, parts, me, devices, first=False, spread=False):
        self.part = jnp.concatenate(parts, axis=1)
        self.widths = [one.shape[1] for one in parts]
        self.me, self.devices, self.staged, self.first = me, devices, devices == 32, first
        self.stage, self.outgoing, self.incoming = -1 if spread else 0, (), ()
        self.spread = spread

    def prepare(self):
        stage = self.stage
        self.stage += 1
        if not self.staged:
            return
        if stage == -1:
            self.outgoing, self.masks = (self.part,), ((8,),)
        elif stage == 0 and self.spread:
            self.outgoing, self.masks = (jnp.concatenate([self.part, *self.incoming]),), ((16,),)
        elif stage == 0:
            self.outgoing, self.masks = (self.part,), ((8, 16, 24),)
        elif stage == 1:
            if self.spread:
                self.outgoing += self.incoming
            else:
                one, two, three = self.incoming
                self.outgoing = jnp.concatenate([self.part, one]), jnp.concatenate([two, three])
            self.masks = (4,), (2,)
        elif stage == 2:
            self.outgoing = tuple(
                jnp.concatenate([own, came]) for own, came in zip(self.outgoing, self.incoming)
            )
            self.masks = (2,), (4,)
        elif self.first:
            self.outgoing, self.masks = self.outgoing + self.incoming, ((1,),) * 4
        else:
            self.outgoing, self.masks = (jnp.concatenate([*self.outgoing, *self.incoming]),), ((1,),)

    def launch(self):
        if self.staged:
            self.incoming = tuple(
                swap(one, mask, self.devices) for one, own in zip(self.outgoing, self.masks) for mask in own
            )

    def whole(self):
        if not self.staged:
            whole = lax.all_gather(self.part, ("dp", "shard"), axis=0, tiled=True)
            ends = [sum(self.widths[:i]) for i in range(1, len(self.widths))]
            return jnp.split(whole, ends, axis=1)
        near, far = (0, 8, 4, 12), (16, 24, 18, 26)
        masks = [near, far, [m | 2 for m in near], [m | 4 for m in far]]
        if not self.first:
            masks = [[m for own in masks for m in own]]
        masks += [[m | 1 for m in own] for own in masks]
        blocks = self.outgoing + self.incoming
        return place(blocks, masks, self.widths, self.me, self.part.shape[0] * self.devices)


class Reduce:
    def __init__(self, grads, me, devices, spread=False):
        self.grads, self.me, self.devices, self.staged = grads, me, devices, devices == 32
        self.spread = spread
        self.size = grads[0].shape[0] // devices
        self.stage, self.outgoing, self.incoming = 0, (), ()

    def both(self, low, high):
        rows = slice(low * self.size, high * self.size)
        return self.keep[rows].astype(jnp.float32) + self.came[rows].astype(jnp.float32)

    def prepare(self):
        stage, size = self.stage, self.size
        self.stage += 1
        if not self.staged:
            if stage == 0:
                grad = jnp.concatenate([one.astype(jnp.float32) for one in self.grads], axis=1)
                self.total = lax.psum_scatter(grad, ("dp", "shard"), scatter_dimension=0, tiled=True)
            return
        incoming = [one.astype(jnp.float32) for one in self.incoming]
        if stage == 0:
            order = [2, 10, 6, 14, 20, 28, 22, 30, 0, 8, 4, 12, 16, 24, 18, 26]
            self.keep, send = pick(self.grads, [order, [m | 1 for m in order]], self.me, size)
            self.outgoing, self.masks = (send,), (1,)
        elif stage == 1:
            (self.came,) = self.incoming
            self.outgoing = self.both(0, 4).astype(LOW), self.both(4, 8).astype(LOW)
            self.masks = 2, 4
        elif stage == 2:
            near, far = self.both(8, 12) + incoming[0], self.both(12, 16) + incoming[1]
            self.outgoing = near[2 * size :].astype(LOW), far[2 * size :].astype(LOW)
            self.near, self.far = near[: 2 * size], far[: 2 * size]
            self.masks = 4, 2
        elif stage == 3 and self.spread:
            self.near = self.near + incoming[0]
            self.outgoing, self.masks = ((self.far + incoming[1]).astype(LOW),), (16,)
        elif stage == 4 and self.spread:
            near = self.near + incoming[0]
            self.own = near[:size]
            self.outgoing, self.masks = (near[size:].astype(LOW),), (8,)
        elif self.spread and stage > 4:
            self.total = self.own + incoming[0]
        elif stage == 3:
            near, far = self.near + incoming[0], self.far + incoming[1]
            self.outgoing = near[size:].astype(LOW), far[:size].astype(LOW), far[size:].astype(LOW)
            self.own, self.masks = near[:size], (8, 16, 24)
        else:
            self.total = (self.own + incoming[0]) + (incoming[1] + incoming[2])

    def launch(self):
        if self.staged:
            self.incoming = tuple(
                swap(one, mask, self.devices) for one, mask in zip(self.outgoing, self.masks)
            )


class Sum:
    def __init__(self, values, devices):
        self.values, self.devices, self.staged = values, devices, devices == 32
        self.stage, self.outgoing, self.incoming = 0, (), ()

    def prepare(self):
        stage = self.stage
        self.stage += 1
        if not self.staged:
            if stage == 0:
                self.values = lax.psum(self.values, ("dp", "shard"))
            return
        if stage:
            self.values = self.values + self.incoming[0]
        if stage < 5:
            self.outgoing, self.masks = (self.values,), ((16,), (8,), (4,), (2,), (1,))[stage]

    def launch(self):
        if self.staged:
            self.incoming = tuple(swap(self.outgoing[0], mask, self.devices) for mask in self.masks)


def open_slot(travellers, *values, ready=()):
    for one in travellers:
        if one not in ready:
            one.prepare()
    travellers = [one for one in travellers if one.staged]
    if not travellers:
        return values
    outgoing, values = lax.optimization_barrier((tuple(one.outgoing for one in travellers), values))
    for one, sent in zip(travellers, outgoing):
        one.outgoing = sent
        one.launch()
    return values


def close_slot(travellers, *values):
    travellers = [one for one in travellers if one.staged]
    if not travellers:
        return values
    incoming, values = lax.optimization_barrier((tuple(one.incoming for one in travellers), values))
    for one, came in zip(travellers, incoming):
        one.incoming = came
    return values


class Pieces:
    def __init__(self, part, devices, shards):
        self.part, self.devices, self.shards = part, devices, shards
        self.staged = devices == 32 and shards == 4
        self.stage, self.outgoing, self.incoming = 0, (), ()

    def prepare(self):
        stage = self.stage
        self.stage += 1
        if stage == 0:
            self.outgoing, self.mask = (self.part,), 2
        elif self.staged:
            self.outgoing, self.mask = (jnp.stack([self.part, *self.incoming]),), 1

    def launch(self):
        if self.staged:
            self.incoming = (swap(self.outgoing[0], self.mask, self.devices),)

    def whole(self):
        if not self.staged:
            return lax.all_gather(self.part, "shard", axis=0), jnp.arange(self.shards, dtype=jnp.int32)
        at = jnp.array([0, 2, 1, 3], jnp.int32) ^ lax.axis_index("shard")
        return jnp.concatenate([self.outgoing[0], self.incoming[0]]), at


class PiecesBack:
    def __init__(self, grad, devices, shards):
        self.grad, self.devices, self.staged = grad, devices, devices == 32 and shards == 4
        self.stage, self.outgoing, self.incoming = 0, (), ()

    def prepare(self):
        stage, grad = self.stage, self.grad
        self.stage += 1
        if not self.staged:
            if stage == 0:
                self.shares = lax.psum_scatter(grad, "shard", scatter_dimension=0)[None], ()
        elif stage == 0:
            self.outgoing, self.mask = (grad[2:].astype(LOW),), 1
        elif stage == 1:
            (self.came,) = self.incoming
            self.over = (grad[1:2] + self.came[1:].astype(jnp.float32)).astype(LOW)
            self.outgoing, self.mask = (self.over[:, :, :1],), 2
        elif stage == 2:
            (self.keys,) = self.incoming
            self.outgoing = (self.over[:, :, 1:],)
        else:
            self.shares = grad, (self.came, jnp.concatenate([self.keys, *self.incoming], axis=2))

    def launch(self):
        if self.staged:
            self.incoming = (swap(self.outgoing[0], self.mask, self.devices),)


def allowed(base, start, valid, key_axis, shape):
    key = base + lax.broadcasted_iota(jnp.int32, shape, key_axis)
    query = start + lax.broadcasted_iota(jnp.int32, shape, 1 - key_axis)
    return (key <= query) & (key < valid)


def over_pieces(info_ref, pieces, length, row, tile, before=None, after=None):
    start, valid = info_ref[0], info_ref[1 + pieces + row]
    everything = slice(0, length)
    early, late = slice(0, length // 2), slice(length // 2, length)

    def one(piece, carry):
        base = info_ref[1 + piece]
        if before is not None:
            before()
        used = (base < start + length) & (base < valid)
        full = (base + length <= start) & (base + length <= valid)
        own = base == start

        def diagonal():
            tile(piece, early, everything, (base, start, valid))
            tile(piece, late, late, (base + length // 2, start + length // 2, valid))

        pl.when(used & full)(lambda: tile(piece, everything, everything, None))
        pl.when(used & own)(diagonal)
        pl.when(used & jnp.logical_not(full | own))(
            lambda: tile(piece, everything, everything, (base, start, valid))
        )
        if after is not None:
            after(piece)
        return carry

    lax.fori_loop(0, pieces, one, 0)


def attention(info, queries, keys_values, first, groups):
    rows, _, length = queries.shape
    pieces = keys_values.shape[0]
    group_width = GROUP * HD

    def kernel(info_ref, q_ref, k_ref, v_ref, out_ref, low_ref, sums_ref, accum_ref, part_ref):
        accum_ref[...] = jnp.zeros_like(accum_ref)
        part_ref[...] = jnp.zeros_like(part_ref)

        def tile(piece, keys, rows_of, bounds):
            key_t, value_t = k_ref[piece, 0, :, keys], v_ref[piece, 0, :, keys]
            key_count, row_count = keys.stop - keys.start, rows_of.stop - rows_of.start
            if bounds is not None:
                mask = allowed(*bounds, 1, (row_count, key_count))
            for head in range(GROUP):
                own = slice(head * HD, (head + 1) * HD)
                exps = jnp.exp(dot(q_ref[0, own, rows_of], key_t, FIRST_FIRST))
                if bounds is not None:
                    exps = jnp.where(mask, exps, 0.0)
                part = exps[:, :128]
                for at in range(128, key_count, 128):
                    part = part + exps[:, at : at + 128]
                part_ref[head, rows_of] += part
                accum_ref[head, rows_of] += dot(exps.astype(LOW), value_t, LAST_LAST)

        over_pieces(info_ref, pieces, length, pl.program_id(0), tile)
        for head in range(GROUP):
            own = slice(head * HD, (head + 1) * HD)
            sums = jnp.sum(part_ref[head].T, axis=0, keepdims=True)
            sums_ref[0, 0, head : head + 1, :] = sums
            out = accum_ref[head].T / sums
            out_ref[0, own, :] = out
            low_ref[0, own, :] = out.astype(LOW)

    q_spec = pl.BlockSpec((1, group_width, length), lambda row, group, *_: (row, group + first, 0))
    o_spec = pl.BlockSpec((1, group_width, length), lambda row, group, *_: (row, group, 0))
    k_spec = pl.BlockSpec((pieces, 1, HD, length), lambda row, group, *_: (0, row, group + first, 0))
    v_spec = pl.BlockSpec(
        (pieces, 1, HD, length), lambda row, group, *_: (0, row, group + first + KV, 0)
    )
    s_spec = pl.BlockSpec((1, 1, GROUP, length), lambda row, group, *_: (row, group, 0, 0))
    work = rows * groups * GROUP * length * length * pieces
    return pl.pallas_call(
        kernel,
        out_shape=[
            jax.ShapeDtypeStruct((rows, groups * group_width, length), jnp.float32),
            jax.ShapeDtypeStruct((rows, groups * group_width, length), LOW),
            jax.ShapeDtypeStruct((rows, groups, GROUP, length), jnp.float32),
        ],
        grid_spec=pltpu.PrefetchScalarGridSpec(
            num_scalar_prefetch=1,
            grid=(rows, groups),
            in_specs=[q_spec, k_spec, v_spec],
            out_specs=[o_spec, o_spec, s_spec],
            scratch_shapes=[
                pltpu.VMEM((GROUP, length, HD), jnp.float32),
                pltpu.VMEM((GROUP, length, 128), jnp.float32),
            ],
        ),
        compiler_params=pltpu.CompilerParams(vmem_limit_bytes=16 << 20),
        cost_estimate=pl.CostEstimate(flops=work, transcendentals=0, bytes_accessed=1 << 20),
    )(info, queries, keys_values, keys_values)


def head_back(grad, raw, gain, cos_t, sin_t):
    half_len = HD // 2
    along = grad * sin_t
    grad = grad * cos_t + jnp.concatenate([along[half_len:], -along[:half_len]], axis=0)
    inverse = lax.rsqrt(jnp.mean(raw * raw, axis=0, keepdims=True) + EPS)
    products = grad * (raw * inverse)
    grad = grad * gain
    cubed = inverse * inverse * inverse
    return inverse * grad - raw * cubed * jnp.mean(grad * raw, axis=0, keepdims=True), products


def fold(values):
    total = values[:, :128]
    for at in range(128, values.shape[1], 128):
        total = total + values[:, at : at + 128]
    return total


def attention_back(
    info, queries, keys_values, out, sums, grad_out, q_raw, gain, cos_t, sin_t, group, carried
):
    rows, _, length = queries.shape
    pieces = keys_values.shape[0]
    group_width = GROUP * HD
    scale_factor = 1.0 / math.sqrt(HD)

    def kernel(
        info_ref, q_ref, k_ref, v_ref, out_ref, sums_ref, grad_ref, raw_ref, gain_ref, cos_ref, sin_ref, *refs
    ):
        refs = refs[len(carried) :]
        dq_ref, dkv_ref, gain_grad_ref = refs[:3]
        grad_low, grad_sums, q_rows, grad_rows, k_accum, v_accum, q_accum = refs[3:]
        q_accum[...] = jnp.zeros_like(q_accum)
        for head in range(GROUP):
            own = slice(head * HD, (head + 1) * HD)
            inverse = 1.0 / sums_ref[0, 0, head : head + 1, :]
            grad = grad_ref[0, own, :]
            grad_sums[head] = -jnp.sum(grad * out_ref[0, own, :], axis=0, keepdims=True) * inverse
            scaled = grad * inverse
            grad_low[own, :] = scaled.astype(LOW)
            grad_rows[head] = scaled.T.astype(LOW)
            q_rows[head] = q_ref[0, own, :].T

        def tile(piece, keys, queries_of, bounds):
            key_t, value_t = k_ref[piece, 0, :, keys], v_ref[piece, 0, :, keys]
            key_count, query_count = keys.stop - keys.start, queries_of.stop - queries_of.start
            if bounds is not None:
                mask = allowed(*bounds, 0, (key_count, query_count))
            for head in range(GROUP):
                own = slice(head * HD, (head + 1) * HD)
                exps = jnp.exp(dot(key_t, q_ref[0, own, queries_of], FIRST_FIRST))
                if bounds is not None:
                    exps = jnp.where(mask, exps, 0.0)
                grad_exps = dot(value_t, grad_low[own, queries_of], FIRST_FIRST)
                grad_scores = (exps * (grad_exps + grad_sums[head, :, queries_of])).astype(LOW)
                v_accum[keys] += dot(exps.astype(LOW), grad_rows[head, queries_of], LAST_FIRST)
                k_accum[keys] += dot(grad_scores, q_rows[head, queries_of], LAST_FIRST)
                q_accum[own, queries_of] += dot(key_t, grad_scores, LAST_FIRST)

        def before():
            k_accum[...] = jnp.zeros_like(k_accum)
            v_accum[...] = jnp.zeros_like(v_accum)

        def after(piece):
            dkv_ref[piece, 0, 0] = k_accum[...].T
            dkv_ref[piece, 0, 1] = v_accum[...].T

        over_pieces(info_ref, pieces, length, pl.program_id(0), tile, before, after)
        total = jnp.zeros((HD, 128), jnp.float32)
        for head in range(GROUP):
            own = slice(head * HD, (head + 1) * HD)
            grad, products = head_back(
                scale_factor * q_accum[own, :], raw_ref[0, own, :], gain_ref[...], cos_ref[...], sin_ref[...]
            )
            dq_ref[0, own, :] = grad.astype(LOW)
            total = total + fold(products)
        gain_grad_ref[0] = total

    q_spec = pl.BlockSpec((1, group_width, length), lambda row, *_: (row, group, 0))
    k_spec = pl.BlockSpec((pieces, 1, HD, length), lambda row, *_: (0, row, group, 0))
    v_spec = pl.BlockSpec((pieces, 1, HD, length), lambda row, *_: (0, row, group + KV, 0))
    s_spec = pl.BlockSpec((1, 1, GROUP, length), lambda row, *_: (row, group, 0, 0))
    table_spec = pl.BlockSpec((HD, length), lambda row, *_: (0, 0))
    gain_spec = pl.BlockSpec((HD, 1), lambda row, *_: (0, 0))
    dkv_spec = pl.BlockSpec((pieces, 1, 2, HD, length), lambda row, *_: (0, row, 0, group, 0))
    work = rows * GROUP * length * length * pieces
    inputs = [info, queries, keys_values, keys_values, out, sums, grad_out, q_raw, gain, cos_t, sin_t]
    return pl.pallas_call(
        kernel,
        out_shape=[
            jax.ShapeDtypeStruct(queries.shape, LOW),
            jax.ShapeDtypeStruct((pieces, rows, 2, KV * HD, length), jnp.float32),
            jax.ShapeDtypeStruct((rows, HD, 128), jnp.float32),
        ],
        grid_spec=pltpu.PrefetchScalarGridSpec(
            num_scalar_prefetch=1,
            grid=(rows,),
            in_specs=[
                q_spec, k_spec, v_spec, q_spec, s_spec, q_spec, q_spec, gain_spec, table_spec, table_spec,
                *[ANY] * len(carried),
            ],
            out_specs=[q_spec, dkv_spec, pl.BlockSpec((1, HD, 128), lambda row, *_: (row, 0, 0))],
            scratch_shapes=[
                pltpu.VMEM((group_width, length), LOW),
                pltpu.VMEM((GROUP, 1, length), jnp.float32),
                pltpu.VMEM((GROUP, length, HD), LOW),
                pltpu.VMEM((GROUP, length, HD), LOW),
                pltpu.VMEM((length, HD), jnp.float32),
                pltpu.VMEM((length, HD), jnp.float32),
                pltpu.VMEM((group_width, length), jnp.float32),
            ],
        ),
        input_output_aliases={len(inputs) + at: at for at in range(len(carried))},
        compiler_params=pltpu.CompilerParams(vmem_limit_bytes=16 << 20),
        cost_estimate=pl.CostEstimate(flops=work, transcendentals=0, bytes_accessed=1 << 20),
    )(*inputs, *carried)


def finish_keys(own, others, k_raw, gain, cos_t, sin_t):
    _, rows, _, width, length = own.shape

    def kernel(own_ref, *refs):
        shares, (raw_ref, gain_ref, cos_ref, sin_ref, out_ref, gain_grad_ref) = refs[:-6], refs[-6:]

        def share(which, rows_of):
            total = own_ref[0, 0, which, rows_of, :]
            for ref in shares:
                total = total + ref[0, 0, which, rows_of, :].astype(jnp.float32)
            return total

        total = jnp.zeros((HD, 128), jnp.float32)
        for head in range(KV):
            rows_of = slice(head * HD, (head + 1) * HD)
            grad, products = head_back(
                share(0, rows_of), raw_ref[0, rows_of, :], gain_ref[...], cos_ref[...], sin_ref[...]
            )
            out_ref[0, rows_of, :] = grad.astype(LOW)
            out_ref[0, slice(width + head * HD, width + (head + 1) * HD), :] = share(1, rows_of).astype(LOW)
            total = total + fold(products)
        gain_grad_ref[0] = total

    piece_spec = pl.BlockSpec((1, 1, 2, width, length), lambda row: (0, row, 0, 0, 0))
    table_spec = pl.BlockSpec((HD, length), lambda row: (0, 0))
    return pl.pallas_call(
        kernel,
        out_shape=[
            jax.ShapeDtypeStruct((rows, 2 * width, length), LOW),
            jax.ShapeDtypeStruct((rows, HD, 128), jnp.float32),
        ],
        grid=(rows,),
        in_specs=[
            *[piece_spec] * (1 + len(others)),
            pl.BlockSpec((1, width, length), lambda row: (row, 0, 0)),
            pl.BlockSpec((HD, 1), lambda row: (0, 0)),
            table_spec,
            table_spec,
        ],
        out_specs=[
            pl.BlockSpec((1, 2 * width, length), lambda row: (row, 0, 0)),
            pl.BlockSpec((1, HD, 128), lambda row: (row, 0, 0)),
        ],
        compiler_params=pltpu.CompilerParams(vmem_limit_bytes=16 << 20),
    )(own, *others, k_raw, gain, cos_t, sin_t)


def local(
    tokens,
    cotangent,
    lengths,
    slot_sequence,
    attn_gain,
    w_qkv,
    q_gain,
    k_gain,
    w_out,
    ffn_gain,
    w_gate,
    w_up,
    w_down,
):
    row_count, piece_len, model_width = tokens.shape
    q_width = HEADS * HD
    kv_width = KV * HD
    total_rows = lengths.shape[0]
    scale_factor = 1.0 / math.sqrt(HD)
    shards = lax.axis_size("shard")
    devices = lax.axis_size("dp") * shards
    part_len = attn_gain.shape[0]
    shard_at = lax.axis_index("shard")
    me = (lax.axis_index("dp") * shards + shard_at).astype(jnp.int32).reshape(1)
    row_valid = jnp.sum(
        jnp.where(
            slot_sequence[:, None] == jnp.arange(total_rows, dtype=jnp.int32)[None, :],
            lengths[None, :],
            0,
        ),
        axis=1,
    )
    start = (shard_at * piece_len).astype(jnp.int32)
    positions = start + jnp.arange(piece_len, dtype=jnp.int32)
    live_mask = (positions[None, :] < row_valid[:, None]).astype(jnp.float32)
    cos_t, sin_t = tables(positions)
    cos_h = cos_t[None, None]
    sin_h = sin_t[None, None]
    q_gain_h = q_gain[None, None, :, None]
    k_gain_h = k_gain[None, None, :, None]

    column = jnp.arange(128)[None, :]
    gain_columns = jnp.where(
        column == 0, attn_gain[:, None], jnp.where(column == 1, ffn_gain[:, None], 0.0)
    ).astype(LOW)
    w_qkv_low, w_gate_low, w_up_low = w_qkv.astype(LOW), w_gate.astype(LOW), w_up.astype(LOW)
    gather_a = Gather([w_qkv_low[:, :q_width], w_qkv_low[:, q_width:], gain_columns], me, devices, True)
    gather_b = Gather([w_out.astype(LOW).T], me, devices)
    w_down_low = w_down.astype(LOW).T
    units = w_down_low.shape[1] // 2
    halves = slice(0, units), slice(units, 2 * units)
    gather_c = [
        Gather(
            [jnp.concatenate([w_gate_low[:, own], w_up_low[:, own]], axis=1), w_down_low[:, own]],
            me,
            devices,
            spread=own is halves[1],
        )
        for own in halves
    ]
    (tokens,) = open_slot([gather_a], tokens)
    x_float = tokens.astype(jnp.float32)
    normed_one, inverse_one = normalize(x_float)
    (normed_one,) = close_slot([gather_a], normed_one)
    (normed_one,) = open_slot([gather_a, gather_c[0]], normed_one)
    (normed_one,) = close_slot([gather_a, gather_c[0]], normed_one)
    (normed_one,) = open_slot([gather_a, gather_b], normed_one)
    (normed_one,) = close_slot([gather_a, gather_b], normed_one)
    (normed_one,) = open_slot([gather_a, gather_c[0]], normed_one)
    (normed_one,) = close_slot([gather_a], normed_one)
    wq, wkv, gains = gather_a.whole()
    gain_attn = gains[:, 0].astype(jnp.float32)
    gain_ffn = gains[:, 1].astype(jnp.float32)
    normed_low = (normed_one * gain_attn).astype(LOW)
    kv_raw = jnp.einsum("rtd,de->ret", normed_low, wkv, preferred_element_type=jnp.float32)
    k_raw = kv_raw[:, :kv_width].reshape(row_count, KV, HD, piece_len)
    v_raw = kv_raw[:, kv_width:]
    k_unit, k_inverse = normalize(k_raw, 2)
    k_low = rotate(k_unit * k_gain_h, cos_h, sin_h).astype(LOW).reshape(row_count, kv_width, piece_len)
    own_kv = jnp.concatenate([k_low, v_raw.astype(LOW)], axis=1)
    own_kv, normed_low = close_slot([gather_c[0]], own_kv, normed_low)
    row_pieces = Pieces(own_kv, devices, shards)
    (normed_low,) = open_slot([row_pieces, gather_b, gather_c[1]], normed_low)
    q_raw = jnp.einsum("rtd,de->ret", normed_low, wq, preferred_element_type=jnp.float32).reshape(
        row_count, HEADS, HD, piece_len
    )
    q_unit, q_inverse = normalize(q_raw, 2)
    q_low = (
        rotate(q_unit * q_gain_h, cos_h, sin_h).astype(LOW) * jnp.array(scale_factor, LOW)
    ).reshape(row_count, q_width, piece_len)
    (q_low,) = close_slot([row_pieces, gather_b, gather_c[1]], q_low)
    (q_low,) = open_slot([row_pieces, gather_b, *gather_c], q_low)
    (q_low,) = close_slot([row_pieces], q_low)
    pieces, piece_at = row_pieces.whole()
    info = jnp.concatenate([start.reshape(1), piece_at * piece_len, row_valid]).astype(jnp.int32)
    o_heads, att_low, sums = attention(info, q_low, pieces, 0, KV)
    o_heads, att_low, sums = close_slot([gather_b, *gather_c], o_heads, att_low, sums)
    (att_low,) = open_slot([gather_b, *gather_c], att_low)
    (att_low,) = close_slot([gather_b], att_low)
    (wout,) = gather_b.whole()
    x_mid = x_float + jnp.einsum("rct,dc->rtd", att_low, wout, preferred_element_type=jnp.float32)
    normed_two, inverse_two = normalize(x_mid)
    ffn_in = (normed_two * gain_ffn).astype(LOW)
    grad_out = cotangent.astype(jnp.float32) * live_mask[..., None]
    grad_low = grad_out.astype(LOW)

    def feed_forward(ffn_in, grad_low, wgu, wdown):
        both = jnp.einsum("rtd,df->rtf", ffn_in, wgu, preferred_element_type=jnp.float32)
        gate_proj, up_proj = both[..., :units], both[..., units:]
        gate_sig = jax.nn.sigmoid(gate_proj)
        silu_gate = gate_proj * gate_sig
        activated = (silu_gate * up_proj).astype(LOW)
        grad_down = jnp.einsum("rtd,rtf->df", grad_low, activated, preferred_element_type=jnp.float32)
        grad_act = jnp.einsum("rtd,df->rtf", grad_low, wdown, preferred_element_type=jnp.float32)
        grad_gate = (grad_act * up_proj * gate_sig * (1.0 + gate_proj * (1.0 - gate_sig))).astype(LOW)
        grad_up = (grad_act * silu_gate).astype(LOW)
        grad_both = jnp.concatenate([grad_gate, grad_up], axis=2)
        grad_wgu = jnp.einsum("rtd,rtf->df", ffn_in, grad_both, preferred_element_type=jnp.float32)
        return activated, grad_both, [grad_wgu.astype(LOW), grad_down.astype(LOW)]

    ffn_in, x_mid = close_slot(gather_c, ffn_in, x_mid)
    (ffn_in,) = open_slot([gather_c[1]], ffn_in)
    wgu_one, wdown_one = gather_c[0].whole()
    act_one, both_one, grads = feed_forward(ffn_in, grad_low, wgu_one, wdown_one)
    red_one = Reduce(grads, me, devices)
    red_one.prepare()
    ffn_in, red_one.outgoing, act_one, both_one = close_slot(
        [gather_c[1]], ffn_in, red_one.outgoing, act_one, both_one
    )
    (ffn_in,) = open_slot([gather_c[1]], ffn_in)
    (ffn_in,) = close_slot([gather_c[1]], ffn_in)
    (ffn_in,) = open_slot([red_one], ffn_in, ready=[red_one])
    wgu_two, wdown_two = gather_c[1].whole()
    act_two, both_two, grads = feed_forward(ffn_in, grad_low, wgu_two, wdown_two)
    red_two = Reduce(grads, me, devices)
    red_two.prepare()
    ffn_in, red_two.outgoing, act_two, both_two = close_slot(
        [red_one], ffn_in, red_two.outgoing, act_two, both_two
    )
    both_two, act_two = open_slot([red_one], both_two, act_two)
    grad_ffn_in = jnp.einsum(
        "rtf,df->rtd", both_one, wgu_one, preferred_element_type=jnp.float32
    ) + jnp.einsum("rtf,df->rtd", both_two, wgu_two, preferred_element_type=jnp.float32)
    grad_mid = grad_out + norm_back(x_mid, inverse_two, grad_ffn_in * gain_ffn)
    mid_low = grad_mid.astype(LOW)
    grad_wout = jnp.einsum("rtd,rct->dc", mid_low, att_low, preferred_element_type=jnp.float32)
    grad_att = jnp.einsum("rtd,dc->rct", mid_low, wout, preferred_element_type=jnp.float32)
    red_out = Reduce([grad_wout.astype(LOW)], me, devices, True)
    red_out.prepare()
    grad_att, red_out.outgoing = close_slot([red_one], grad_att, red_out.outgoing)
    grad_att, act_two = open_slot([red_one, red_two], grad_att, act_two, ready=[red_two])

    q_gain_c, k_gain_c = q_gain[:, None], k_gain[:, None]
    q_raw_flat = q_raw.reshape(row_count, q_width, piece_len)
    k_raw_flat = k_raw.reshape(row_count, kv_width, piece_len)

    def back(group, grad_att, carried=()):
        return attention_back(
            info, q_low, pieces, o_heads, sums, grad_att, q_raw_flat, q_gain_c, cos_t, sin_t, group, carried
        )

    output = (
        x_mid
        + jnp.einsum("rtf,df->rtd", act_one, wdown_one, preferred_element_type=jnp.float32)
        + jnp.einsum("rtf,df->rtd", act_two, wdown_two, preferred_element_type=jnp.float32)
    ).astype(LOW)
    gain_parts = []

    def more(group, grad_att, carried=()):
        *carried, gain_part = back(group, grad_att, carried)
        gain_parts.append(gain_part)
        return tuple(carried)

    carried = more(0, grad_att)
    carried, grad_att, output = close_slot([red_one, red_two], carried, grad_att, output)
    (grad_att,) = open_slot([red_one, red_two], grad_att)
    carried = more(1, grad_att, carried)
    carried, grad_att = close_slot([red_one, red_two], carried, grad_att)
    (grad_att,) = open_slot([red_two, red_out], grad_att, ready=[red_out])
    carried = more(2, grad_att, carried)
    carried, grad_att = close_slot([red_two, red_out], carried, grad_att)
    (grad_att,) = open_slot([red_two, red_out], grad_att)
    carried = more(3, grad_att, carried)
    grad_q_low, grad_pieces = close_slot([red_two, red_out], carried)[0]
    kv_back = PiecesBack(grad_pieces, devices, shards)
    (grad_q_low,) = open_slot([kv_back, red_out], grad_q_low)
    (grad_q_low,) = close_slot([kv_back], grad_q_low)
    (grad_q_low,) = open_slot([kv_back], grad_q_low)
    grad_wq = jnp.einsum("rtd,ret->de", normed_low, grad_q_low, preferred_element_type=jnp.float32)
    red_q = Reduce([grad_wq.astype(LOW)], me, devices)
    red_q.prepare()
    red_q.outgoing, grad_q_low = close_slot([kv_back, red_out], red_q.outgoing, grad_q_low)
    (grad_q_low,) = open_slot([kv_back, red_q, red_out], grad_q_low, ready=[red_q])
    grad_normed_q = jnp.einsum("ret,de->rtd", grad_q_low, wq, preferred_element_type=jnp.float32)
    (grad_normed_q,) = close_slot([kv_back, red_q], grad_normed_q)
    kv_back.prepare()
    grad_kv_low, k_gain_part = finish_keys(*kv_back.shares, k_raw_flat, k_gain_c, cos_t, sin_t)
    shared = Sum(
        jnp.concatenate([jnp.sum(sum(gain_parts), axis=(0, 2)), jnp.sum(k_gain_part, axis=(0, 2))])[None],
        devices,
    )
    (grad_kv_low,) = open_slot([red_q, shared], grad_kv_low)
    grad_wkv = jnp.einsum("rtd,ret->de", normed_low, grad_kv_low, preferred_element_type=jnp.float32)
    red_kv = Reduce([grad_wkv.astype(LOW)], me, devices)
    red_kv.prepare()
    red_kv.outgoing, grad_kv_low = close_slot([red_q, red_out, shared], red_kv.outgoing, grad_kv_low)
    (grad_kv_low,) = open_slot([red_q, red_kv, shared, red_out], grad_kv_low, ready=[red_kv])
    grad_normed = grad_normed_q + jnp.einsum(
        "ret,de->rtd", grad_kv_low, wkv, preferred_element_type=jnp.float32
    )
    input_grad = grad_mid + norm_back(x_float, inverse_one, grad_normed * gain_attn)
    (input_grad,) = close_slot([red_q, red_kv, shared, red_out, red_one, red_two], input_grad)
    for one in (red_out, red_one, red_two):
        one.prepare()
    open_slot([red_q, red_kv, shared])
    close_slot([red_q, red_kv, shared])
    red_q.prepare()
    open_slot([red_kv, shared])
    close_slot([red_kv, shared])
    open_slot([red_kv, shared])
    close_slot([red_kv, shared])
    red_kv.prepare()
    shared.prepare()
    shared = shared.values
    three, four = red_q.total, red_kv.total
    summed = red_one.total, red_two.total
    summed_wgate, summed_wup, summed_down = (
        jnp.concatenate([one[:, at * units : (at + 1) * units] for one in summed], axis=1) for at in range(3)
    )
    summed_down, summed_wout = summed_down.T, red_out.total.T
    summed_wqkv = jnp.concatenate([three, four], axis=1)
    grad_gain_one = jnp.sum(summed_wqkv * w_qkv_low, axis=1) / attn_gain.astype(LOW)
    grad_gain_two = jnp.sum(summed_wgate * w_gate_low + summed_wup * w_up_low, axis=1) / ffn_gain.astype(LOW)
    return (
        output,
        input_grad,
        grad_gain_one,
        summed_wqkv,
        shared[0, :HD],
        shared[0, HD:],
        summed_wout,
        grad_gain_two,
        summed_wgate,
        summed_wup,
        summed_down,
    )


def solution(mesh):
    in_specs = (
        P("dp", "shard", None),
        P("dp", "shard", None),
        P(),
        P("dp"),
        P(("dp", "shard")),
        P(("dp", "shard"), None),
        P(),
        P(),
        P(None, ("dp", "shard")),
        P(("dp", "shard")),
        P(("dp", "shard"), None),
        P(("dp", "shard"), None),
        P(None, ("dp", "shard")),
    )
    out_specs = (
        P("dp", "shard", None),
        P("dp", "shard", None),
        P(("dp", "shard")),
        P(("dp", "shard"), None),
        P(),
        P(),
        P(None, ("dp", "shard")),
        P(("dp", "shard")),
        P(("dp", "shard"), None),
        P(("dp", "shard"), None),
        P(None, ("dp", "shard")),
    )
    return jax.shard_map(local, mesh=mesh, in_specs=in_specs, out_specs=out_specs, check_vma=False)
```

```python
import functools
import math

import jax
import jax.numpy as jnp
from jax import lax
from jax.experimental import pallas as pl
from jax.experimental.pallas import tpu as pltpu
from jax.sharding import PartitionSpec as P

HEADS = 16
KV = 4
HD = 64
GROUP = HEADS // KV
EPS = 1e-06
LOW = jnp.bfloat16
ANY = pl.BlockSpec(memory_space=pl.ANY)
VMEM = pl.BlockSpec(memory_space=pltpu.VMEM)
SMEM = pl.BlockSpec(memory_space=pltpu.SMEM)
FIRST_FIRST = (((0,), (0,)), ((), ()))
LAST_FIRST = (((1,), (0,)), ((), ()))
LAST_LAST = (((1,), (1,)), ((), ()))


def dot(left, right, dims):
    return lax.dot_general(left, right, dims, preferred_element_type=jnp.float32)


def normalize(values, axis=-1):
    inverse = lax.rsqrt(jnp.mean(values * values, axis=axis, keepdims=True) + EPS)
    return (values * inverse, inverse)


def norm_back(values, inverse, grad_normed, axis=-1):
    cubed = inverse * inverse * inverse
    return inverse * grad_normed - values * cubed * jnp.mean(
        grad_normed * values, axis=axis, keepdims=True
    )


def rotate(values, cos_t, sin_t):
    half_len = HD // 2
    turned = jnp.concatenate([-values[:, :, half_len:], values[:, :, :half_len]], axis=2)
    return values * cos_t + turned * sin_t


def rotate_back(grad_in, cos_t, sin_t):
    half_len = HD // 2
    along = grad_in * sin_t
    return grad_in * cos_t + jnp.concatenate([along[:, :, half_len:], -along[:, :, :half_len]], axis=2)


def tables(positions):
    freq = 10000.0 ** (-(2.0 * jnp.arange(HD // 2, dtype=jnp.float32)) / HD)
    angles = freq[:, None] * positions.astype(jnp.float32)[None, :]
    angles = jnp.concatenate([angles, angles], axis=0)
    return (jnp.cos(angles), jnp.sin(angles))


def swap(values, mask, devices):
    return lax.ppermute(values, ("dp", "shard"), [(i, i ^ mask) for i in range(devices)])


def place(blocks, masks, widths, me, total_rows):
    count = len(blocks)
    size = blocks[0].shape[0] // len(masks[0])
    copies = sum(len(own) for own in masks) * len(widths)

    def kernel(me_ref, *refs):
        sources, outs, sems = refs[:count], refs[count:-1], refs[-1]
        started = []
        for array, own in zip(sources, masks):
            for at, mask in enumerate(own):
                row = pl.multiple_of((me_ref[0] ^ mask) * size, size)
                column = 0
                for out, width in zip(outs, widths):
                    copy = pltpu.make_async_copy(
                        array.at[pl.ds(at * size, size), pl.ds(column, width)],
                        out.at[pl.ds(row, size)],
                        sems.at[len(started)],
                    )
                    copy.start()
                    started.append(copy)
                    column += width
        for copy in started:
            copy.wait()

    return pl.pallas_call(
        kernel,
        out_shape=[jax.ShapeDtypeStruct((total_rows, width), blocks[0].dtype) for width in widths],
        in_specs=[SMEM] + [ANY] * count,
        out_specs=[VMEM] * len(widths),
        scratch_shapes=[pltpu.SemaphoreType.DMA((copies,))],
        compiler_params=pltpu.CompilerParams(vmem_limit_bytes=24 << 20),
        cost_estimate=pl.CostEstimate(flops=0, transcendentals=0, bytes_accessed=1 << 16),
    )(me, *blocks)


def pick(arrays, orders, me, size):
    count = len(arrays)
    copies = sum(len(own) for own in orders) * count
    width = sum(array.shape[1] for array in arrays)

    def kernel(me_ref, *refs):
        sources, outs, sems = refs[:count], refs[count:-1], refs[-1]
        started = []
        for out, own in zip(outs, orders):
            for at, mask in enumerate(own):
                row = pl.multiple_of((me_ref[0] ^ mask) * size, size)
                column = 0
                for array in sources:
                    copy = pltpu.make_async_copy(
                        array.at[pl.ds(row, size)],
                        out.at[pl.ds(at * size, size), pl.ds(column, array.shape[1])],
                        sems.at[len(started)],
                    )
                    copy.start()
                    started.append(copy)
                    column += array.shape[1]
        for copy in started:
            copy.wait()

    return pl.pallas_call(
        kernel,
        out_shape=[jax.ShapeDtypeStruct((len(own) * size, width), arrays[0].dtype) for own in orders],
        in_specs=[SMEM] + [VMEM] * count,
        out_specs=[ANY] * len(orders),
        scratch_shapes=[pltpu.SemaphoreType.DMA((copies,))],
        compiler_params=pltpu.CompilerParams(vmem_limit_bytes=24 << 20),
        cost_estimate=pl.CostEstimate(flops=0, transcendentals=0, bytes_accessed=1 << 16),
    )(me, *arrays)


class Gather:
    def __init__(self, parts, me, devices, first=False, spread=False):
        self.part = jnp.concatenate(parts, axis=1)
        self.widths = [one.shape[1] for one in parts]
        self.me, self.devices, self.staged, self.first = me, devices, devices == 32, first
        self.stage, self.outgoing, self.incoming = -1 if spread else 0, (), ()
        self.spread = spread

    def prepare(self):
        stage = self.stage
        self.stage += 1
        if not self.staged:
            return
        if stage == -1:
            self.outgoing, self.masks = (self.part,), ((8,),)
        elif stage == 0 and self.spread:
            self.outgoing, self.masks = (jnp.concatenate([self.part, *self.incoming]),), ((16,),)
        elif stage == 0:
            self.outgoing, self.masks = (self.part,), ((8, 16, 24),)
        elif stage == 1:
            if self.spread:
                self.outgoing += self.incoming
            else:
                one, two, three = self.incoming
                self.outgoing = jnp.concatenate([self.part, one]), jnp.concatenate([two, three])
            self.masks = (4,), (2,)
        elif stage == 2:
            self.outgoing = tuple(
                jnp.concatenate([own, came]) for own, came in zip(self.outgoing, self.incoming)
            )
            self.masks = (2,), (4,)
        elif self.first:
            self.outgoing, self.masks = self.outgoing + self.incoming, ((1,),) * 4
        else:
            self.outgoing, self.masks = (jnp.concatenate([*self.outgoing, *self.incoming]),), ((1,),)

    def launch(self):
        if self.staged:
            self.incoming = tuple(
                swap(one, mask, self.devices) for one, own in zip(self.outgoing, self.masks) for mask in own
            )

    def whole(self):
        if not self.staged:
            whole = lax.all_gather(self.part, ("dp", "shard"), axis=0, tiled=True)
            ends = [sum(self.widths[:i]) for i in range(1, len(self.widths))]
            return jnp.split(whole, ends, axis=1)
        near, far = (0, 8, 4, 12), (16, 24, 18, 26)
        masks = [near, far, [m | 2 for m in near], [m | 4 for m in far]]
        if not self.first:
            masks = [[m for own in masks for m in own]]
        masks += [[m | 1 for m in own] for own in masks]
        blocks = self.outgoing + self.incoming
        return place(blocks, masks, self.widths, self.me, self.part.shape[0] * self.devices)


class Reduce:
    def __init__(self, grads, me, devices, spread=False):
        self.grads, self.me, self.devices, self.staged = grads, me, devices, devices == 32
        self.spread = spread
        self.size = grads[0].shape[0] // devices
        self.stage, self.outgoing, self.incoming = 0, (), ()

    def both(self, low, high):
        rows = slice(low * self.size, high * self.size)
        return self.keep[rows].astype(jnp.float32) + self.came[rows].astype(jnp.float32)

    def prepare(self):
        stage, size = self.stage, self.size
        self.stage += 1
        if not self.staged:
            if stage == 0:
                grad = jnp.concatenate([one.astype(jnp.float32) for one in self.grads], axis=1)
                self.total = lax.psum_scatter(grad, ("dp", "shard"), scatter_dimension=0, tiled=True)
            return
        incoming = [one.astype(jnp.float32) for one in self.incoming]
        if stage == 0:
            order = [2, 10, 6, 14, 20, 28, 22, 30, 0, 8, 4, 12, 16, 24, 18, 26]
            self.keep, send = pick(self.grads, [order, [m | 1 for m in order]], self.me, size)
            self.outgoing, self.masks = (send,), (1,)
        elif stage == 1:
            (self.came,) = self.incoming
            self.outgoing = self.both(0, 4).astype(LOW), self.both(4, 8).astype(LOW)
            self.masks = 2, 4
        elif stage == 2:
            near, far = self.both(8, 12) + incoming[0], self.both(12, 16) + incoming[1]
            self.outgoing = near[2 * size :].astype(LOW), far[2 * size :].astype(LOW)
            self.near, self.far = near[: 2 * size], far[: 2 * size]
            self.masks = 4, 2
        elif stage == 3 and self.spread:
            self.near = self.near + incoming[0]
            self.outgoing, self.masks = ((self.far + incoming[1]).astype(LOW),), (16,)
        elif stage == 4 and self.spread:
            near = self.near + incoming[0]
            self.own = near[:size]
            self.outgoing, self.masks = (near[size:].astype(LOW),), (8,)
        elif self.spread and stage > 4:
            self.total = self.own + incoming[0]
        elif stage == 3:
            near, far = self.near + incoming[0], self.far + incoming[1]
            self.outgoing = near[size:].astype(LOW), far[:size].astype(LOW), far[size:].astype(LOW)
            self.own, self.masks = near[:size], (8, 16, 24)
        else:
            self.total = (self.own + incoming[0]) + (incoming[1] + incoming[2])

    def launch(self):
        if self.staged:
            self.incoming = tuple(
                swap(one, mask, self.devices) for one, mask in zip(self.outgoing, self.masks)
            )


class Sum:
    def __init__(self, values, devices):
        self.values, self.devices, self.staged = values, devices, devices == 32
        self.stage, self.outgoing, self.incoming = 0, (), ()

    def prepare(self):
        stage = self.stage
        self.stage += 1
        if not self.staged:
            if stage == 0:
                self.values = lax.psum(self.values, ("dp", "shard"))
            return
        if len(self.incoming) == 3:
            one, two, three = self.incoming
            self.values = (self.values + one) + (two + three)
        elif stage:
            self.values = self.values + self.incoming[0]
        if stage < 4:
            self.outgoing, self.masks = (self.values,), ((16,), (8,), (4, 2, 6), (1,))[stage]

    def launch(self):
        if self.staged:
            self.incoming = tuple(swap(self.outgoing[0], mask, self.devices) for mask in self.masks)


def open_slot(travellers, *values, ready=()):
    for one in travellers:
        if one not in ready:
            one.prepare()
    travellers = [one for one in travellers if one.staged]
    if not travellers:
        return values
    outgoing, values = lax.optimization_barrier((tuple(one.outgoing for one in travellers), values))
    for one, sent in zip(travellers, outgoing):
        one.outgoing = sent
        one.launch()
    return values


def close_slot(travellers, *values):
    travellers = [one for one in travellers if one.staged]
    if not travellers:
        return values
    incoming, values = lax.optimization_barrier((tuple(one.incoming for one in travellers), values))
    for one, came in zip(travellers, incoming):
        one.incoming = came
    return values


class Pieces:
    def __init__(self, part, devices, shards):
        self.part, self.devices, self.shards = part, devices, shards
        self.staged = devices == 32 and shards == 4
        self.stage, self.outgoing, self.incoming = 0, (), ()

    def prepare(self):
        stage = self.stage
        self.stage += 1
        if stage == 0:
            self.outgoing, self.mask = (self.part,), 2
        elif self.staged:
            self.outgoing, self.mask = (jnp.stack([self.part, *self.incoming]),), 1

    def launch(self):
        if self.staged:
            self.incoming = (swap(self.outgoing[0], self.mask, self.devices),)

    def whole(self):
        if not self.staged:
            return lax.all_gather(self.part, "shard", axis=0), jnp.arange(self.shards, dtype=jnp.int32)
        at = jnp.array([0, 2, 1, 3], jnp.int32) ^ lax.axis_index("shard")
        return jnp.concatenate([self.outgoing[0], self.incoming[0]]), at


class PiecesBack:
    def __init__(self, grad, devices, shards):
        self.grad, self.devices, self.staged = grad, devices, devices == 32 and shards == 4
        self.stage, self.outgoing, self.incoming = 0, (), ()

    def prepare(self):
        stage, grad = self.stage, self.grad
        self.stage += 1
        if not self.staged:
            if stage == 0:
                self.shares = lax.psum_scatter(grad, "shard", scatter_dimension=0)[None], ()
        elif stage == 0:
            self.outgoing, self.mask = (grad[2:].astype(LOW),), 1
        elif stage == 1:
            (self.came,) = self.incoming
            self.over = (grad[1:2] + self.came[1:].astype(jnp.float32)).astype(LOW)
            self.outgoing, self.mask = (self.over[:, :, :1],), 2
        elif stage == 2:
            (self.keys,) = self.incoming
            self.outgoing = (self.over[:, :, 1:],)
        else:
            self.shares = grad, (self.came, jnp.concatenate([self.keys, *self.incoming], axis=2))

    def launch(self):
        if self.staged:
            self.incoming = (swap(self.outgoing[0], self.mask, self.devices),)


def allowed(base, start, valid, key_axis, shape):
    key = base + lax.broadcasted_iota(jnp.int32, shape, key_axis)
    query = start + lax.broadcasted_iota(jnp.int32, shape, 1 - key_axis)
    return (key <= query) & (key < valid)


def over_pieces(info_ref, pieces, length, row, tile, before=None, after=None):
    start, valid = info_ref[0], info_ref[1 + pieces + row]
    everything = slice(0, length)
    early, late = slice(0, length // 2), slice(length // 2, length)

    def one(piece, carry):
        base = info_ref[1 + piece]
        if before is not None:
            before()
        used = (base < start + length) & (base < valid)
        full = (base + length <= start) & (base + length <= valid)
        own = base == start

        def diagonal():
            tile(piece, early, everything, (base, start, valid))
            tile(piece, late, late, (base + length // 2, start + length // 2, valid))

        pl.when(used & full)(lambda: tile(piece, everything, everything, None))
        pl.when(used & own)(diagonal)
        pl.when(used & jnp.logical_not(full | own))(
            lambda: tile(piece, everything, everything, (base, start, valid))
        )
        if after is not None:
            after(piece)
        return carry

    lax.fori_loop(0, pieces, one, 0)


def attention(info, queries, keys_values, first, groups):
    rows, _, length = queries.shape
    pieces = keys_values.shape[0]
    group_width = GROUP * HD

    def kernel(info_ref, q_ref, k_ref, v_ref, out_ref, low_ref, sums_ref, accum_ref, part_ref):
        accum_ref[...] = jnp.zeros_like(accum_ref)
        part_ref[...] = jnp.zeros_like(part_ref)

        def tile(piece, keys, rows_of, bounds):
            key_t, value_t = k_ref[piece, 0, :, keys], v_ref[piece, 0, :, keys]
            key_count, row_count = keys.stop - keys.start, rows_of.stop - rows_of.start
            if bounds is not None:
                mask = allowed(*bounds, 1, (row_count, key_count))
            for head in range(GROUP):
                own = slice(head * HD, (head + 1) * HD)
                exps = jnp.exp(dot(q_ref[0, own, rows_of], key_t, FIRST_FIRST))
                if bounds is not None:
                    exps = jnp.where(mask, exps, 0.0)
                part = exps[:, :128]
                for at in range(128, key_count, 128):
                    part = part + exps[:, at : at + 128]
                part_ref[head, rows_of] += part
                accum_ref[head, rows_of] += dot(exps.astype(LOW), value_t, LAST_LAST)

        over_pieces(info_ref, pieces, length, pl.program_id(0), tile)
        for head in range(GROUP):
            own = slice(head * HD, (head + 1) * HD)
            sums = jnp.sum(part_ref[head].T, axis=0, keepdims=True)
            sums_ref[0, 0, head : head + 1, :] = sums
            out = accum_ref[head].T / sums
            out_ref[0, own, :] = out
            low_ref[0, own, :] = out.astype(LOW)

    q_spec = pl.BlockSpec((1, group_width, length), lambda row, group, *_: (row, group + first, 0))
    o_spec = pl.BlockSpec((1, group_width, length), lambda row, group, *_: (row, group, 0))
    k_spec = pl.BlockSpec((pieces, 1, HD, length), lambda row, group, *_: (0, row, group + first, 0))
    v_spec = pl.BlockSpec(
        (pieces, 1, HD, length), lambda row, group, *_: (0, row, group + first + KV, 0)
    )
    s_spec = pl.BlockSpec((1, 1, GROUP, length), lambda row, group, *_: (row, group, 0, 0))
    work = rows * groups * GROUP * length * length * pieces
    return pl.pallas_call(
        kernel,
        out_shape=[
            jax.ShapeDtypeStruct((rows, groups * group_width, length), jnp.float32),
            jax.ShapeDtypeStruct((rows, groups * group_width, length), LOW),
            jax.ShapeDtypeStruct((rows, groups, GROUP, length), jnp.float32),
        ],
        grid_spec=pltpu.PrefetchScalarGridSpec(
            num_scalar_prefetch=1,
            grid=(rows, groups),
            in_specs=[q_spec, k_spec, v_spec],
            out_specs=[o_spec, o_spec, s_spec],
            scratch_shapes=[
                pltpu.VMEM((GROUP, length, HD), jnp.float32),
                pltpu.VMEM((GROUP, length, 128), jnp.float32),
            ],
        ),
        compiler_params=pltpu.CompilerParams(vmem_limit_bytes=16 << 20),
        cost_estimate=pl.CostEstimate(flops=work, transcendentals=0, bytes_accessed=1 << 20),
    )(info, queries, keys_values, keys_values)


def head_back(grad, raw, gain, cos_t, sin_t):
    half_len = HD // 2
    along = grad * sin_t
    grad = grad * cos_t + jnp.concatenate([along[half_len:], -along[:half_len]], axis=0)
    inverse = lax.rsqrt(jnp.mean(raw * raw, axis=0, keepdims=True) + EPS)
    products = grad * (raw * inverse)
    grad = grad * gain
    cubed = inverse * inverse * inverse
    return inverse * grad - raw * cubed * jnp.mean(grad * raw, axis=0, keepdims=True), products


def fold(values):
    total = values[:, :128]
    for at in range(128, values.shape[1], 128):
        total = total + values[:, at : at + 128]
    return total


def attention_back(
    info, queries, keys_values, out, sums, grad_out, q_raw, gain, cos_t, sin_t, group, carried
):
    rows, _, length = queries.shape
    pieces = keys_values.shape[0]
    group_width = GROUP * HD
    scale_factor = 1.0 / math.sqrt(HD)

    def kernel(
        info_ref, q_ref, k_ref, v_ref, out_ref, sums_ref, grad_ref, raw_ref, gain_ref, cos_ref, sin_ref, *refs
    ):
        refs = refs[len(carried) :]
        dq_ref, dkv_ref, gain_grad_ref = refs[:3]
        grad_low, grad_sums, q_rows, grad_rows, k_accum, v_accum, q_accum = refs[3:]
        q_accum[...] = jnp.zeros_like(q_accum)
        for head in range(GROUP):
            own = slice(head * HD, (head + 1) * HD)
            inverse = 1.0 / sums_ref[0, 0, head : head + 1, :]
            grad = grad_ref[0, own, :]
            grad_sums[head] = -jnp.sum(grad * out_ref[0, own, :], axis=0, keepdims=True) * inverse
            scaled = grad * inverse
            grad_low[own, :] = scaled.astype(LOW)
            grad_rows[head] = scaled.T.astype(LOW)
            q_rows[head] = q_ref[0, own, :].T

        def tile(piece, keys, queries_of, bounds):
            key_t, value_t = k_ref[piece, 0, :, keys], v_ref[piece, 0, :, keys]
            key_count, query_count = keys.stop - keys.start, queries_of.stop - queries_of.start
            if bounds is not None:
                mask = allowed(*bounds, 0, (key_count, query_count))
            for head in range(GROUP):
                own = slice(head * HD, (head + 1) * HD)
                exps = jnp.exp(dot(key_t, q_ref[0, own, queries_of], FIRST_FIRST))
                if bounds is not None:
                    exps = jnp.where(mask, exps, 0.0)
                grad_exps = dot(value_t, grad_low[own, queries_of], FIRST_FIRST)
                grad_scores = (exps * (grad_exps + grad_sums[head, :, queries_of])).astype(LOW)
                v_accum[keys] += dot(exps.astype(LOW), grad_rows[head, queries_of], LAST_FIRST)
                k_accum[keys] += dot(grad_scores, q_rows[head, queries_of], LAST_FIRST)
                q_accum[own, queries_of] += dot(key_t, grad_scores, LAST_FIRST)

        def before():
            k_accum[...] = jnp.zeros_like(k_accum)
            v_accum[...] = jnp.zeros_like(v_accum)

        def after(piece):
            dkv_ref[piece, 0, 0] = k_accum[...].T
            dkv_ref[piece, 0, 1] = v_accum[...].T

        over_pieces(info_ref, pieces, length, pl.program_id(0), tile, before, after)
        total = jnp.zeros((HD, 128), jnp.float32)
        for head in range(GROUP):
            own = slice(head * HD, (head + 1) * HD)
            grad, products = head_back(
                scale_factor * q_accum[own, :], raw_ref[0, own, :], gain_ref[...], cos_ref[...], sin_ref[...]
            )
            dq_ref[0, own, :] = grad.astype(LOW)
            total = total + fold(products)
        gain_grad_ref[0] = total

    q_spec = pl.BlockSpec((1, group_width, length), lambda row, *_: (row, group, 0))
    k_spec = pl.BlockSpec((pieces, 1, HD, length), lambda row, *_: (0, row, group, 0))
    v_spec = pl.BlockSpec((pieces, 1, HD, length), lambda row, *_: (0, row, group + KV, 0))
    s_spec = pl.BlockSpec((1, 1, GROUP, length), lambda row, *_: (row, group, 0, 0))
    table_spec = pl.BlockSpec((HD, length), lambda row, *_: (0, 0))
    gain_spec = pl.BlockSpec((HD, 1), lambda row, *_: (0, 0))
    dkv_spec = pl.BlockSpec((pieces, 1, 2, HD, length), lambda row, *_: (0, row, 0, group, 0))
    work = rows * GROUP * length * length * pieces
    inputs = [info, queries, keys_values, keys_values, out, sums, grad_out, q_raw, gain, cos_t, sin_t]
    return pl.pallas_call(
        kernel,
        out_shape=[
            jax.ShapeDtypeStruct(queries.shape, LOW),
            jax.ShapeDtypeStruct((pieces, rows, 2, KV * HD, length), jnp.float32),
            jax.ShapeDtypeStruct((rows, HD, 128), jnp.float32),
        ],
        grid_spec=pltpu.PrefetchScalarGridSpec(
            num_scalar_prefetch=1,
            grid=(rows,),
            in_specs=[
                q_spec, k_spec, v_spec, q_spec, s_spec, q_spec, q_spec, gain_spec, table_spec, table_spec,
                *[ANY] * len(carried),
            ],
            out_specs=[q_spec, dkv_spec, pl.BlockSpec((1, HD, 128), lambda row, *_: (row, 0, 0))],
            scratch_shapes=[
                pltpu.VMEM((group_width, length), LOW),
                pltpu.VMEM((GROUP, 1, length), jnp.float32),
                pltpu.VMEM((GROUP, length, HD), LOW),
                pltpu.VMEM((GROUP, length, HD), LOW),
                pltpu.VMEM((length, HD), jnp.float32),
                pltpu.VMEM((length, HD), jnp.float32),
                pltpu.VMEM((group_width, length), jnp.float32),
            ],
        ),
        input_output_aliases={len(inputs) + at: at for at in range(len(carried))},
        compiler_params=pltpu.CompilerParams(vmem_limit_bytes=16 << 20),
        cost_estimate=pl.CostEstimate(flops=work, transcendentals=0, bytes_accessed=1 << 20),
    )(*inputs, *carried)


def finish_keys(own, others, k_raw, gain, cos_t, sin_t):
    _, rows, _, width, length = own.shape

    def kernel(own_ref, *refs):
        shares, (raw_ref, gain_ref, cos_ref, sin_ref, out_ref, gain_grad_ref) = refs[:-6], refs[-6:]

        def share(which, rows_of):
            total = own_ref[0, 0, which, rows_of, :]
            for ref in shares:
                total = total + ref[0, 0, which, rows_of, :].astype(jnp.float32)
            return total

        total = jnp.zeros((HD, 128), jnp.float32)
        for head in range(KV):
            rows_of = slice(head * HD, (head + 1) * HD)
            grad, products = head_back(
                share(0, rows_of), raw_ref[0, rows_of, :], gain_ref[...], cos_ref[...], sin_ref[...]
            )
            out_ref[0, rows_of, :] = grad.astype(LOW)
            out_ref[0, slice(width + head * HD, width + (head + 1) * HD), :] = share(1, rows_of).astype(LOW)
            total = total + fold(products)
        gain_grad_ref[0] = total

    piece_spec = pl.BlockSpec((1, 1, 2, width, length), lambda row: (0, row, 0, 0, 0))
    table_spec = pl.BlockSpec((HD, length), lambda row: (0, 0))
    return pl.pallas_call(
        kernel,
        out_shape=[
            jax.ShapeDtypeStruct((rows, 2 * width, length), LOW),
            jax.ShapeDtypeStruct((rows, HD, 128), jnp.float32),
        ],
        grid=(rows,),
        in_specs=[
            *[piece_spec] * (1 + len(others)),
            pl.BlockSpec((1, width, length), lambda row: (row, 0, 0)),
            pl.BlockSpec((HD, 1), lambda row: (0, 0)),
            table_spec,
            table_spec,
        ],
        out_specs=[
            pl.BlockSpec((1, 2 * width, length), lambda row: (row, 0, 0)),
            pl.BlockSpec((1, HD, 128), lambda row: (row, 0, 0)),
        ],
        compiler_params=pltpu.CompilerParams(vmem_limit_bytes=16 << 20),
    )(own, *others, k_raw, gain, cos_t, sin_t)


def local(
    tokens,
    cotangent,
    lengths,
    slot_sequence,
    attn_gain,
    w_qkv,
    q_gain,
    k_gain,
    w_out,
    ffn_gain,
    w_gate,
    w_up,
    w_down,
):
    row_count, piece_len, model_width = tokens.shape
    q_width = HEADS * HD
    kv_width = KV * HD
    total_rows = lengths.shape[0]
    scale_factor = 1.0 / math.sqrt(HD)
    shards = lax.axis_size("shard")
    devices = lax.axis_size("dp") * shards
    part_len = attn_gain.shape[0]
    shard_at = lax.axis_index("shard")
    me = (lax.axis_index("dp") * shards + shard_at).astype(jnp.int32).reshape(1)
    row_valid = jnp.sum(
        jnp.where(
            slot_sequence[:, None] == jnp.arange(total_rows, dtype=jnp.int32)[None, :],
            lengths[None, :],
            0,
        ),
        axis=1,
    )
    start = (shard_at * piece_len).astype(jnp.int32)
    positions = start + jnp.arange(piece_len, dtype=jnp.int32)
    live_mask = (positions[None, :] < row_valid[:, None]).astype(jnp.float32)
    cos_t, sin_t = tables(positions)
    cos_h = cos_t[None, None]
    sin_h = sin_t[None, None]
    q_gain_h = q_gain[None, None, :, None]
    k_gain_h = k_gain[None, None, :, None]

    column = jnp.arange(128)[None, :]
    gain_columns = jnp.where(
        column == 0, attn_gain[:, None], jnp.where(column == 1, ffn_gain[:, None], 0.0)
    ).astype(LOW)
    w_qkv_low, w_gate_low, w_up_low = w_qkv.astype(LOW), w_gate.astype(LOW), w_up.astype(LOW)
    gather_a = Gather([w_qkv_low[:, :q_width], w_qkv_low[:, q_width:], gain_columns], me, devices, True)
    gather_b = Gather([w_out.astype(LOW).T], me, devices)
    w_down_low = w_down.astype(LOW).T
    units = w_down_low.shape[1] // 2
    halves = slice(0, units), slice(units, 2 * units)
    gather_c = [
        Gather(
            [jnp.concatenate([w_gate_low[:, own], w_up_low[:, own]], axis=1), w_down_low[:, own]],
            me,
            devices,
            spread=own is halves[1],
        )
        for own in halves
    ]
    (tokens,) = open_slot([gather_a], tokens)
    x_float = tokens.astype(jnp.float32)
    normed_one, inverse_one = normalize(x_float)
    (normed_one,) = close_slot([gather_a], normed_one)
    (normed_one,) = open_slot([gather_a, gather_c[0]], normed_one)
    (normed_one,) = close_slot([gather_a, gather_c[0]], normed_one)
    (normed_one,) = open_slot([gather_a, gather_b], normed_one)
    (normed_one,) = close_slot([gather_a, gather_b], normed_one)
    (normed_one,) = open_slot([gather_a, gather_c[0]], normed_one)
    (normed_one,) = close_slot([gather_a], normed_one)
    wq, wkv, gains = gather_a.whole()
    gain_attn = gains[:, 0].astype(jnp.float32)
    gain_ffn = gains[:, 1].astype(jnp.float32)
    normed_low = (normed_one * gain_attn).astype(LOW)
    kv_raw = jnp.einsum("rtd,de->ret", normed_low, wkv, preferred_element_type=jnp.float32)
    k_raw = kv_raw[:, :kv_width].reshape(row_count, KV, HD, piece_len)
    v_raw = kv_raw[:, kv_width:]
    k_unit, k_inverse = normalize(k_raw, 2)
    k_low = rotate(k_unit * k_gain_h, cos_h, sin_h).astype(LOW).reshape(row_count, kv_width, piece_len)
    own_kv = jnp.concatenate([k_low, v_raw.astype(LOW)], axis=1)
    own_kv, normed_low = close_slot([gather_c[0]], own_kv, normed_low)
    row_pieces = Pieces(own_kv, devices, shards)
    (normed_low,) = open_slot([row_pieces, gather_b, gather_c[1]], normed_low)
    q_raw = jnp.einsum("rtd,de->ret", normed_low, wq, preferred_element_type=jnp.float32).reshape(
        row_count, HEADS, HD, piece_len
    )
    q_unit, q_inverse = normalize(q_raw, 2)
    q_low = (
        rotate(q_unit * q_gain_h, cos_h, sin_h).astype(LOW) * jnp.array(scale_factor, LOW)
    ).reshape(row_count, q_width, piece_len)
    (q_low,) = close_slot([row_pieces, gather_b, gather_c[1]], q_low)
    (q_low,) = open_slot([row_pieces, gather_b, *gather_c], q_low)
    (q_low,) = close_slot([row_pieces], q_low)
    pieces, piece_at = row_pieces.whole()
    info = jnp.concatenate([start.reshape(1), piece_at * piece_len, row_valid]).astype(jnp.int32)
    o_heads, att_low, sums = attention(info, q_low, pieces, 0, KV)
    o_heads, att_low, sums = close_slot([gather_b, *gather_c], o_heads, att_low, sums)
    (att_low,) = open_slot([gather_b, *gather_c], att_low)
    (att_low,) = close_slot([gather_b], att_low)
    (wout,) = gather_b.whole()
    x_mid = x_float + jnp.einsum("rct,dc->rtd", att_low, wout, preferred_element_type=jnp.float32)
    normed_two, inverse_two = normalize(x_mid)
    ffn_in = (normed_two * gain_ffn).astype(LOW)
    grad_out = cotangent.astype(jnp.float32) * live_mask[..., None]
    grad_low = grad_out.astype(LOW)

    def feed_forward(ffn_in, grad_low, wgu, wdown):
        both = jnp.einsum("rtd,df->rtf", ffn_in, wgu, preferred_element_type=jnp.float32)
        gate_proj, up_proj = both[..., :units], both[..., units:]
        gate_sig = jax.nn.sigmoid(gate_proj)
        silu_gate = gate_proj * gate_sig
        activated = (silu_gate * up_proj).astype(LOW)
        grad_down = jnp.einsum("rtd,rtf->df", grad_low, activated, preferred_element_type=jnp.float32)
        grad_act = jnp.einsum("rtd,df->rtf", grad_low, wdown, preferred_element_type=jnp.float32)
        grad_gate = (grad_act * up_proj * gate_sig * (1.0 + gate_proj * (1.0 - gate_sig))).astype(LOW)
        grad_up = (grad_act * silu_gate).astype(LOW)
        grad_both = jnp.concatenate([grad_gate, grad_up], axis=2)
        grad_wgu = jnp.einsum("rtd,rtf->df", ffn_in, grad_both, preferred_element_type=jnp.float32)
        return activated, grad_both, [grad_wgu.astype(LOW), grad_down.astype(LOW)]

    ffn_in, x_mid = close_slot(gather_c, ffn_in, x_mid)
    (ffn_in,) = open_slot([gather_c[1]], ffn_in)
    wgu_one, wdown_one = gather_c[0].whole()
    act_one, both_one, grads = feed_forward(ffn_in, grad_low, wgu_one, wdown_one)
    red_one = Reduce(grads, me, devices)
    red_one.prepare()
    ffn_in, red_one.outgoing, act_one, both_one = close_slot(
        [gather_c[1]], ffn_in, red_one.outgoing, act_one, both_one
    )
    (ffn_in,) = open_slot([gather_c[1]], ffn_in)
    (ffn_in,) = close_slot([gather_c[1]], ffn_in)
    (ffn_in,) = open_slot([red_one], ffn_in, ready=[red_one])
    wgu_two, wdown_two = gather_c[1].whole()
    act_two, both_two, grads = feed_forward(ffn_in, grad_low, wgu_two, wdown_two)
    red_two = Reduce(grads, me, devices)
    red_two.prepare()
    ffn_in, red_two.outgoing, act_two, both_two = close_slot(
        [red_one], ffn_in, red_two.outgoing, act_two, both_two
    )
    both_two, act_two = open_slot([red_one], both_two, act_two)
    grad_ffn_in = jnp.einsum(
        "rtf,df->rtd", both_one, wgu_one, preferred_element_type=jnp.float32
    ) + jnp.einsum("rtf,df->rtd", both_two, wgu_two, preferred_element_type=jnp.float32)
    grad_mid = grad_out + norm_back(x_mid, inverse_two, grad_ffn_in * gain_ffn)
    mid_low = grad_mid.astype(LOW)
    grad_wout = jnp.einsum("rtd,rct->dc", mid_low, att_low, preferred_element_type=jnp.float32)
    grad_att = jnp.einsum("rtd,dc->rct", mid_low, wout, preferred_element_type=jnp.float32)
    red_out = Reduce([grad_wout.astype(LOW)], me, devices, True)
    red_out.prepare()
    grad_att, red_out.outgoing = close_slot([red_one], grad_att, red_out.outgoing)
    (grad_att,) = open_slot([red_one, red_two], grad_att, ready=[red_two])

    q_gain_c, k_gain_c = q_gain[:, None], k_gain[:, None]
    q_raw_flat = q_raw.reshape(row_count, q_width, piece_len)
    k_raw_flat = k_raw.reshape(row_count, kv_width, piece_len)

    def back(group, grad_att, carried=()):
        return attention_back(
            info, q_low, pieces, o_heads, sums, grad_att, q_raw_flat, q_gain_c, cos_t, sin_t, group, carried
        )

    gain_parts = []

    def more(group, grad_att, carried=()):
        *carried, gain_part = back(group, grad_att, carried)
        gain_parts.append(gain_part)
        return tuple(carried)

    carried = more(0, grad_att)
    carried, grad_att = close_slot([red_one, red_two], carried, grad_att)
    (grad_att,) = open_slot([red_one, red_two], grad_att)
    carried = more(1, grad_att, carried)
    carried, grad_att = close_slot([red_one, red_two], carried, grad_att)
    (grad_att,) = open_slot([red_two, red_out], grad_att, ready=[red_out])
    carried = more(2, grad_att, carried)
    carried, grad_att = close_slot([red_two, red_out], carried, grad_att)
    (grad_att,) = open_slot([red_two, red_out], grad_att)
    carried = more(3, grad_att, carried)
    grad_q_low, grad_pieces = close_slot([red_two, red_out], carried)[0]
    kv_back = PiecesBack(grad_pieces, devices, shards)
    (grad_q_low,) = open_slot([kv_back, red_out], grad_q_low)
    (grad_q_low,) = close_slot([kv_back], grad_q_low)
    (grad_q_low,) = open_slot([kv_back], grad_q_low)
    grad_wq = jnp.einsum("rtd,ret->de", normed_low, grad_q_low, preferred_element_type=jnp.float32)
    red_q = Reduce([grad_wq.astype(LOW)], me, devices)
    red_q.prepare()
    red_q.outgoing, grad_q_low = close_slot([kv_back, red_out], red_q.outgoing, grad_q_low)
    (grad_q_low,) = open_slot([kv_back, red_q, red_out], grad_q_low, ready=[red_q])
    grad_normed_q = jnp.einsum("ret,de->rtd", grad_q_low, wq, preferred_element_type=jnp.float32)
    (grad_normed_q,) = close_slot([kv_back, red_q], grad_normed_q)
    kv_back.prepare()
    grad_kv_low, k_gain_part = finish_keys(*kv_back.shares, k_raw_flat, k_gain_c, cos_t, sin_t)
    shared = Sum(
        jnp.concatenate([jnp.sum(sum(gain_parts), axis=(0, 2)), jnp.sum(k_gain_part, axis=(0, 2))])[None],
        devices,
    )
    (grad_kv_low,) = open_slot([red_q, shared], grad_kv_low)
    grad_wkv = jnp.einsum("rtd,ret->de", normed_low, grad_kv_low, preferred_element_type=jnp.float32)
    red_kv = Reduce([grad_wkv.astype(LOW)], me, devices)
    red_kv.prepare()
    red_kv.outgoing, grad_kv_low = close_slot([red_q, red_out, shared], red_kv.outgoing, grad_kv_low)
    (grad_kv_low,) = open_slot([red_q, red_kv, shared, red_out], grad_kv_low, ready=[red_kv])
    grad_normed = grad_normed_q + jnp.einsum(
        "ret,de->rtd", grad_kv_low, wkv, preferred_element_type=jnp.float32
    )
    input_grad = grad_mid + norm_back(x_float, inverse_one, grad_normed * gain_attn)
    (input_grad,) = close_slot([red_q, red_kv, shared, red_out, red_one, red_two], input_grad)
    for one in (red_out, red_one, red_two):
        one.prepare()
    (act_one,) = open_slot([red_q, red_kv], act_one)
    output = (
        x_mid
        + jnp.einsum("rtf,df->rtd", act_one, wdown_one, preferred_element_type=jnp.float32)
        + jnp.einsum("rtf,df->rtd", act_two, wdown_two, preferred_element_type=jnp.float32)
    ).astype(LOW)
    (output,) = close_slot([red_q, red_kv], output)
    red_q.prepare()
    open_slot([red_kv, shared])
    close_slot([red_kv, shared])
    open_slot([red_kv, shared])
    close_slot([red_kv, shared])
    red_kv.prepare()
    shared.prepare()
    shared = shared.values
    three, four = red_q.total, red_kv.total
    summed = red_one.total, red_two.total
    summed_wgate, summed_wup, summed_down = (
        jnp.concatenate([one[:, at * units : (at + 1) * units] for one in summed], axis=1) for at in range(3)
    )
    summed_down, summed_wout = summed_down.T, red_out.total.T
    summed_wqkv = jnp.concatenate([three, four], axis=1)
    grad_gain_one = jnp.sum(summed_wqkv * w_qkv_low, axis=1) / attn_gain.astype(LOW)
    grad_gain_two = jnp.sum(summed_wgate * w_gate_low + summed_wup * w_up_low, axis=1) / ffn_gain.astype(LOW)
    return (
        output,
        input_grad,
        grad_gain_one,
        summed_wqkv,
        shared[0, :HD],
        shared[0, HD:],
        summed_wout,
        grad_gain_two,
        summed_wgate,
        summed_wup,
        summed_down,
    )


def solution(mesh):
    in_specs = (
        P("dp", "shard", None),
        P("dp", "shard", None),
        P(),
        P("dp"),
        P(("dp", "shard")),
        P(("dp", "shard"), None),
        P(),
        P(),
        P(None, ("dp", "shard")),
        P(("dp", "shard")),
        P(("dp", "shard"), None),
        P(("dp", "shard"), None),
        P(None, ("dp", "shard")),
    )
    out_specs = (
        P("dp", "shard", None),
        P("dp", "shard", None),
        P(("dp", "shard")),
        P(("dp", "shard"), None),
        P(),
        P(),
        P(None, ("dp", "shard")),
        P(("dp", "shard")),
        P(("dp", "shard"), None),
        P(("dp", "shard"), None),
        P(None, ("dp", "shard")),
    )
    return jax.shard_map(local, mesh=mesh, in_specs=in_specs, out_specs=out_specs, check_vma=False)
```

```python
import functools
import math

import jax
import jax.numpy as jnp
from jax import lax
from jax.experimental import pallas as pl
from jax.experimental.pallas import tpu as pltpu
from jax.sharding import PartitionSpec as P

HEADS = 16
KV = 4
HD = 64
GROUP = HEADS // KV
EPS = 1e-06
LOW = jnp.bfloat16
ANY = pl.BlockSpec(memory_space=pl.ANY)
VMEM = pl.BlockSpec(memory_space=pltpu.VMEM)
SMEM = pl.BlockSpec(memory_space=pltpu.SMEM)
FIRST_FIRST = (((0,), (0,)), ((), ()))
LAST_FIRST = (((1,), (0,)), ((), ()))
LAST_LAST = (((1,), (1,)), ((), ()))


def dot(left, right, dims):
    return lax.dot_general(left, right, dims, preferred_element_type=jnp.float32)


def normalize(values, axis=-1):
    inverse = lax.rsqrt(jnp.mean(values * values, axis=axis, keepdims=True) + EPS)
    return (values * inverse, inverse)


def norm_back(values, inverse, grad_normed, axis=-1):
    cubed = inverse * inverse * inverse
    return inverse * grad_normed - values * cubed * jnp.mean(
        grad_normed * values, axis=axis, keepdims=True
    )


def rotate(values, cos_t, sin_t):
    half_len = HD // 2
    turned = jnp.concatenate([-values[:, :, half_len:], values[:, :, :half_len]], axis=2)
    return values * cos_t + turned * sin_t


def rotate_back(grad_in, cos_t, sin_t):
    half_len = HD // 2
    along = grad_in * sin_t
    return grad_in * cos_t + jnp.concatenate([along[:, :, half_len:], -along[:, :, :half_len]], axis=2)


def tables(positions):
    freq = 10000.0 ** (-(2.0 * jnp.arange(HD // 2, dtype=jnp.float32)) / HD)
    angles = freq[:, None] * positions.astype(jnp.float32)[None, :]
    angles = jnp.concatenate([angles, angles], axis=0)
    return (jnp.cos(angles), jnp.sin(angles))


def swap(values, mask, devices):
    return lax.ppermute(values, ("dp", "shard"), [(i, i ^ mask) for i in range(devices)])


def place(blocks, masks, widths, me, total_rows):
    count = len(blocks)
    size = blocks[0].shape[0] // len(masks[0])
    copies = sum(len(own) for own in masks) * len(widths)

    def kernel(me_ref, *refs):
        sources, outs, sems = refs[:count], refs[count:-1], refs[-1]
        started = []
        for array, own in zip(sources, masks):
            for at, mask in enumerate(own):
                row = pl.multiple_of((me_ref[0] ^ mask) * size, size)
                column = 0
                for out, width in zip(outs, widths):
                    copy = pltpu.make_async_copy(
                        array.at[pl.ds(at * size, size), pl.ds(column, width)],
                        out.at[pl.ds(row, size)],
                        sems.at[len(started)],
                    )
                    copy.start()
                    started.append(copy)
                    column += width
        for copy in started:
            copy.wait()

    return pl.pallas_call(
        kernel,
        out_shape=[jax.ShapeDtypeStruct((total_rows, width), blocks[0].dtype) for width in widths],
        in_specs=[SMEM] + [ANY] * count,
        out_specs=[VMEM] * len(widths),
        scratch_shapes=[pltpu.SemaphoreType.DMA((copies,))],
        compiler_params=pltpu.CompilerParams(vmem_limit_bytes=24 << 20),
        cost_estimate=pl.CostEstimate(flops=0, transcendentals=0, bytes_accessed=1 << 16),
    )(me, *blocks)


def pick(arrays, orders, me, size):
    count = len(arrays)
    copies = sum(len(own) for own in orders) * count
    width = sum(array.shape[1] for array in arrays)

    def kernel(me_ref, *refs):
        sources, outs, sems = refs[:count], refs[count:-1], refs[-1]
        started = []
        for out, own in zip(outs, orders):
            for at, mask in enumerate(own):
                row = pl.multiple_of((me_ref[0] ^ mask) * size, size)
                column = 0
                for array in sources:
                    copy = pltpu.make_async_copy(
                        array.at[pl.ds(row, size)],
                        out.at[pl.ds(at * size, size), pl.ds(column, array.shape[1])],
                        sems.at[len(started)],
                    )
                    copy.start()
                    started.append(copy)
                    column += array.shape[1]
        for copy in started:
            copy.wait()

    return pl.pallas_call(
        kernel,
        out_shape=[jax.ShapeDtypeStruct((len(own) * size, width), arrays[0].dtype) for own in orders],
        in_specs=[SMEM] + [VMEM] * count,
        out_specs=[ANY] * len(orders),
        scratch_shapes=[pltpu.SemaphoreType.DMA((copies,))],
        compiler_params=pltpu.CompilerParams(vmem_limit_bytes=24 << 20),
        cost_estimate=pl.CostEstimate(flops=0, transcendentals=0, bytes_accessed=1 << 16),
    )(me, *arrays)


class Gather:
    def __init__(self, parts, me, devices, first=False, spread=False):
        self.part = jnp.concatenate(parts, axis=1)
        self.widths = [one.shape[1] for one in parts]
        self.me, self.devices, self.staged, self.first = me, devices, devices == 32, first
        self.stage, self.outgoing, self.incoming = -1 if spread else 0, (), ()
        self.spread = spread

    def prepare(self):
        stage = self.stage
        self.stage += 1
        if not self.staged:
            return
        if stage == -1:
            self.outgoing, self.masks = (self.part,), ((8,),)
        elif stage == 0 and self.spread:
            self.outgoing, self.masks = (jnp.concatenate([self.part, *self.incoming]),), ((16,),)
        elif stage == 0:
            self.outgoing, self.masks = (self.part,), ((8, 16, 24),)
        elif stage == 1:
            if self.spread:
                self.outgoing += self.incoming
            else:
                one, two, three = self.incoming
                self.outgoing = jnp.concatenate([self.part, one]), jnp.concatenate([two, three])
            self.masks = (4,), (2,)
        elif stage == 2:
            self.outgoing = tuple(
                jnp.concatenate([own, came]) for own, came in zip(self.outgoing, self.incoming)
            )
            self.masks = (2,), (4,)
        elif self.first:
            self.outgoing, self.masks = self.outgoing + self.incoming, ((1,),) * 4
        else:
            self.outgoing, self.masks = (jnp.concatenate([*self.outgoing, *self.incoming]),), ((1,),)

    def launch(self):
        if self.staged:
            self.incoming = tuple(
                swap(one, mask, self.devices) for one, own in zip(self.outgoing, self.masks) for mask in own
            )

    def whole(self):
        if not self.staged:
            whole = lax.all_gather(self.part, ("dp", "shard"), axis=0, tiled=True)
            ends = [sum(self.widths[:i]) for i in range(1, len(self.widths))]
            return jnp.split(whole, ends, axis=1)
        near, far = (0, 8, 4, 12), (16, 24, 18, 26)
        masks = [near, far, [m | 2 for m in near], [m | 4 for m in far]]
        if not self.first:
            masks = [[m for own in masks for m in own]]
        masks += [[m | 1 for m in own] for own in masks]
        blocks = self.outgoing + self.incoming
        return place(blocks, masks, self.widths, self.me, self.part.shape[0] * self.devices)


class Reduce:
    def __init__(self, grads, me, devices, spread=False):
        self.grads, self.me, self.devices, self.staged = grads, me, devices, devices == 32
        self.spread = spread
        self.size = grads[0].shape[0] // devices
        self.stage, self.outgoing, self.incoming = 0, (), ()

    def both(self, low, high):
        rows = slice(low * self.size, high * self.size)
        return self.keep[rows].astype(jnp.float32) + self.came[rows].astype(jnp.float32)

    def prepare(self):
        stage, size = self.stage, self.size
        self.stage += 1
        if not self.staged:
            if stage == 0:
                grad = jnp.concatenate([one.astype(jnp.float32) for one in self.grads], axis=1)
                self.total = lax.psum_scatter(grad, ("dp", "shard"), scatter_dimension=0, tiled=True)
            return
        incoming = [one.astype(jnp.float32) for one in self.incoming]
        if stage == 0:
            order = [2, 10, 6, 14, 20, 28, 22, 30, 0, 8, 4, 12, 16, 24, 18, 26]
            self.keep, send = pick(self.grads, [order, [m | 1 for m in order]], self.me, size)
            self.outgoing, self.masks = (send,), (1,)
        elif stage == 1:
            (self.came,) = self.incoming
            self.outgoing = self.both(0, 4).astype(LOW), self.both(4, 8).astype(LOW)
            self.masks = 2, 4
        elif stage == 2:
            near, far = self.both(8, 12) + incoming[0], self.both(12, 16) + incoming[1]
            self.outgoing = near[2 * size :].astype(LOW), far[2 * size :].astype(LOW)
            self.near, self.far = near[: 2 * size], far[: 2 * size]
            self.masks = 4, 2
        elif stage == 3 and self.spread:
            self.near = self.near + incoming[0]
            self.outgoing, self.masks = ((self.far + incoming[1]).astype(LOW),), (16,)
        elif stage == 4 and self.spread:
            near = self.near + incoming[0]
            self.own = near[:size]
            self.outgoing, self.masks = (near[size:].astype(LOW),), (8,)
        elif self.spread and stage > 4:
            self.total = self.own + incoming[0]
        elif stage == 3:
            near, far = self.near + incoming[0], self.far + incoming[1]
            self.outgoing = near[size:].astype(LOW), far[:size].astype(LOW), far[size:].astype(LOW)
            self.own, self.masks = near[:size], (8, 16, 24)
        else:
            self.total = (self.own + incoming[0]) + (incoming[1] + incoming[2])

    def launch(self):
        if self.staged:
            self.incoming = tuple(
                swap(one, mask, self.devices) for one, mask in zip(self.outgoing, self.masks)
            )


class Sum:
    def __init__(self, values, devices):
        self.values, self.devices, self.staged = values, devices, devices == 32
        self.stage, self.outgoing, self.incoming = 0, (), ()

    def prepare(self):
        stage = self.stage
        self.stage += 1
        if not self.staged:
            if stage == 0:
                self.values = lax.psum(self.values, ("dp", "shard"))
            return
        if len(self.incoming) == 3:
            one, two, three = self.incoming
            self.values = (self.values + one) + (two + three)
        elif stage:
            self.values = self.values + self.incoming[0]
        if stage < 4:
            self.outgoing, self.masks = (self.values,), ((16,), (8,), (4, 2, 6), (1,))[stage]

    def launch(self):
        if self.staged:
            self.incoming = tuple(swap(self.outgoing[0], mask, self.devices) for mask in self.masks)


def open_slot(travellers, *values, ready=()):
    for one in travellers:
        if one not in ready:
            one.prepare()
    travellers = [one for one in travellers if one.staged]
    if not travellers:
        return values
    outgoing, values = lax.optimization_barrier((tuple(one.outgoing for one in travellers), values))
    for one, sent in zip(travellers, outgoing):
        one.outgoing = sent
        one.launch()
    return values


def close_slot(travellers, *values):
    travellers = [one for one in travellers if one.staged]
    if not travellers:
        return values
    incoming, values = lax.optimization_barrier((tuple(one.incoming for one in travellers), values))
    for one, came in zip(travellers, incoming):
        one.incoming = came
    return values


class Pieces:
    def __init__(self, part, devices, shards):
        self.part, self.devices, self.shards = part, devices, shards
        self.staged = devices == 32 and shards == 4
        self.stage, self.outgoing, self.incoming = 0, (), ()

    def prepare(self):
        stage = self.stage
        self.stage += 1
        if stage == 0:
            self.outgoing, self.mask = (self.part,), 2
        elif self.staged:
            self.outgoing, self.mask = (jnp.stack([self.part, *self.incoming]),), 1

    def launch(self):
        if self.staged:
            self.incoming = (swap(self.outgoing[0], self.mask, self.devices),)

    def whole(self):
        if not self.staged:
            return lax.all_gather(self.part, "shard", axis=0), jnp.arange(self.shards, dtype=jnp.int32)
        at = jnp.array([0, 2, 1, 3], jnp.int32) ^ lax.axis_index("shard")
        return jnp.concatenate([self.outgoing[0], self.incoming[0]]), at


class PiecesBack:
    def __init__(self, grad, devices, shards):
        self.grad, self.devices, self.staged = grad, devices, devices == 32 and shards == 4
        self.stage, self.outgoing, self.incoming = 0, (), ()

    def prepare(self):
        stage, grad = self.stage, self.grad
        self.stage += 1
        if not self.staged:
            if stage == 0:
                self.shares = lax.psum_scatter(grad, "shard", scatter_dimension=0)[None], ()
        elif stage == 0:
            self.outgoing, self.mask = (grad[2:].astype(LOW),), 1
        elif stage == 1:
            (self.came,) = self.incoming
            self.over = (grad[1:2] + self.came[1:].astype(jnp.float32)).astype(LOW)
            self.outgoing, self.mask = (self.over[:, :, :1],), 2
        elif stage == 2:
            (self.keys,) = self.incoming
            self.outgoing = (self.over[:, :, 1:],)
        else:
            self.shares = grad, (self.came, jnp.concatenate([self.keys, *self.incoming], axis=2))

    def launch(self):
        if self.staged:
            self.incoming = (swap(self.outgoing[0], self.mask, self.devices),)


def allowed(base, start, valid, key_axis, shape):
    key = base + lax.broadcasted_iota(jnp.int32, shape, key_axis)
    query = start + lax.broadcasted_iota(jnp.int32, shape, 1 - key_axis)
    return (key <= query) & (key < valid)


def over_pieces(info_ref, pieces, length, row, tile, before=None, after=None):
    start, valid = info_ref[0], info_ref[1 + pieces + row]
    everything = slice(0, length)
    early, late = slice(0, length // 2), slice(length // 2, length)

    def one(piece, carry):
        base = info_ref[1 + piece]
        if before is not None:
            before()
        used = (base < start + length) & (base < valid)
        full = (base + length <= start) & (base + length <= valid)
        own = base == start

        def diagonal():
            tile(piece, early, everything, (base, start, valid))
            tile(piece, late, late, (base + length // 2, start + length // 2, valid))

        pl.when(used & full)(lambda: tile(piece, everything, everything, None))
        pl.when(used & own)(diagonal)
        pl.when(used & jnp.logical_not(full | own))(
            lambda: tile(piece, everything, everything, (base, start, valid))
        )
        if after is not None:
            after(piece)
        return carry

    lax.fori_loop(0, pieces, one, 0)


def attention(info, queries, keys_values, first, groups):
    rows, _, length = queries.shape
    pieces = keys_values.shape[0]
    group_width = GROUP * HD

    def kernel(info_ref, q_ref, k_ref, v_ref, out_ref, low_ref, sums_ref, accum_ref, part_ref):
        accum_ref[...] = jnp.zeros_like(accum_ref)
        part_ref[...] = jnp.zeros_like(part_ref)

        def tile(piece, keys, rows_of, bounds):
            key_t, value_t = k_ref[piece, 0, :, keys], v_ref[piece, 0, :, keys]
            key_count, row_count = keys.stop - keys.start, rows_of.stop - rows_of.start
            if bounds is not None:
                mask = allowed(*bounds, 1, (row_count, key_count))
            for head in range(GROUP):
                own = slice(head * HD, (head + 1) * HD)
                exps = jnp.exp(dot(q_ref[0, own, rows_of], key_t, FIRST_FIRST))
                if bounds is not None:
                    exps = jnp.where(mask, exps, 0.0)
                part = exps[:, :128]
                for at in range(128, key_count, 128):
                    part = part + exps[:, at : at + 128]
                part_ref[head, rows_of] += part
                accum_ref[head, rows_of] += dot(exps.astype(LOW), value_t, LAST_LAST)

        over_pieces(info_ref, pieces, length, pl.program_id(0), tile)
        for head in range(GROUP):
            own = slice(head * HD, (head + 1) * HD)
            sums = jnp.sum(part_ref[head].T, axis=0, keepdims=True)
            sums_ref[0, 0, head : head + 1, :] = sums
            out = accum_ref[head].T / sums
            out_ref[0, own, :] = out
            low_ref[0, own, :] = out.astype(LOW)

    q_spec = pl.BlockSpec((1, group_width, length), lambda row, group, *_: (row, group + first, 0))
    o_spec = pl.BlockSpec((1, group_width, length), lambda row, group, *_: (row, group, 0))
    k_spec = pl.BlockSpec((pieces, 1, HD, length), lambda row, group, *_: (0, row, group + first, 0))
    v_spec = pl.BlockSpec(
        (pieces, 1, HD, length), lambda row, group, *_: (0, row, group + first + KV, 0)
    )
    s_spec = pl.BlockSpec((1, 1, GROUP, length), lambda row, group, *_: (row, group, 0, 0))
    work = rows * groups * GROUP * length * length * pieces
    return pl.pallas_call(
        kernel,
        out_shape=[
            jax.ShapeDtypeStruct((rows, groups * group_width, length), jnp.float32),
            jax.ShapeDtypeStruct((rows, groups * group_width, length), LOW),
            jax.ShapeDtypeStruct((rows, groups, GROUP, length), jnp.float32),
        ],
        grid_spec=pltpu.PrefetchScalarGridSpec(
            num_scalar_prefetch=1,
            grid=(rows, groups),
            in_specs=[q_spec, k_spec, v_spec],
            out_specs=[o_spec, o_spec, s_spec],
            scratch_shapes=[
                pltpu.VMEM((GROUP, length, HD), jnp.float32),
                pltpu.VMEM((GROUP, length, 128), jnp.float32),
            ],
        ),
        compiler_params=pltpu.CompilerParams(vmem_limit_bytes=16 << 20),
        cost_estimate=pl.CostEstimate(flops=work, transcendentals=0, bytes_accessed=1 << 20),
    )(info, queries, keys_values, keys_values)


def head_back(grad, raw, gain, cos_t, sin_t):
    half_len = HD // 2
    along = grad * sin_t
    grad = grad * cos_t + jnp.concatenate([along[half_len:], -along[:half_len]], axis=0)
    inverse = lax.rsqrt(jnp.mean(raw * raw, axis=0, keepdims=True) + EPS)
    products = grad * (raw * inverse)
    grad = grad * gain
    cubed = inverse * inverse * inverse
    return inverse * grad - raw * cubed * jnp.mean(grad * raw, axis=0, keepdims=True), products


def fold(values):
    total = values[:, :128]
    for at in range(128, values.shape[1], 128):
        total = total + values[:, at : at + 128]
    return total


def attention_back(
    info, queries, keys_values, out, sums, grad_out, q_raw, gain, cos_t, sin_t, group, carried
):
    rows, _, length = queries.shape
    pieces = keys_values.shape[0]
    group_width = GROUP * HD
    scale_factor = 1.0 / math.sqrt(HD)

    def kernel(
        info_ref, q_ref, k_ref, v_ref, out_ref, sums_ref, grad_ref, raw_ref, gain_ref, cos_ref, sin_ref, *refs
    ):
        refs = refs[len(carried) :]
        dq_ref, dkv_ref, gain_grad_ref = refs[:3]
        grad_low, grad_sums, q_rows, grad_rows, k_accum, v_accum, q_accum = refs[3:]
        q_accum[...] = jnp.zeros_like(q_accum)
        for head in range(GROUP):
            own = slice(head * HD, (head + 1) * HD)
            inverse = 1.0 / sums_ref[0, 0, head : head + 1, :]
            grad = grad_ref[0, own, :]
            grad_sums[head] = -jnp.sum(grad * out_ref[0, own, :], axis=0, keepdims=True) * inverse
            scaled = grad * inverse
            grad_low[own, :] = scaled.astype(LOW)
            grad_rows[head] = scaled.T.astype(LOW)
            q_rows[head] = q_ref[0, own, :].T

        def tile(piece, keys, queries_of, bounds):
            key_t, value_t = k_ref[piece, 0, :, keys], v_ref[piece, 0, :, keys]
            key_count, query_count = keys.stop - keys.start, queries_of.stop - queries_of.start
            if bounds is not None:
                mask = allowed(*bounds, 0, (key_count, query_count))
            for head in range(GROUP):
                own = slice(head * HD, (head + 1) * HD)
                exps = jnp.exp(dot(key_t, q_ref[0, own, queries_of], FIRST_FIRST))
                if bounds is not None:
                    exps = jnp.where(mask, exps, 0.0)
                grad_exps = dot(value_t, grad_low[own, queries_of], FIRST_FIRST)
                grad_scores = (exps * (grad_exps + grad_sums[head, :, queries_of])).astype(LOW)
                v_accum[keys] += dot(exps.astype(LOW), grad_rows[head, queries_of], LAST_FIRST)
                k_accum[keys] += dot(grad_scores, q_rows[head, queries_of], LAST_FIRST)
                q_accum[own, queries_of] += dot(key_t, grad_scores, LAST_FIRST)

        def before():
            k_accum[...] = jnp.zeros_like(k_accum)
            v_accum[...] = jnp.zeros_like(v_accum)

        def after(piece):
            dkv_ref[piece, 0, 0] = k_accum[...].T
            dkv_ref[piece, 0, 1] = v_accum[...].T

        over_pieces(info_ref, pieces, length, pl.program_id(0), tile, before, after)
        total = jnp.zeros((HD, 128), jnp.float32)
        for head in range(GROUP):
            own = slice(head * HD, (head + 1) * HD)
            grad, products = head_back(
                scale_factor * q_accum[own, :], raw_ref[0, own, :], gain_ref[...], cos_ref[...], sin_ref[...]
            )
            dq_ref[0, own, :] = grad.astype(LOW)
            total = total + fold(products)
        gain_grad_ref[0] = total

    q_spec = pl.BlockSpec((1, group_width, length), lambda row, *_: (row, group, 0))
    k_spec = pl.BlockSpec((pieces, 1, HD, length), lambda row, *_: (0, row, group, 0))
    v_spec = pl.BlockSpec((pieces, 1, HD, length), lambda row, *_: (0, row, group + KV, 0))
    s_spec = pl.BlockSpec((1, 1, GROUP, length), lambda row, *_: (row, group, 0, 0))
    table_spec = pl.BlockSpec((HD, length), lambda row, *_: (0, 0))
    gain_spec = pl.BlockSpec((HD, 1), lambda row, *_: (0, 0))
    dkv_spec = pl.BlockSpec((pieces, 1, 2, HD, length), lambda row, *_: (0, row, 0, group, 0))
    work = rows * GROUP * length * length * pieces
    out, grad_out, q_raw = (
        pltpu.with_memory_space_constraint(one, pltpu.HBM) for one in (out, grad_out, q_raw)
    )
    inputs = [info, queries, keys_values, keys_values, out, sums, grad_out, q_raw, gain, cos_t, sin_t]
    return pl.pallas_call(
        kernel,
        out_shape=[
            jax.ShapeDtypeStruct(queries.shape, LOW),
            jax.ShapeDtypeStruct((pieces, rows, 2, KV * HD, length), jnp.float32),
            jax.ShapeDtypeStruct((rows, HD, 128), jnp.float32),
        ],
        grid_spec=pltpu.PrefetchScalarGridSpec(
            num_scalar_prefetch=1,
            grid=(rows,),
            in_specs=[
                q_spec, k_spec, v_spec, q_spec, s_spec, q_spec, q_spec, gain_spec, table_spec, table_spec,
                *[ANY] * len(carried),
            ],
            out_specs=[q_spec, dkv_spec, pl.BlockSpec((1, HD, 128), lambda row, *_: (row, 0, 0))],
            scratch_shapes=[
                pltpu.VMEM((group_width, length), LOW),
                pltpu.VMEM((GROUP, 1, length), jnp.float32),
                pltpu.VMEM((GROUP, length, HD), LOW),
                pltpu.VMEM((GROUP, length, HD), LOW),
                pltpu.VMEM((length, HD), jnp.float32),
                pltpu.VMEM((length, HD), jnp.float32),
                pltpu.VMEM((group_width, length), jnp.float32),
            ],
        ),
        input_output_aliases={len(inputs) + at: at for at in range(len(carried))},
        compiler_params=pltpu.CompilerParams(vmem_limit_bytes=16 << 20),
        cost_estimate=pl.CostEstimate(flops=work, transcendentals=0, bytes_accessed=1 << 20),
    )(*inputs, *carried)


def finish_keys(own, others, k_raw, gain, cos_t, sin_t):
    _, rows, _, width, length = own.shape

    def kernel(own_ref, *refs):
        shares, (raw_ref, gain_ref, cos_ref, sin_ref, out_ref, gain_grad_ref) = refs[:-6], refs[-6:]

        def share(which, rows_of):
            total = own_ref[0, 0, which, rows_of, :]
            for ref in shares:
                total = total + ref[0, 0, which, rows_of, :].astype(jnp.float32)
            return total

        total = jnp.zeros((HD, 128), jnp.float32)
        for head in range(KV):
            rows_of = slice(head * HD, (head + 1) * HD)
            grad, products = head_back(
                share(0, rows_of), raw_ref[0, rows_of, :], gain_ref[...], cos_ref[...], sin_ref[...]
            )
            out_ref[0, rows_of, :] = grad.astype(LOW)
            out_ref[0, slice(width + head * HD, width + (head + 1) * HD), :] = share(1, rows_of).astype(LOW)
            total = total + fold(products)
        gain_grad_ref[0] = total

    piece_spec = pl.BlockSpec((1, 1, 2, width, length), lambda row: (0, row, 0, 0, 0))
    table_spec = pl.BlockSpec((HD, length), lambda row: (0, 0))
    return pl.pallas_call(
        kernel,
        out_shape=[
            jax.ShapeDtypeStruct((rows, 2 * width, length), LOW),
            jax.ShapeDtypeStruct((rows, HD, 128), jnp.float32),
        ],
        grid=(rows,),
        in_specs=[
            *[piece_spec] * (1 + len(others)),
            pl.BlockSpec((1, width, length), lambda row: (row, 0, 0)),
            pl.BlockSpec((HD, 1), lambda row: (0, 0)),
            table_spec,
            table_spec,
        ],
        out_specs=[
            pl.BlockSpec((1, 2 * width, length), lambda row: (row, 0, 0)),
            pl.BlockSpec((1, HD, 128), lambda row: (row, 0, 0)),
        ],
        compiler_params=pltpu.CompilerParams(vmem_limit_bytes=16 << 20),
    )(own, *others, k_raw, gain, cos_t, sin_t)


def local(
    tokens,
    cotangent,
    lengths,
    slot_sequence,
    attn_gain,
    w_qkv,
    q_gain,
    k_gain,
    w_out,
    ffn_gain,
    w_gate,
    w_up,
    w_down,
):
    row_count, piece_len, model_width = tokens.shape
    q_width = HEADS * HD
    kv_width = KV * HD
    total_rows = lengths.shape[0]
    scale_factor = 1.0 / math.sqrt(HD)
    shards = lax.axis_size("shard")
    devices = lax.axis_size("dp") * shards
    part_len = attn_gain.shape[0]
    shard_at = lax.axis_index("shard")
    me = (lax.axis_index("dp") * shards + shard_at).astype(jnp.int32).reshape(1)
    row_valid = jnp.sum(
        jnp.where(
            slot_sequence[:, None] == jnp.arange(total_rows, dtype=jnp.int32)[None, :],
            lengths[None, :],
            0,
        ),
        axis=1,
    )
    start = (shard_at * piece_len).astype(jnp.int32)
    positions = start + jnp.arange(piece_len, dtype=jnp.int32)
    live_mask = (positions[None, :] < row_valid[:, None]).astype(jnp.float32)
    cos_t, sin_t = tables(positions)
    cos_h = cos_t[None, None]
    sin_h = sin_t[None, None]
    q_gain_h = q_gain[None, None, :, None]
    k_gain_h = k_gain[None, None, :, None]

    column = jnp.arange(128)[None, :]
    gain_columns = jnp.where(
        column == 0, attn_gain[:, None], jnp.where(column == 1, ffn_gain[:, None], 0.0)
    ).astype(LOW)
    w_qkv_low, w_gate_low, w_up_low = w_qkv.astype(LOW), w_gate.astype(LOW), w_up.astype(LOW)
    gather_a = Gather([w_qkv_low[:, :q_width], w_qkv_low[:, q_width:], gain_columns], me, devices, True)
    gather_b = Gather([w_out.astype(LOW).T], me, devices)
    w_down_low = w_down.astype(LOW).T
    units = w_down_low.shape[1] // 2
    halves = slice(0, units), slice(units, 2 * units)
    gather_c = [
        Gather(
            [jnp.concatenate([w_gate_low[:, own], w_up_low[:, own]], axis=1), w_down_low[:, own]],
            me,
            devices,
            spread=own is halves[1],
        )
        for own in halves
    ]
    (tokens,) = open_slot([gather_a], tokens)
    x_float = tokens.astype(jnp.float32)
    normed_one, inverse_one = normalize(x_float)
    (normed_one,) = close_slot([gather_a], normed_one)
    (normed_one,) = open_slot([gather_a, gather_c[0]], normed_one)
    (normed_one,) = close_slot([gather_a, gather_c[0]], normed_one)
    (normed_one,) = open_slot([gather_a, gather_b], normed_one)
    (normed_one,) = close_slot([gather_a, gather_b], normed_one)
    (normed_one,) = open_slot([gather_a, gather_c[0]], normed_one)
    (normed_one,) = close_slot([gather_a], normed_one)
    wq, wkv, gains = gather_a.whole()
    gain_attn = gains[:, 0].astype(jnp.float32)
    gain_ffn = gains[:, 1].astype(jnp.float32)
    normed_low = (normed_one * gain_attn).astype(LOW)
    kv_raw = jnp.einsum("rtd,de->ret", normed_low, wkv, preferred_element_type=jnp.float32)
    k_raw = kv_raw[:, :kv_width].reshape(row_count, KV, HD, piece_len)
    v_raw = kv_raw[:, kv_width:]
    k_unit, k_inverse = normalize(k_raw, 2)
    k_low = rotate(k_unit * k_gain_h, cos_h, sin_h).astype(LOW).reshape(row_count, kv_width, piece_len)
    own_kv = jnp.concatenate([k_low, v_raw.astype(LOW)], axis=1)
    own_kv, normed_low = close_slot([gather_c[0]], own_kv, normed_low)
    row_pieces = Pieces(own_kv, devices, shards)
    (normed_low,) = open_slot([row_pieces, gather_b, gather_c[1]], normed_low)
    q_raw = jnp.einsum("rtd,de->ret", normed_low, wq, preferred_element_type=jnp.float32).reshape(
        row_count, HEADS, HD, piece_len
    )
    q_unit, q_inverse = normalize(q_raw, 2)
    q_low = (
        rotate(q_unit * q_gain_h, cos_h, sin_h).astype(LOW) * jnp.array(scale_factor, LOW)
    ).reshape(row_count, q_width, piece_len)
    (q_low,) = close_slot([row_pieces, gather_b, gather_c[1]], q_low)
    (q_low,) = open_slot([row_pieces, gather_b, *gather_c], q_low)
    (q_low,) = close_slot([row_pieces], q_low)
    pieces, piece_at = row_pieces.whole()
    info = jnp.concatenate([start.reshape(1), piece_at * piece_len, row_valid]).astype(jnp.int32)
    o_heads, att_low, sums = attention(info, q_low, pieces, 0, KV)
    o_heads, att_low, sums = close_slot([gather_b, *gather_c], o_heads, att_low, sums)
    (att_low,) = open_slot([gather_b, *gather_c], att_low)
    (att_low,) = close_slot([gather_b], att_low)
    (wout,) = gather_b.whole()
    x_mid = x_float + jnp.einsum("rct,dc->rtd", att_low, wout, preferred_element_type=jnp.float32)
    normed_two, inverse_two = normalize(x_mid)
    ffn_in = (normed_two * gain_ffn).astype(LOW)
    grad_out = cotangent.astype(jnp.float32) * live_mask[..., None]
    grad_low = grad_out.astype(LOW)

    def feed_forward(ffn_in, grad_low, wgu, wdown):
        both = jnp.einsum("rtd,df->rtf", ffn_in, wgu, preferred_element_type=jnp.float32)
        gate_proj, up_proj = both[..., :units], both[..., units:]
        gate_sig = jax.nn.sigmoid(gate_proj)
        silu_gate = gate_proj * gate_sig
        activated = (silu_gate * up_proj).astype(LOW)
        grad_down = jnp.einsum("rtd,rtf->df", grad_low, activated, preferred_element_type=jnp.float32)
        grad_act = jnp.einsum("rtd,df->rtf", grad_low, wdown, preferred_element_type=jnp.float32)
        grad_gate = (grad_act * up_proj * gate_sig * (1.0 + gate_proj * (1.0 - gate_sig))).astype(LOW)
        grad_up = (grad_act * silu_gate).astype(LOW)
        grad_both = jnp.concatenate([grad_gate, grad_up], axis=2)
        grad_wgu = jnp.einsum("rtd,rtf->df", ffn_in, grad_both, preferred_element_type=jnp.float32)
        return activated, grad_both, [grad_wgu.astype(LOW), grad_down.astype(LOW)]

    ffn_in, x_mid = close_slot(gather_c, ffn_in, x_mid)
    (ffn_in,) = open_slot([gather_c[1]], ffn_in)
    wgu_one, wdown_one = gather_c[0].whole()
    act_one, both_one, grads = feed_forward(ffn_in, grad_low, wgu_one, wdown_one)
    red_one = Reduce(grads, me, devices)
    red_one.prepare()
    ffn_in, red_one.outgoing, act_one, both_one = close_slot(
        [gather_c[1]], ffn_in, red_one.outgoing, act_one, both_one
    )
    (ffn_in,) = open_slot([gather_c[1]], ffn_in)
    (ffn_in,) = close_slot([gather_c[1]], ffn_in)
    (ffn_in,) = open_slot([red_one], ffn_in, ready=[red_one])
    wgu_two, wdown_two = gather_c[1].whole()
    act_two, both_two, grads = feed_forward(ffn_in, grad_low, wgu_two, wdown_two)
    red_two = Reduce(grads, me, devices)
    red_two.prepare()
    ffn_in, red_two.outgoing, act_two, both_two = close_slot(
        [red_one], ffn_in, red_two.outgoing, act_two, both_two
    )
    both_two, act_two = open_slot([red_one], both_two, act_two)
    grad_ffn_in = jnp.einsum(
        "rtf,df->rtd", both_one, wgu_one, preferred_element_type=jnp.float32
    ) + jnp.einsum("rtf,df->rtd", both_two, wgu_two, preferred_element_type=jnp.float32)
    grad_mid = grad_out + norm_back(x_mid, inverse_two, grad_ffn_in * gain_ffn)
    mid_low = grad_mid.astype(LOW)
    grad_wout = jnp.einsum("rtd,rct->dc", mid_low, att_low, preferred_element_type=jnp.float32)
    grad_att = jnp.einsum("rtd,dc->rct", mid_low, wout, preferred_element_type=jnp.float32)
    red_out = Reduce([grad_wout.astype(LOW)], me, devices, True)
    red_out.prepare()
    grad_att, red_out.outgoing = close_slot([red_one], grad_att, red_out.outgoing)
    (grad_att,) = open_slot([red_one, red_two], grad_att, ready=[red_two])

    q_gain_c, k_gain_c = q_gain[:, None], k_gain[:, None]
    q_raw_flat = q_raw.reshape(row_count, q_width, piece_len)
    k_raw_flat = k_raw.reshape(row_count, kv_width, piece_len)

    def back(group, grad_att, carried=()):
        return attention_back(
            info, q_low, pieces, o_heads, sums, grad_att, q_raw_flat, q_gain_c, cos_t, sin_t, group, carried
        )

    gain_parts = []

    def more(group, grad_att, carried=()):
        *carried, gain_part = back(group, grad_att, carried)
        gain_parts.append(gain_part)
        return tuple(carried)

    carried = more(0, grad_att)
    carried, grad_att = close_slot([red_one, red_two], carried, grad_att)
    (grad_att,) = open_slot([red_one, red_two], grad_att)
    carried = more(1, grad_att, carried)
    carried, grad_att = close_slot([red_one, red_two], carried, grad_att)
    (grad_att,) = open_slot([red_two, red_out], grad_att, ready=[red_out])
    carried = more(2, grad_att, carried)
    carried, grad_att = close_slot([red_two, red_out], carried, grad_att)
    (grad_att,) = open_slot([red_two, red_out], grad_att)
    carried = more(3, grad_att, carried)
    grad_q_low, grad_pieces = close_slot([red_two, red_out], carried)[0]
    kv_back = PiecesBack(grad_pieces, devices, shards)
    (grad_q_low,) = open_slot([kv_back, red_out], grad_q_low)
    (grad_q_low,) = close_slot([kv_back], grad_q_low)
    (grad_q_low,) = open_slot([kv_back], grad_q_low)
    grad_wq = jnp.einsum("rtd,ret->de", normed_low, grad_q_low, preferred_element_type=jnp.float32)
    red_q = Reduce([grad_wq.astype(LOW)], me, devices)
    red_q.prepare()
    red_q.outgoing, grad_q_low = close_slot([kv_back, red_out], red_q.outgoing, grad_q_low)
    (grad_q_low,) = open_slot([kv_back, red_q, red_out], grad_q_low, ready=[red_q])
    grad_normed_q = jnp.einsum("ret,de->rtd", grad_q_low, wq, preferred_element_type=jnp.float32)
    (grad_normed_q,) = close_slot([kv_back, red_q], grad_normed_q)
    kv_back.prepare()
    grad_kv_low, k_gain_part = finish_keys(*kv_back.shares, k_raw_flat, k_gain_c, cos_t, sin_t)
    shared = Sum(
        jnp.concatenate([jnp.sum(sum(gain_parts), axis=(0, 2)), jnp.sum(k_gain_part, axis=(0, 2))])[None],
        devices,
    )
    (grad_kv_low,) = open_slot([red_q, shared], grad_kv_low)
    grad_wkv = jnp.einsum("rtd,ret->de", normed_low, grad_kv_low, preferred_element_type=jnp.float32)
    red_kv = Reduce([grad_wkv.astype(LOW)], me, devices)
    red_kv.prepare()
    red_kv.outgoing, grad_kv_low = close_slot([red_q, red_out, shared], red_kv.outgoing, grad_kv_low)
    (grad_kv_low,) = open_slot([red_q, red_kv, shared, red_out], grad_kv_low, ready=[red_kv])
    grad_normed = grad_normed_q + jnp.einsum(
        "ret,de->rtd", grad_kv_low, wkv, preferred_element_type=jnp.float32
    )
    input_grad = grad_mid + norm_back(x_float, inverse_one, grad_normed * gain_attn)
    (input_grad,) = close_slot([red_q, red_kv, shared, red_out, red_one, red_two], input_grad)
    for one in (red_out, red_one, red_two):
        one.prepare()
    (act_one,) = open_slot([red_q, red_kv], act_one)
    output = (
        x_mid
        + jnp.einsum("rtf,df->rtd", act_one, wdown_one, preferred_element_type=jnp.float32)
        + jnp.einsum("rtf,df->rtd", act_two, wdown_two, preferred_element_type=jnp.float32)
    ).astype(LOW)
    (output,) = close_slot([red_q, red_kv], output)
    red_q.prepare()
    open_slot([red_kv, shared])
    close_slot([red_kv, shared])
    open_slot([red_kv, shared])
    close_slot([red_kv, shared])
    red_kv.prepare()
    shared.prepare()
    shared = shared.values
    three, four = red_q.total, red_kv.total
    summed = red_one.total, red_two.total
    summed_wgate, summed_wup, summed_down = (
        jnp.concatenate([one[:, at * units : (at + 1) * units] for one in summed], axis=1) for at in range(3)
    )
    summed_down, summed_wout = summed_down.T, red_out.total.T
    summed_wqkv = jnp.concatenate([three, four], axis=1)
    grad_gain_one = jnp.sum(summed_wqkv * w_qkv_low, axis=1) / attn_gain.astype(LOW)
    grad_gain_two = jnp.sum(summed_wgate * w_gate_low + summed_wup * w_up_low, axis=1) / ffn_gain.astype(LOW)
    return (
        output,
        input_grad,
        grad_gain_one,
        summed_wqkv,
        shared[0, :HD],
        shared[0, HD:],
        summed_wout,
        grad_gain_two,
        summed_wgate,
        summed_wup,
        summed_down,
    )


def solution(mesh):
    in_specs = (
        P("dp", "shard", None),
        P("dp", "shard", None),
        P(),
        P("dp"),
        P(("dp", "shard")),
        P(("dp", "shard"), None),
        P(),
        P(),
        P(None, ("dp", "shard")),
        P(("dp", "shard")),
        P(("dp", "shard"), None),
        P(("dp", "shard"), None),
        P(None, ("dp", "shard")),
    )
    out_specs = (
        P("dp", "shard", None),
        P("dp", "shard", None),
        P(("dp", "shard")),
        P(("dp", "shard"), None),
        P(),
        P(),
        P(None, ("dp", "shard")),
        P(("dp", "shard")),
        P(("dp", "shard"), None),
        P(("dp", "shard"), None),
        P(None, ("dp", "shard")),
    )
    return jax.shard_map(local, mesh=mesh, in_specs=in_specs, out_specs=out_specs, check_vma=False)
```

```python
import functools
import math

import jax
import jax.numpy as jnp
from jax import lax
from jax.experimental import pallas as pl
from jax.experimental.pallas import tpu as pltpu
from jax.sharding import PartitionSpec as P

HEADS = 16
KV = 4
HD = 64
GROUP = HEADS // KV
EPS = 1e-06
LOW = jnp.bfloat16
ANY = pl.BlockSpec(memory_space=pl.ANY)
VMEM = pl.BlockSpec(memory_space=pltpu.VMEM)
SMEM = pl.BlockSpec(memory_space=pltpu.SMEM)
FIRST_FIRST = (((0,), (0,)), ((), ()))
LAST_FIRST = (((1,), (0,)), ((), ()))
LAST_LAST = (((1,), (1,)), ((), ()))


def dot(left, right, dims):
    return lax.dot_general(left, right, dims, preferred_element_type=jnp.float32)


def normalize(values, axis=-1):
    inverse = lax.rsqrt(jnp.mean(values * values, axis=axis, keepdims=True) + EPS)
    return (values * inverse, inverse)


def norm_back(values, inverse, grad_normed, axis=-1):
    cubed = inverse * inverse * inverse
    return inverse * grad_normed - values * cubed * jnp.mean(
        grad_normed * values, axis=axis, keepdims=True
    )


def rotate(values, cos_t, sin_t):
    half_len = HD // 2
    turned = jnp.concatenate([-values[:, :, half_len:], values[:, :, :half_len]], axis=2)
    return values * cos_t + turned * sin_t


def rotate_back(grad_in, cos_t, sin_t):
    half_len = HD // 2
    along = grad_in * sin_t
    return grad_in * cos_t + jnp.concatenate([along[:, :, half_len:], -along[:, :, :half_len]], axis=2)


def tables(positions):
    freq = 10000.0 ** (-(2.0 * jnp.arange(HD // 2, dtype=jnp.float32)) / HD)
    angles = freq[:, None] * positions.astype(jnp.float32)[None, :]
    angles = jnp.concatenate([angles, angles], axis=0)
    return (jnp.cos(angles), jnp.sin(angles))


def swap(values, mask, devices):
    return lax.ppermute(values, ("dp", "shard"), [(i, i ^ mask) for i in range(devices)])


def place(blocks, masks, widths, me, total_rows):
    count = len(blocks)
    size = blocks[0].shape[0] // len(masks[0])
    copies = sum(len(own) for own in masks) * len(widths)

    def kernel(me_ref, *refs):
        sources, outs, sems = refs[:count], refs[count:-1], refs[-1]
        started = []
        for array, own in zip(sources, masks):
            for at, mask in enumerate(own):
                row = pl.multiple_of((me_ref[0] ^ mask) * size, size)
                column = 0
                for out, width in zip(outs, widths):
                    copy = pltpu.make_async_copy(
                        array.at[pl.ds(at * size, size), pl.ds(column, width)],
                        out.at[pl.ds(row, size)],
                        sems.at[len(started)],
                    )
                    copy.start()
                    started.append(copy)
                    column += width
        for copy in started:
            copy.wait()

    return pl.pallas_call(
        kernel,
        out_shape=[jax.ShapeDtypeStruct((total_rows, width), blocks[0].dtype) for width in widths],
        in_specs=[SMEM] + [ANY] * count,
        out_specs=[VMEM] * len(widths),
        scratch_shapes=[pltpu.SemaphoreType.DMA((copies,))],
        compiler_params=pltpu.CompilerParams(vmem_limit_bytes=24 << 20),
        cost_estimate=pl.CostEstimate(flops=0, transcendentals=0, bytes_accessed=1 << 16),
    )(me, *blocks)


def pick(arrays, orders, me, size):
    count = len(arrays)
    copies = sum(len(own) for own in orders) * count
    width = sum(array.shape[1] for array in arrays)

    def kernel(me_ref, *refs):
        sources, outs, sems = refs[:count], refs[count:-1], refs[-1]
        started = []
        for out, own in zip(outs, orders):
            for at, mask in enumerate(own):
                row = pl.multiple_of((me_ref[0] ^ mask) * size, size)
                column = 0
                for array in sources:
                    copy = pltpu.make_async_copy(
                        array.at[pl.ds(row, size)],
                        out.at[pl.ds(at * size, size), pl.ds(column, array.shape[1])],
                        sems.at[len(started)],
                    )
                    copy.start()
                    started.append(copy)
                    column += array.shape[1]
        for copy in started:
            copy.wait()

    return pl.pallas_call(
        kernel,
        out_shape=[jax.ShapeDtypeStruct((len(own) * size, width), arrays[0].dtype) for own in orders],
        in_specs=[SMEM] + [VMEM] * count,
        out_specs=[ANY] * len(orders),
        scratch_shapes=[pltpu.SemaphoreType.DMA((copies,))],
        compiler_params=pltpu.CompilerParams(vmem_limit_bytes=24 << 20),
        cost_estimate=pl.CostEstimate(flops=0, transcendentals=0, bytes_accessed=1 << 16),
    )(me, *arrays)


class Gather:
    def __init__(self, parts, me, devices, first=False, spread=False):
        self.part = jnp.concatenate(parts, axis=1)
        self.widths = [one.shape[1] for one in parts]
        self.me, self.devices, self.staged, self.first = me, devices, devices == 32, first
        self.stage, self.outgoing, self.incoming = -1 if spread else 0, (), ()
        self.spread = spread

    def prepare(self):
        stage = self.stage
        self.stage += 1
        if not self.staged:
            return
        if stage == -1:
            self.outgoing, self.masks = (self.part,), ((8,),)
        elif stage == 0 and self.spread:
            self.outgoing, self.masks = (jnp.concatenate([self.part, *self.incoming]),), ((16,),)
        elif stage == 0:
            self.outgoing, self.masks = (self.part,), ((8, 16, 24),)
        elif stage == 1:
            if self.spread:
                self.outgoing += self.incoming
            else:
                one, two, three = self.incoming
                self.outgoing = jnp.concatenate([self.part, one]), jnp.concatenate([two, three])
            self.masks = (4,), (2,)
        elif stage == 2:
            self.outgoing = tuple(
                jnp.concatenate([own, came]) for own, came in zip(self.outgoing, self.incoming)
            )
            self.masks = (2,), (4,)
        elif self.first:
            self.outgoing, self.masks = self.outgoing + self.incoming, ((1,),) * 4
        else:
            self.outgoing, self.masks = (jnp.concatenate([*self.outgoing, *self.incoming]),), ((1,),)

    def launch(self):
        if self.staged:
            self.incoming = tuple(
                swap(one, mask, self.devices) for one, own in zip(self.outgoing, self.masks) for mask in own
            )

    def whole(self):
        if not self.staged:
            whole = lax.all_gather(self.part, ("dp", "shard"), axis=0, tiled=True)
            ends = [sum(self.widths[:i]) for i in range(1, len(self.widths))]
            return jnp.split(whole, ends, axis=1)
        near, far = (0, 8, 4, 12), (16, 24, 18, 26)
        masks = [near, far, [m | 2 for m in near], [m | 4 for m in far]]
        if not self.first:
            masks = [[m for own in masks for m in own]]
        masks += [[m | 1 for m in own] for own in masks]
        blocks = self.outgoing + self.incoming
        return place(blocks, masks, self.widths, self.me, self.part.shape[0] * self.devices)


class Reduce:
    def __init__(self, grads, me, devices, spread=False):
        self.grads, self.me, self.devices, self.staged = grads, me, devices, devices == 32
        self.spread = spread
        self.size = grads[0].shape[0] // devices
        self.stage, self.outgoing, self.incoming = 0, (), ()

    def both(self, low, high):
        rows = slice(low * self.size, high * self.size)
        return self.keep[rows].astype(jnp.float32) + self.came[rows].astype(jnp.float32)

    def prepare(self):
        stage, size = self.stage, self.size
        self.stage += 1
        if not self.staged:
            if stage == 0:
                grad = jnp.concatenate([one.astype(jnp.float32) for one in self.grads], axis=1)
                self.total = lax.psum_scatter(grad, ("dp", "shard"), scatter_dimension=0, tiled=True)
            return
        incoming = [one.astype(jnp.float32) for one in self.incoming]
        if stage == 0:
            order = [2, 10, 6, 14, 20, 28, 22, 30, 0, 8, 4, 12, 16, 24, 18, 26]
            self.keep, send = pick(self.grads, [order, [m | 1 for m in order]], self.me, size)
            self.outgoing, self.masks = (send,), (1,)
        elif stage == 1:
            (self.came,) = self.incoming
            self.outgoing = self.both(0, 4).astype(LOW), self.both(4, 8).astype(LOW)
            self.masks = 2, 4
        elif stage == 2:
            near, far = self.both(8, 12) + incoming[0], self.both(12, 16) + incoming[1]
            self.outgoing = near[2 * size :].astype(LOW), far[2 * size :].astype(LOW)
            self.near, self.far = near[: 2 * size], far[: 2 * size]
            self.masks = 4, 2
        elif stage == 3 and self.spread:
            self.near = self.near + incoming[0]
            self.outgoing, self.masks = ((self.far + incoming[1]).astype(LOW),), (16,)
        elif stage == 4 and self.spread:
            near = self.near + incoming[0]
            self.own = near[:size]
            self.outgoing, self.masks = (near[size:].astype(LOW),), (8,)
        elif self.spread and stage > 4:
            self.total = self.own + incoming[0]
        elif stage == 3:
            near, far = self.near + incoming[0], self.far + incoming[1]
            self.outgoing = near[size:].astype(LOW), far[:size].astype(LOW), far[size:].astype(LOW)
            self.own, self.masks = near[:size], (8, 16, 24)
        else:
            self.total = (self.own + incoming[0]) + (incoming[1] + incoming[2])

    def launch(self):
        if self.staged:
            self.incoming = tuple(
                swap(one, mask, self.devices) for one, mask in zip(self.outgoing, self.masks)
            )


class Sum:
    def __init__(self, values, devices):
        self.values, self.devices, self.staged = values, devices, devices == 32
        self.stage, self.outgoing, self.incoming = 0, (), ()

    def prepare(self):
        stage = self.stage
        self.stage += 1
        if not self.staged:
            if stage == 0:
                self.values = lax.psum(self.values, ("dp", "shard"))
            return
        if len(self.incoming) == 3:
            one, two, three = self.incoming
            self.values = (self.values + one) + (two + three)
        elif stage:
            self.values = self.values + self.incoming[0]
        if stage < 4:
            self.outgoing, self.masks = (self.values,), ((1,), (16,), (4, 2, 6), (8,))[stage]

    def launch(self):
        if self.staged:
            self.incoming = tuple(swap(self.outgoing[0], mask, self.devices) for mask in self.masks)


def open_slot(travellers, *values, ready=()):
    for one in travellers:
        if one not in ready:
            one.prepare()
    travellers = [one for one in travellers if one.staged]
    if not travellers:
        return values
    outgoing, values = lax.optimization_barrier((tuple(one.outgoing for one in travellers), values))
    for one, sent in zip(travellers, outgoing):
        one.outgoing = sent
        one.launch()
    return values


def close_slot(travellers, *values):
    travellers = [one for one in travellers if one.staged]
    if not travellers:
        return values
    incoming, values = lax.optimization_barrier((tuple(one.incoming for one in travellers), values))
    for one, came in zip(travellers, incoming):
        one.incoming = came
    return values


class Pieces:
    def __init__(self, part, devices, shards):
        self.part, self.devices, self.shards = part, devices, shards
        self.staged = devices == 32 and shards == 4
        self.stage, self.outgoing, self.incoming = 0, (), ()

    def prepare(self):
        stage = self.stage
        self.stage += 1
        if stage == 0:
            self.outgoing, self.mask = (self.part,), 2
        elif self.staged:
            self.outgoing, self.mask = (jnp.stack([self.part, *self.incoming]),), 1

    def launch(self):
        if self.staged:
            self.incoming = (swap(self.outgoing[0], self.mask, self.devices),)

    def whole(self):
        if not self.staged:
            return lax.all_gather(self.part, "shard", axis=0), jnp.arange(self.shards, dtype=jnp.int32)
        at = jnp.array([0, 2, 1, 3], jnp.int32) ^ lax.axis_index("shard")
        return jnp.concatenate([self.outgoing[0], self.incoming[0]]), at


class PiecesBack:
    def __init__(self, grad, devices, shards):
        self.grad, self.devices, self.staged = grad, devices, devices == 32 and shards == 4
        self.stage, self.outgoing, self.incoming = 0, (), ()

    def prepare(self):
        stage, grad = self.stage, self.grad
        self.stage += 1
        if not self.staged:
            if stage == 0:
                self.shares = lax.psum_scatter(grad, "shard", scatter_dimension=0)[None], ()
        elif stage == 0:
            self.outgoing, self.mask = (grad[2:].astype(LOW),), 1
        elif stage == 1:
            (self.came,) = self.incoming
            self.over = (grad[1:2] + self.came[1:].astype(jnp.float32)).astype(LOW)
            self.outgoing, self.mask = (self.over[:, :, :1],), 2
        elif stage == 2:
            (self.keys,) = self.incoming
            self.outgoing = (self.over[:, :, 1:],)
        else:
            self.shares = grad, (self.came, jnp.concatenate([self.keys, *self.incoming], axis=2))

    def launch(self):
        if self.staged:
            self.incoming = (swap(self.outgoing[0], self.mask, self.devices),)


def allowed(base, start, valid, key_axis, shape):
    key = base + lax.broadcasted_iota(jnp.int32, shape, key_axis)
    query = start + lax.broadcasted_iota(jnp.int32, shape, 1 - key_axis)
    return (key <= query) & (key < valid)


def over_pieces(info_ref, pieces, length, row, tile, before=None, after=None):
    start, valid = info_ref[0], info_ref[1 + pieces + row]
    everything = slice(0, length)
    early, late = slice(0, length // 2), slice(length // 2, length)

    def one(piece, carry):
        base = info_ref[1 + piece]
        if before is not None:
            before()
        used = (base < start + length) & (base < valid)
        full = (base + length <= start) & (base + length <= valid)
        own = base == start

        def diagonal():
            tile(piece, early, everything, (base, start, valid))
            tile(piece, late, late, (base + length // 2, start + length // 2, valid))

        pl.when(used & full)(lambda: tile(piece, everything, everything, None))
        pl.when(used & own)(diagonal)
        pl.when(used & jnp.logical_not(full | own))(
            lambda: tile(piece, everything, everything, (base, start, valid))
        )
        if after is not None:
            after(piece)
        return carry

    lax.fori_loop(0, pieces, one, 0)


def attention(info, queries, keys_values, first, groups):
    rows, _, length = queries.shape
    pieces = keys_values.shape[0]
    group_width = GROUP * HD

    def kernel(info_ref, q_ref, k_ref, v_ref, out_ref, low_ref, sums_ref, accum_ref, part_ref):
        accum_ref[...] = jnp.zeros_like(accum_ref)
        part_ref[...] = jnp.zeros_like(part_ref)

        def tile(piece, keys, rows_of, bounds):
            key_t, value_t = k_ref[piece, 0, :, keys], v_ref[piece, 0, :, keys]
            key_count, row_count = keys.stop - keys.start, rows_of.stop - rows_of.start
            if bounds is not None:
                mask = allowed(*bounds, 1, (row_count, key_count))
            for head in range(GROUP):
                own = slice(head * HD, (head + 1) * HD)
                exps = jnp.exp(dot(q_ref[0, own, rows_of], key_t, FIRST_FIRST))
                if bounds is not None:
                    exps = jnp.where(mask, exps, 0.0)
                part = exps[:, :128]
                for at in range(128, key_count, 128):
                    part = part + exps[:, at : at + 128]
                part_ref[head, rows_of] += part
                accum_ref[head, rows_of] += dot(exps.astype(LOW), value_t, LAST_LAST)

        over_pieces(info_ref, pieces, length, pl.program_id(0), tile)
        for head in range(GROUP):
            own = slice(head * HD, (head + 1) * HD)
            sums = jnp.sum(part_ref[head].T, axis=0, keepdims=True)
            sums_ref[0, 0, head : head + 1, :] = sums
            out = accum_ref[head].T / sums
            out_ref[0, own, :] = out
            low_ref[0, own, :] = out.astype(LOW)

    q_spec = pl.BlockSpec((1, group_width, length), lambda row, group, *_: (row, group + first, 0))
    o_spec = pl.BlockSpec((1, group_width, length), lambda row, group, *_: (row, group, 0))
    k_spec = pl.BlockSpec((pieces, 1, HD, length), lambda row, group, *_: (0, row, group + first, 0))
    v_spec = pl.BlockSpec(
        (pieces, 1, HD, length), lambda row, group, *_: (0, row, group + first + KV, 0)
    )
    s_spec = pl.BlockSpec((1, 1, GROUP, length), lambda row, group, *_: (row, group, 0, 0))
    work = rows * groups * GROUP * length * length * pieces
    return pl.pallas_call(
        kernel,
        out_shape=[
            jax.ShapeDtypeStruct((rows, groups * group_width, length), jnp.float32),
            jax.ShapeDtypeStruct((rows, groups * group_width, length), LOW),
            jax.ShapeDtypeStruct((rows, groups, GROUP, length), jnp.float32),
        ],
        grid_spec=pltpu.PrefetchScalarGridSpec(
            num_scalar_prefetch=1,
            grid=(rows, groups),
            in_specs=[q_spec, k_spec, v_spec],
            out_specs=[o_spec, o_spec, s_spec],
            scratch_shapes=[
                pltpu.VMEM((GROUP, length, HD), jnp.float32),
                pltpu.VMEM((GROUP, length, 128), jnp.float32),
            ],
        ),
        compiler_params=pltpu.CompilerParams(vmem_limit_bytes=16 << 20),
        cost_estimate=pl.CostEstimate(flops=work, transcendentals=0, bytes_accessed=1 << 20),
    )(info, queries, keys_values, keys_values)


def head_back(grad, raw, gain, cos_t, sin_t):
    half_len = HD // 2
    along = grad * sin_t
    grad = grad * cos_t + jnp.concatenate([along[half_len:], -along[:half_len]], axis=0)
    inverse = lax.rsqrt(jnp.mean(raw * raw, axis=0, keepdims=True) + EPS)
    products = grad * (raw * inverse)
    grad = grad * gain
    cubed = inverse * inverse * inverse
    return inverse * grad - raw * cubed * jnp.mean(grad * raw, axis=0, keepdims=True), products


def fold(values):
    total = values[:, :128]
    for at in range(128, values.shape[1], 128):
        total = total + values[:, at : at + 128]
    return total


def attention_back(
    info, queries, keys_values, out, sums, grad_out, q_raw, gain, cos_t, sin_t, group, carried
):
    rows, _, length = queries.shape
    pieces = keys_values.shape[0]
    group_width = GROUP * HD
    scale_factor = 1.0 / math.sqrt(HD)

    def kernel(
        info_ref, q_ref, k_ref, v_ref, out_ref, sums_ref, grad_ref, raw_ref, gain_ref, cos_ref, sin_ref, *refs
    ):
        refs = refs[len(carried) :]
        dq_ref, dkv_ref, gain_grad_ref = refs[:3]
        grad_low, grad_sums, q_rows, grad_rows, k_accum, v_accum, q_accum = refs[3:]
        q_accum[...] = jnp.zeros_like(q_accum)
        for head in range(GROUP):
            own = slice(head * HD, (head + 1) * HD)
            inverse = 1.0 / sums_ref[0, 0, head : head + 1, :]
            grad = grad_ref[0, own, :]
            grad_sums[head] = -jnp.sum(grad * out_ref[0, own, :], axis=0, keepdims=True) * inverse
            scaled = grad * inverse
            grad_low[own, :] = scaled.astype(LOW)
            grad_rows[head] = scaled.T.astype(LOW)
            q_rows[head] = q_ref[0, own, :].T

        def tile(piece, keys, queries_of, bounds):
            key_t, value_t = k_ref[piece, 0, :, keys], v_ref[piece, 0, :, keys]
            key_count, query_count = keys.stop - keys.start, queries_of.stop - queries_of.start
            if bounds is not None:
                mask = allowed(*bounds, 0, (key_count, query_count))
            for head in range(GROUP):
                own = slice(head * HD, (head + 1) * HD)
                exps = jnp.exp(dot(key_t, q_ref[0, own, queries_of], FIRST_FIRST))
                if bounds is not None:
                    exps = jnp.where(mask, exps, 0.0)
                grad_exps = dot(value_t, grad_low[own, queries_of], FIRST_FIRST)
                grad_scores = (exps * (grad_exps + grad_sums[head, :, queries_of])).astype(LOW)
                v_accum[keys] += dot(exps.astype(LOW), grad_rows[head, queries_of], LAST_FIRST)
                k_accum[keys] += dot(grad_scores, q_rows[head, queries_of], LAST_FIRST)
                q_accum[own, queries_of] += dot(key_t, grad_scores, LAST_FIRST)

        def before():
            k_accum[...] = jnp.zeros_like(k_accum)
            v_accum[...] = jnp.zeros_like(v_accum)

        def after(piece):
            dkv_ref[piece, 0, 0] = k_accum[...].T
            dkv_ref[piece, 0, 1] = v_accum[...].T

        over_pieces(info_ref, pieces, length, pl.program_id(0), tile, before, after)
        total = jnp.zeros((HD, 128), jnp.float32)
        for head in range(GROUP):
            own = slice(head * HD, (head + 1) * HD)
            grad, products = head_back(
                scale_factor * q_accum[own, :], raw_ref[0, own, :], gain_ref[...], cos_ref[...], sin_ref[...]
            )
            dq_ref[0, own, :] = grad.astype(LOW)
            total = total + fold(products)
        gain_grad_ref[0] = total

    q_spec = pl.BlockSpec((1, group_width, length), lambda row, *_: (row, group, 0))
    k_spec = pl.BlockSpec((pieces, 1, HD, length), lambda row, *_: (0, row, group, 0))
    v_spec = pl.BlockSpec((pieces, 1, HD, length), lambda row, *_: (0, row, group + KV, 0))
    s_spec = pl.BlockSpec((1, 1, GROUP, length), lambda row, *_: (row, group, 0, 0))
    table_spec = pl.BlockSpec((HD, length), lambda row, *_: (0, 0))
    gain_spec = pl.BlockSpec((HD, 1), lambda row, *_: (0, 0))
    dkv_spec = pl.BlockSpec((pieces, 1, 2, HD, length), lambda row, *_: (0, row, 0, group, 0))
    work = rows * GROUP * length * length * pieces
    out, grad_out, q_raw = (
        pltpu.with_memory_space_constraint(one, pltpu.HBM) for one in (out, grad_out, q_raw)
    )
    inputs = [info, queries, keys_values, keys_values, out, sums, grad_out, q_raw, gain, cos_t, sin_t]
    return pl.pallas_call(
        kernel,
        out_shape=[
            jax.ShapeDtypeStruct(queries.shape, LOW),
            jax.ShapeDtypeStruct((pieces, rows, 2, KV * HD, length), jnp.float32),
            jax.ShapeDtypeStruct((rows, HD, 128), jnp.float32),
        ],
        grid_spec=pltpu.PrefetchScalarGridSpec(
            num_scalar_prefetch=1,
            grid=(rows,),
            in_specs=[
                q_spec, k_spec, v_spec, q_spec, s_spec, q_spec, q_spec, gain_spec, table_spec, table_spec,
                *[ANY] * len(carried),
            ],
            out_specs=[q_spec, dkv_spec, pl.BlockSpec((1, HD, 128), lambda row, *_: (row, 0, 0))],
            scratch_shapes=[
                pltpu.VMEM((group_width, length), LOW),
                pltpu.VMEM((GROUP, 1, length), jnp.float32),
                pltpu.VMEM((GROUP, length, HD), LOW),
                pltpu.VMEM((GROUP, length, HD), LOW),
                pltpu.VMEM((length, HD), jnp.float32),
                pltpu.VMEM((length, HD), jnp.float32),
                pltpu.VMEM((group_width, length), jnp.float32),
            ],
        ),
        input_output_aliases={len(inputs) + at: at for at in range(len(carried))},
        compiler_params=pltpu.CompilerParams(vmem_limit_bytes=16 << 20),
        cost_estimate=pl.CostEstimate(flops=work, transcendentals=0, bytes_accessed=1 << 20),
    )(*inputs, *carried)


def finish_keys(own, others, k_raw, gain, cos_t, sin_t):
    _, rows, _, width, length = own.shape

    def kernel(own_ref, *refs):
        shares, (raw_ref, gain_ref, cos_ref, sin_ref, out_ref, gain_grad_ref) = refs[:-6], refs[-6:]

        def share(which, rows_of):
            total = own_ref[0, 0, which, rows_of, :]
            for ref in shares:
                total = total + ref[0, 0, which, rows_of, :].astype(jnp.float32)
            return total

        total = jnp.zeros((HD, 128), jnp.float32)
        for head in range(KV):
            rows_of = slice(head * HD, (head + 1) * HD)
            grad, products = head_back(
                share(0, rows_of), raw_ref[0, rows_of, :], gain_ref[...], cos_ref[...], sin_ref[...]
            )
            out_ref[0, rows_of, :] = grad.astype(LOW)
            out_ref[0, slice(width + head * HD, width + (head + 1) * HD), :] = share(1, rows_of).astype(LOW)
            total = total + fold(products)
        gain_grad_ref[0] = total

    piece_spec = pl.BlockSpec((1, 1, 2, width, length), lambda row: (0, row, 0, 0, 0))
    table_spec = pl.BlockSpec((HD, length), lambda row: (0, 0))
    return pl.pallas_call(
        kernel,
        out_shape=[
            jax.ShapeDtypeStruct((rows, 2 * width, length), LOW),
            jax.ShapeDtypeStruct((rows, HD, 128), jnp.float32),
        ],
        grid=(rows,),
        in_specs=[
            *[piece_spec] * (1 + len(others)),
            pl.BlockSpec((1, width, length), lambda row: (row, 0, 0)),
            pl.BlockSpec((HD, 1), lambda row: (0, 0)),
            table_spec,
            table_spec,
        ],
        out_specs=[
            pl.BlockSpec((1, 2 * width, length), lambda row: (row, 0, 0)),
            pl.BlockSpec((1, HD, 128), lambda row: (row, 0, 0)),
        ],
        compiler_params=pltpu.CompilerParams(vmem_limit_bytes=16 << 20),
    )(own, *others, k_raw, gain, cos_t, sin_t)


def local(
    tokens,
    cotangent,
    lengths,
    slot_sequence,
    attn_gain,
    w_qkv,
    q_gain,
    k_gain,
    w_out,
    ffn_gain,
    w_gate,
    w_up,
    w_down,
):
    row_count, piece_len, model_width = tokens.shape
    q_width = HEADS * HD
    kv_width = KV * HD
    total_rows = lengths.shape[0]
    scale_factor = 1.0 / math.sqrt(HD)
    shards = lax.axis_size("shard")
    devices = lax.axis_size("dp") * shards
    part_len = attn_gain.shape[0]
    shard_at = lax.axis_index("shard")
    me = (lax.axis_index("dp") * shards + shard_at).astype(jnp.int32).reshape(1)
    row_valid = jnp.sum(
        jnp.where(
            slot_sequence[:, None] == jnp.arange(total_rows, dtype=jnp.int32)[None, :],
            lengths[None, :],
            0,
        ),
        axis=1,
    )
    start = (shard_at * piece_len).astype(jnp.int32)
    positions = start + jnp.arange(piece_len, dtype=jnp.int32)
    live_mask = (positions[None, :] < row_valid[:, None]).astype(jnp.float32)
    cos_t, sin_t = tables(positions)
    cos_h = cos_t[None, None]
    sin_h = sin_t[None, None]
    q_gain_h = q_gain[None, None, :, None]
    k_gain_h = k_gain[None, None, :, None]

    column = jnp.arange(128)[None, :]
    gain_columns = jnp.where(
        column == 0, attn_gain[:, None], jnp.where(column == 1, ffn_gain[:, None], 0.0)
    ).astype(LOW)
    w_qkv_low, w_gate_low, w_up_low = w_qkv.astype(LOW), w_gate.astype(LOW), w_up.astype(LOW)
    gather_a = Gather([w_qkv_low[:, :q_width], w_qkv_low[:, q_width:], gain_columns], me, devices, True)
    gather_b = Gather([w_out.astype(LOW).T], me, devices)
    w_down_low = w_down.astype(LOW).T
    units = w_down_low.shape[1] // 2
    halves = slice(0, units), slice(units, 2 * units)
    gather_c = [
        Gather(
            [jnp.concatenate([w_gate_low[:, own], w_up_low[:, own]], axis=1), w_down_low[:, own]],
            me,
            devices,
            spread=own is halves[1],
        )
        for own in halves
    ]
    (tokens,) = open_slot([gather_a], tokens)
    x_float = tokens.astype(jnp.float32)
    normed_one, inverse_one = normalize(x_float)
    (normed_one,) = close_slot([gather_a], normed_one)
    (normed_one,) = open_slot([gather_a, gather_c[0]], normed_one)
    (normed_one,) = close_slot([gather_a, gather_c[0]], normed_one)
    (normed_one,) = open_slot([gather_a, gather_b], normed_one)
    (normed_one,) = close_slot([gather_a, gather_b], normed_one)
    (normed_one,) = open_slot([gather_a, gather_c[0]], normed_one)
    (normed_one,) = close_slot([gather_a], normed_one)
    wq, wkv, gains = gather_a.whole()
    gain_attn = gains[:, 0].astype(jnp.float32)
    gain_ffn = gains[:, 1].astype(jnp.float32)
    normed_low = (normed_one * gain_attn).astype(LOW)
    kv_raw = jnp.einsum("rtd,de->ret", normed_low, wkv, preferred_element_type=jnp.float32)
    k_raw = kv_raw[:, :kv_width].reshape(row_count, KV, HD, piece_len)
    v_raw = kv_raw[:, kv_width:]
    k_unit, k_inverse = normalize(k_raw, 2)
    k_low = rotate(k_unit * k_gain_h, cos_h, sin_h).astype(LOW).reshape(row_count, kv_width, piece_len)
    own_kv = jnp.concatenate([k_low, v_raw.astype(LOW)], axis=1)
    own_kv, normed_low = close_slot([gather_c[0]], own_kv, normed_low)
    row_pieces = Pieces(own_kv, devices, shards)
    (normed_low,) = open_slot([row_pieces, gather_b, gather_c[1]], normed_low)
    q_raw = jnp.einsum("rtd,de->ret", normed_low, wq, preferred_element_type=jnp.float32).reshape(
        row_count, HEADS, HD, piece_len
    )
    q_unit, q_inverse = normalize(q_raw, 2)
    q_low = (
        rotate(q_unit * q_gain_h, cos_h, sin_h).astype(LOW) * jnp.array(scale_factor, LOW)
    ).reshape(row_count, q_width, piece_len)
    (q_low,) = close_slot([row_pieces, gather_b, gather_c[1]], q_low)
    (q_low,) = open_slot([row_pieces, gather_b, *gather_c], q_low)
    (q_low,) = close_slot([row_pieces], q_low)
    pieces, piece_at = row_pieces.whole()
    info = jnp.concatenate([start.reshape(1), piece_at * piece_len, row_valid]).astype(jnp.int32)
    o_heads, att_low, sums = attention(info, q_low, pieces, 0, KV)
    o_heads, att_low, sums = close_slot([gather_b, *gather_c], o_heads, att_low, sums)
    (att_low,) = open_slot([gather_b, *gather_c], att_low)
    (att_low,) = close_slot([gather_b], att_low)
    (wout,) = gather_b.whole()
    x_mid = x_float + jnp.einsum("rct,dc->rtd", att_low, wout, preferred_element_type=jnp.float32)
    normed_two, inverse_two = normalize(x_mid)
    ffn_in = (normed_two * gain_ffn).astype(LOW)
    grad_out = cotangent.astype(jnp.float32) * live_mask[..., None]
    grad_low = grad_out.astype(LOW)

    def feed_forward(ffn_in, grad_low, wgu, wdown):
        both = jnp.einsum("rtd,df->rtf", ffn_in, wgu, preferred_element_type=jnp.float32)
        gate_proj, up_proj = both[..., :units], both[..., units:]
        gate_sig = jax.nn.sigmoid(gate_proj)
        silu_gate = gate_proj * gate_sig
        activated = (silu_gate * up_proj).astype(LOW)
        grad_down = jnp.einsum("rtd,rtf->df", grad_low, activated, preferred_element_type=jnp.float32)
        grad_act = jnp.einsum("rtd,df->rtf", grad_low, wdown, preferred_element_type=jnp.float32)
        grad_gate = (grad_act * up_proj * gate_sig * (1.0 + gate_proj * (1.0 - gate_sig))).astype(LOW)
        grad_up = (grad_act * silu_gate).astype(LOW)
        grad_both = jnp.concatenate([grad_gate, grad_up], axis=2)
        grad_wgu = jnp.einsum("rtd,rtf->df", ffn_in, grad_both, preferred_element_type=jnp.float32)
        return activated, grad_both, [grad_wgu.astype(LOW), grad_down.astype(LOW)]

    ffn_in, x_mid = close_slot(gather_c, ffn_in, x_mid)
    (ffn_in,) = open_slot([gather_c[1]], ffn_in)
    wgu_one, wdown_one = gather_c[0].whole()
    act_one, both_one, grads = feed_forward(ffn_in, grad_low, wgu_one, wdown_one)
    red_one = Reduce(grads, me, devices)
    red_one.prepare()
    ffn_in, red_one.outgoing, act_one, both_one = close_slot(
        [gather_c[1]], ffn_in, red_one.outgoing, act_one, both_one
    )
    (ffn_in,) = open_slot([gather_c[1]], ffn_in)
    (ffn_in,) = close_slot([gather_c[1]], ffn_in)
    (ffn_in,) = open_slot([red_one], ffn_in, ready=[red_one])
    wgu_two, wdown_two = gather_c[1].whole()
    act_two, both_two, grads = feed_forward(ffn_in, grad_low, wgu_two, wdown_two)
    red_two = Reduce(grads, me, devices)
    red_two.prepare()
    ffn_in, red_two.outgoing, act_two, both_two = close_slot(
        [red_one], ffn_in, red_two.outgoing, act_two, both_two
    )
    both_two, act_two = open_slot([red_one], both_two, act_two)
    grad_ffn_in = jnp.einsum(
        "rtf,df->rtd", both_one, wgu_one, preferred_element_type=jnp.float32
    ) + jnp.einsum("rtf,df->rtd", both_two, wgu_two, preferred_element_type=jnp.float32)
    grad_mid = grad_out + norm_back(x_mid, inverse_two, grad_ffn_in * gain_ffn)
    mid_low = grad_mid.astype(LOW)
    grad_wout = jnp.einsum("rtd,rct->dc", mid_low, att_low, preferred_element_type=jnp.float32)
    grad_att = jnp.einsum("rtd,dc->rct", mid_low, wout, preferred_element_type=jnp.float32)
    red_out = Reduce([grad_wout.astype(LOW)], me, devices, True)
    red_out.prepare()
    grad_att, red_out.outgoing = close_slot([red_one], grad_att, red_out.outgoing)
    (grad_att,) = open_slot([red_one, red_two], grad_att, ready=[red_two])

    q_gain_c, k_gain_c = q_gain[:, None], k_gain[:, None]
    q_raw_flat = q_raw.reshape(row_count, q_width, piece_len)
    k_raw_flat = k_raw.reshape(row_count, kv_width, piece_len)

    def back(group, grad_att, carried=()):
        return attention_back(
            info, q_low, pieces, o_heads, sums, grad_att, q_raw_flat, q_gain_c, cos_t, sin_t, group, carried
        )

    gain_parts = []

    def more(group, grad_att, carried=()):
        *carried, gain_part = back(group, grad_att, carried)
        gain_parts.append(gain_part)
        return tuple(carried)

    carried = more(0, grad_att)
    carried, grad_att = close_slot([red_one, red_two], carried, grad_att)
    (grad_att,) = open_slot([red_one, red_two], grad_att)
    carried = more(1, grad_att, carried)
    carried, grad_att = close_slot([red_one, red_two], carried, grad_att)
    (grad_att,) = open_slot([red_two, red_out], grad_att, ready=[red_out])
    carried = more(2, grad_att, carried)
    carried, grad_att = close_slot([red_two, red_out], carried, grad_att)
    (grad_att,) = open_slot([red_two, red_out], grad_att)
    carried = more(3, grad_att, carried)
    grad_q_low, grad_pieces = close_slot([red_two, red_out], carried)[0]
    kv_back = PiecesBack(grad_pieces, devices, shards)
    (grad_q_low,) = open_slot([kv_back, red_out], grad_q_low)
    (grad_q_low,) = close_slot([kv_back], grad_q_low)
    (grad_q_low,) = open_slot([kv_back], grad_q_low)
    grad_wq = jnp.einsum("rtd,ret->de", normed_low, grad_q_low, preferred_element_type=jnp.float32)
    red_q = Reduce([grad_wq.astype(LOW)], me, devices)
    red_q.prepare()
    red_q.outgoing, grad_q_low = close_slot([kv_back, red_out], red_q.outgoing, grad_q_low)
    (grad_q_low,) = open_slot([kv_back, red_q], grad_q_low, ready=[red_q])
    grad_normed_q = jnp.einsum("ret,de->rtd", grad_q_low, wq, preferred_element_type=jnp.float32)
    (grad_normed_q,) = close_slot([kv_back, red_q], grad_normed_q)
    kv_back.prepare()
    grad_kv_low, k_gain_part = finish_keys(*kv_back.shares, k_raw_flat, k_gain_c, cos_t, sin_t)
    shared = Sum(
        jnp.concatenate([jnp.sum(sum(gain_parts), axis=(0, 2)), jnp.sum(k_gain_part, axis=(0, 2))])[None],
        devices,
    )
    (grad_kv_low,) = open_slot([red_q, shared], grad_kv_low)
    grad_wkv = jnp.einsum("rtd,ret->de", normed_low, grad_kv_low, preferred_element_type=jnp.float32)
    red_kv = Reduce([grad_wkv.astype(LOW)], me, devices)
    red_kv.prepare()
    (red_kv.outgoing,) = open_slot([red_out], red_kv.outgoing)
    red_kv.outgoing, grad_kv_low = close_slot([red_q, shared], red_kv.outgoing, grad_kv_low)
    (grad_kv_low,) = open_slot([red_q, red_kv, shared], grad_kv_low, ready=[red_kv])
    grad_normed = grad_normed_q + jnp.einsum(
        "ret,de->rtd", grad_kv_low, wkv, preferred_element_type=jnp.float32
    )
    input_grad = grad_mid + norm_back(x_float, inverse_one, grad_normed * gain_attn)
    (input_grad,) = close_slot([red_q, red_kv, shared, red_out, red_one, red_two], input_grad)
    for one in (red_one, red_two):
        one.prepare()
    (act_one,) = open_slot([red_q, red_kv], act_one)
    output = (
        x_mid
        + jnp.einsum("rtf,df->rtd", act_one, wdown_one, preferred_element_type=jnp.float32)
        + jnp.einsum("rtf,df->rtd", act_two, wdown_two, preferred_element_type=jnp.float32)
    ).astype(LOW)
    (output,) = close_slot([red_q, red_kv], output)
    red_q.prepare()
    open_slot([red_kv, shared])
    close_slot([red_kv, shared])
    open_slot([red_kv, shared, red_out])
    close_slot([red_kv, shared, red_out])
    red_out.prepare()
    red_kv.prepare()
    shared.prepare()
    shared = shared.values
    three, four = red_q.total, red_kv.total
    summed = red_one.total, red_two.total
    summed_wgate, summed_wup, summed_down = (
        jnp.concatenate([one[:, at * units : (at + 1) * units] for one in summed], axis=1) for at in range(3)
    )
    summed_down, summed_wout = summed_down.T, red_out.total.T
    summed_wqkv = jnp.concatenate([three, four], axis=1)
    grad_gain_one = jnp.sum(summed_wqkv * w_qkv_low, axis=1) / attn_gain.astype(LOW)
    grad_gain_two = jnp.sum(summed_wgate * w_gate_low + summed_wup * w_up_low, axis=1) / ffn_gain.astype(LOW)
    return (
        output,
        input_grad,
        grad_gain_one,
        summed_wqkv,
        shared[0, :HD],
        shared[0, HD:],
        summed_wout,
        grad_gain_two,
        summed_wgate,
        summed_wup,
        summed_down,
    )


def solution(mesh):
    in_specs = (
        P("dp", "shard", None),
        P("dp", "shard", None),
        P(),
        P("dp"),
        P(("dp", "shard")),
        P(("dp", "shard"), None),
        P(),
        P(),
        P(None, ("dp", "shard")),
        P(("dp", "shard")),
        P(("dp", "shard"), None),
        P(("dp", "shard"), None),
        P(None, ("dp", "shard")),
    )
    out_specs = (
        P("dp", "shard", None),
        P("dp", "shard", None),
        P(("dp", "shard")),
        P(("dp", "shard"), None),
        P(),
        P(),
        P(None, ("dp", "shard")),
        P(("dp", "shard")),
        P(("dp", "shard"), None),
        P(("dp", "shard"), None),
        P(None, ("dp", "shard")),
    )
    return jax.shard_map(local, mesh=mesh, in_specs=in_specs, out_specs=out_specs, check_vma=False)
```
